512 devices in a mesh: dp: 8 (over x, y_lo), ctx: 64 (over z, y_hi, core).
Axes of the slice: x: 4, y: 8 (y_hi: 4, y_lo: 2; y = y_hi * 2 + y_lo), z: 8, core: 2. Of those that a mesh axis runs over, the one named last changes fastest.
Arguments:
- query_nope: bfloat16 [1536, 128, 128], P('dp', 'ctx'), may hold values from -6 to 6
- query_rope: bfloat16 [1536, 128, 64], P('dp', 'ctx'), may hold values from -8 to 8
- grad_output: bfloat16 [1536, 128, 128], P('dp', 'ctx'), may hold values from -6 to 6
- latents: bfloat16 [1536, 512], P('dp'), may hold values from -6 to 6
- key_rope: bfloat16 [1536, 64], P('dp'), may hold values from -8 to 8
- key_up: bfloat16 [128, 128, 512], P('ctx'), may hold values from -0.25 to 0.25
- value_up: bfloat16 [128, 128, 512], P('ctx'), may hold values from -0.25 to 0.25
- pair_order: int32 [256], replicated, may hold values from 0 to 255, each once
Outputs:
- grad_query_nope: bfloat16 [1536, 128, 128], P('dp', 'ctx')
- grad_query_rope: bfloat16 [1536, 128, 64], P('dp', 'ctx')
- grad_latents: bfloat16 [1536, 512], P(('dp', 'ctx'))
- grad_key_rope: bfloat16 [1536, 64], P(('dp', 'ctx'))
- grad_key_up: float32 [128, 128, 512], P('ctx')
- grad_value_up: float32 [128, 128, 512], P('ctx')
The draws below stay inside these ranges and needn't reach their ends.
Inputs may be any that keep to these rules, and one draw needn't show every extreme that they name: pair_order holds every number of 0 to 255 once.
All inputs are finite; a program needn't handle non-finite values.
Results may differ from the reference program's by a relative error of at most 0.024.
Values may be sent and summed in bfloat16 or wider, within the bound.
A program may use at most 64 MiB of HBM per device.

```python
import math
import jax
import jax.numpy as jnp
from jax import lax

H = 128
DN = 128
DR = 64
DV = 128
DL = 512
TOK_DEV = 192
S = 1536
PAIRS = 256
N_DP = 8


def draw_key_rope(key, part):
    return jnp.clip(jax.random.normal(jax.random.fold_in(key, 3), (S, DR), jnp.float32), -6.0, 6.0).astype(jnp.bfloat16)


def draw_query_rope(key, part):
    return jnp.clip(jax.random.normal(jax.random.fold_in(key, 5), (S, H, DR), jnp.float32), -6.0, 6.0).astype(jnp.bfloat16)


def block_scale(own_key, dims, pieces, least, high):
    gain = 1.0
    for axis_at, blocks in pieces:
        heights = jax.random.uniform(jax.random.fold_in(jax.random.fold_in(own_key, 6), axis_at), (blocks,), jnp.float32, least / len(pieces), high / len(pieces))
        gain = gain * jnp.repeat(jnp.exp(heights), dims[axis_at] // blocks).reshape((-1,) + (1,) * (len(dims) - 1 - axis_at))
    return gain


def scatter_about(stream_key, extent, width, most, shards=(), kind=jnp.bfloat16):
    array = jax.random.normal(stream_key, extent, jnp.float32) * width
    if len(shards) > 0:
        array = block_scale(stream_key, extent, shards, -0.22, 0.18) * array
    return jnp.clip(array, min=-most, max=most).astype(kind)


def setup_inputs(seed: int = 0) -> dict:
    key_of = jax.random.split(jax.random.key(seed), 9)
    return {
        "query_nope": scatter_about(key_of[0], (S, H, DN), 1.0, 6.0, ((0, 8), (1, 64))),
        "query_rope": draw_query_rope(jax.random.fold_in(key_of[8], 71), 0),
        "grad_output": scatter_about(key_of[2], (S, H, DV), 1.0, 6.0, ((0, 8), (1, 64))),
        "latents": scatter_about(key_of[3], (S, DL), 1.0, 6.0, ((0, 8),)),
        "key_rope": draw_key_rope(jax.random.fold_in(key_of[8], 71), 0),
        "key_up": scatter_about(key_of[5], (H, DN, DL), DL ** -0.5, 0.25, ((0, 64),)),
        "value_up": scatter_about(key_of[6], (H, DV, DL), DL ** -0.5, 0.25, ((0, 64),)),
        "pair_order": jax.random.permutation(key_of[7], PAIRS).astype(jnp.int32),
    }


def token_positions(order_row, dev_count, tok_dev):
    pair_count = order_row.shape[0]
    per_dev = pair_count // dev_count
    group_len = tok_dev // (2 * per_dev)
    half_len = tok_dev // 2
    within = jnp.arange(tok_dev, dtype=jnp.int32)
    slot_ids = within % half_len // group_len
    pair_ids = order_row.reshape(dev_count, per_dev)[:, slot_ids]
    late_ids = 2 * pair_count - 1 - pair_ids
    group_ids = jnp.where(within[None, :] < half_len, pair_ids, late_ids)
    return (group_ids * group_len + (within % group_len)[None, :]).reshape(-1).astype(jnp.int32)

def reference(query_nope, query_rope, grad_output, latents, key_rope, key_up, value_up, pair_order):
    positions = token_positions(pair_order, N_DP, TOK_DEV)
    allowed = positions[None, :] <= positions[:, None]
    softmax_scale = 1.0 / math.sqrt(DN + DR)
    latents_t = latents.T
    krope_t = key_rope.T

    def per_head(carry, inputs):
        lat_sum, rope_sum = carry
        head_nope, head_rope, head_grad, head_kup, head_vup = inputs
        absorbed = jnp.dot(head_nope, head_kup, preferred_element_type=jnp.float32).astype(jnp.bfloat16)
        scores = (jnp.dot(absorbed, latents_t, preferred_element_type=jnp.float32) + jnp.dot(head_rope, krope_t, preferred_element_type=jnp.float32)) * softmax_scale
        scores = jnp.where(allowed, scores, -jnp.inf)
        row_max = lax.optimization_barrier(jnp.max(scores, axis=1, keepdims=True))
        exp_scores = jnp.exp(scores - row_max)
        weights = exp_scores / lax.optimization_barrier(jnp.sum(exp_scores, axis=1, keepdims=True))
        weights_bf = weights.astype(jnp.bfloat16)
        latent_out = jnp.dot(weights_bf, latents, preferred_element_type=jnp.float32)
        grad_lat_out = jnp.dot(head_grad, head_vup, preferred_element_type=jnp.float32).astype(jnp.bfloat16)
        row_dot = lax.optimization_barrier(jnp.sum(grad_lat_out.astype(jnp.float32) * latent_out, axis=1, keepdims=True))
        grad_weights = jnp.dot(grad_lat_out, latents_t, preferred_element_type=jnp.float32)
        grad_scores = (weights * (grad_weights - row_dot) * softmax_scale).astype(jnp.bfloat16)
        grad_absorbed = jnp.dot(grad_scores, latents, preferred_element_type=jnp.float32).astype(jnp.bfloat16)
        grad_rope = jnp.dot(grad_scores, key_rope, preferred_element_type=jnp.float32).astype(jnp.bfloat16)
        lat_sum = lat_sum + jnp.dot(grad_scores.T, absorbed, preferred_element_type=jnp.float32) + jnp.dot(weights_bf.T, grad_lat_out, preferred_element_type=jnp.float32)
        rope_sum = rope_sum + jnp.dot(grad_scores.T, head_rope, preferred_element_type=jnp.float32)
        grad_nope = jnp.dot(grad_absorbed, head_kup.T, preferred_element_type=jnp.float32).astype(jnp.bfloat16)
        grad_kup = jnp.dot(head_nope.T, grad_absorbed, preferred_element_type=jnp.float32)
        grad_vup = jnp.dot(head_grad.T, latent_out.astype(jnp.bfloat16), preferred_element_type=jnp.float32)
        return ((lat_sum, rope_sum), (grad_nope, grad_rope, grad_kup, grad_vup))
    inputs = (jnp.transpose(query_nope, (1, 0, 2)), jnp.transpose(query_rope, (1, 0, 2)), jnp.transpose(grad_output, (1, 0, 2)), key_up, value_up)
    start = (jnp.zeros((S, DL), jnp.float32), jnp.zeros((S, DR), jnp.float32))
    (lat_sum, rope_sum), (grad_nope, grad_rope, grad_kup, grad_vup) = lax.scan(per_head, start, inputs)
    return (jnp.transpose(grad_nope, (1, 0, 2)), jnp.transpose(grad_rope, (1, 0, 2)), lat_sum.astype(jnp.bfloat16), rope_sum.astype(jnp.bfloat16), grad_kup, grad_vup)
```

```python
import functools
import math

import jax
import jax.numpy as jnp
from jax import lax
from jax.experimental import pallas as pl
from jax.experimental.pallas import tpu as pltpu
from jax.sharding import PartitionSpec as P

MESH = pl.DeviceIdType.MESH
F32 = jnp.float32
BF16 = jnp.bfloat16
NEG = -1e30

NX, NYL, NZ, NYH = 4, 2, 8, 4
TOK = 192
HALF = TOK // 2
DL, DR, DN = 512, 64, 128
ROWS = 2 * TOK
EXT = DL + 2 * DR
PAIRS = 256
PER_DEV = 32
BLK = 4 * HALF + 48
CUT = 224
CH = NZ * 96 + 96
CHH = CH // 2

REL = (0, 3, 1, 2)

N_SEM = 65


def dot(a, b, ca=1, cb=0):
    return lax.dot_general(a, b, (((ca,), (cb,)), ((), ())), preferred_element_type=F32)


def iota(shape, axis):
    return lax.broadcasted_iota(jnp.int32, shape, axis)


def third(v):
    return (v * 43691) >> 17


def kernel(
    q_hbm, qr_hbm, go_hbm, lat_hbm, kr_hbm, kup_hbm, vup_hbm, po_hbm,
    gn_ref, gr_ref, ol_ref, or_ref, gk_ref, gv_ref,
    q_v, qr_v, go_v, kr_v, kup_v, vup_v, po_v,
    agb, lx_s, lxt, ax, axt, gx, gxt, qtx, gotx,
    pcol, prow, st, gw, mb, lb, wt, gst, lot, gat,
    csend, crecv, cown, xs, xsum, r2p, r2m, ra1, ra2, rb1, rb2,
    zs, zrecv, ys, yrecv,
    vb, vry, vs, vr2p, vr2m, vra1, vra2, vrb1, vrb2, vfin,
    vkeep, kb, kr2p, kr2m, kra1, kra2, krb1, krb2, kkeep, kx, kry, kfin,
    lsem, ss, rs,
):
    dp, ctx = lax.axis_index("dp"), lax.axis_index("ctx")
    x, yl = dp // NYL, dp % NYL
    z, yh, c = ctx // (NYH * 2), (ctx // 2) % NYH, ctx % 2
    sib = 1 - c
    xp, xm, x2 = (x + 1) % NX, (x + 3) % NX, (x + 2) % NX

    def device(x_=None, yl_=None, z_=None, yh_=None, c_=None):
        x_, yl_ = x if x_ is None else x_, yl if yl_ is None else yl_
        z_, yh_, c_ = z if z_ is None else z_, yh if yh_ is None else yh_, c if c_ is None else c_
        return {"dp": x_ * NYL + yl_, "ctx": (z_ * NYH + yh_) * 2 + c_}

    to_sib = device(c_=sib)
    to_y = device(yl_=1 - yl)
    to_xp, to_xm = device(x_=xp), device(x_=xm)

    def remote(n, src, dst, dev):
        return pltpu.make_async_remote_copy(
            src_ref=src, dst_ref=dst, send_sem=ss.at[n], recv_sem=rs.at[n],
            device_id=dev, device_id_type=MESH,
        )

    sent = []

    def send(n, src, dst, dev):
        copy = remote(n, src, dst, dev)
        copy.start()
        sent.append(copy)

    def got(n, dst):
        remote(n, dst, dst, to_sib).wait_recv()

    barrier = pltpu.get_barrier_semaphore()

    def greet(dev):
        pl.semaphore_signal(barrier, inc=1, device_id=dev, device_id_type=MESH)

    greet(to_xp)
    greet(to_xm)
    greet(device(yl_=1 - yl))
    for d in range(NYH):
        far = (yh + d) % NYH
        greet(device(yh_=far, c_=sib))
        greet(device(yh_=far, yl_=1 - yl, c_=sib))
        if d:
            greet(device(yh_=far, yl_=(yl + c) % 2, c_=c))
    for d in range(1, NZ):
        greet(device(z_=(z + d) % NZ))

    local = []

    def fetch(src, dst):
        copy = pltpu.make_async_copy(src, dst, lsem.at[len(local)])
        copy.start()
        local.append(copy)
        return copy

    kr_in = fetch(kr_hbm, kr_v)
    lat_in = []
    for h in range(2):
        for t in range(4):
            lat_in.append(fetch(
                lat_hbm.at[pl.ds(h * HALF, HALF), pl.ds(t * 128, 128)],
                agb.at[0, 0, h, pl.ds(t * HALF, HALF)],
            ))
    q_in, kup_in = fetch(q_hbm, q_v), fetch(kup_hbm, kup_v)
    go_in, vup_in = fetch(go_hbm, go_v), fetch(vup_hbm, vup_v)
    qr_in, po_in = fetch(qr_hbm, qr_v), fetch(po_hbm, po_v)

    kr_in.wait()
    kr_own = kr_v[...].astype(F32).T
    krp = jnp.concatenate([kr_own[:HALF], kr_own[HALF:]], axis=1).astype(BF16)
    agb[0, 0, 0, pl.ds(4 * HALF, 48)] = krp[:48]
    agb[0, 0, 1, pl.ds(4 * HALF, 48)] = krp[48:]
    for copy in lat_in:
        copy.wait()

    pl.semaphore_wait(barrier, 21)

    send(0, agb.at[0, 0, c], agb.at[0, 1, c], to_y)
    send(1, agb.at[0, 0, c], agb.at[1, 0, c], to_xp)
    send(2, agb.at[0, 0, c], agb.at[2, 0, c], to_xm)

    q_in.wait()
    go_in.wait()
    kup_in.wait()
    vup_in.wait()
    qr_in.wait()
    po_in.wait()
    blank = jnp.zeros((TOK, DN), F32)

    def block_diagonal(ref):
        top = jnp.concatenate([ref[0].astype(F32), blank], axis=1)
        low = jnp.concatenate([blank, ref[1].astype(F32)], axis=1)
        return jnp.concatenate([top, low], axis=0)

    qx = block_diagonal(q_v)
    gox = block_diagonal(go_v)
    qtx[...] = qx.T.astype(BF16)
    gotx[...] = gox.T.astype(BF16)
    kup2 = kup_v[...].reshape(2 * DN, DL)
    vup2 = vup_v[...].reshape(2 * DN, DL)
    absorbed = dot(qx.astype(BF16), kup2)
    grad_lat = dot(gox.astype(BF16), vup2)
    qr_rows = jnp.concatenate([qr_v[0].astype(F32).T, qr_v[1].astype(F32).T], axis=0)
    qr2 = jnp.concatenate([qr_rows, qr_rows], axis=1)
    ax[:, :DL] = absorbed.astype(BF16)
    ax[:, DL:] = qr2.astype(BF16)
    axt[:DL, :] = absorbed.T.astype(BF16)
    axt[DL:, :] = qr2.T.astype(BF16)
    gx[...] = grad_lat.astype(BF16)
    gxt[...] = grad_lat.T.astype(BF16)

    po_row = jnp.broadcast_to(po_v[...].astype(F32), (8, PAIRS))
    slot_t = third(iota((PAIRS, ROWS), 1) % HALF)
    pick = jnp.where(iota((PAIRS, ROWS), 0) == dp * PER_DEV + slot_t, 1.0, 0.0).astype(BF16)
    pid_row = dot(po_row.astype(BF16), pick)
    within = iota((8, ROWS), 1)
    in_half = within % HALF
    late = (within % TOK) >= HALF
    group = jnp.where(late, 2.0 * PAIRS - 1.0 - pid_row, pid_row)
    prow[...] = group * 3.0 + (in_half - 3 * third(in_half)).astype(F32)

    po_col = jnp.broadcast_to(po_row[:1], (128, PAIRS)).T.astype(BF16)
    half_of = iota((TOK, PER_DEV), 0) % HALF
    expand = jnp.where(third(half_of) == iota((TOK, PER_DEV), 1), 1.0, 0.0).astype(BF16)
    row_no = iota((TOK, 128), 0)
    row_half = row_no % HALF
    for b in range(NX * NYL):
        pid = dot(expand, po_col[b * PER_DEV:(b + 1) * PER_DEV])
        grp = jnp.where(row_no >= HALF, 2.0 * PAIRS - 1.0 - pid, pid)
        pcol[b] = grp * 3.0 + (row_half - 3 * third(row_half)).astype(F32)

    scale = 1.0 / math.sqrt(DN + DR)
    low_lane = iota((HALF, 128), 1) < DR

    def attend(k, j):
        b = 2 * k + j
        key_dev = ((x + REL[k]) % NX) * NYL + (yl + j) % 2
        halves = []
        krp = jnp.concatenate(
            [agb[k, j, 0, pl.ds(4 * HALF, 48)], agb[k, j, 1, pl.ds(4 * HALF, 48)]], axis=0
        )
        zero = jnp.zeros((HALF, 128), BF16)
        for h in range(2):
            tiles = [agb[k, j, h, pl.ds(t * HALF, HALF)] for t in range(4)]
            tiles.append(jnp.where(low_lane, krp, zero) if h == 0 else jnp.where(low_lane, zero, krp))
            halves.append(jnp.concatenate(tiles, axis=1))
        lx = jnp.concatenate(halves, axis=0)
        lx_s[pl.ds(b * TOK, TOK), :] = lx
        s = dot(lx, axt[...]) * scale
        gw[b] = dot(lx[:, :DL], gxt[...])
        key_pos = pcol[key_dev]
        allowed = jnp.concatenate([key_pos] * 3, axis=1) <= prow[0:1]
        s = jnp.where(allowed, s, NEG)
        m = jnp.max(s, axis=0, keepdims=True)
        p = jnp.where(allowed, jnp.exp(s - m), 0.0)
        st[b] = p
        mb[b] = jnp.broadcast_to(m, (8, ROWS))
        lb[b] = jnp.broadcast_to(jnp.sum(p, axis=0, keepdims=True), (8, ROWS))

    def attend_pair(k):
        attend(k, 0)
        attend(k, 1)
        for t in range(EXT // 128):
            lxt[pl.ds(t * 128, 128), pl.ds(k * 2 * TOK, 2 * TOK)] = (
                lx_s[pl.ds(k * 2 * TOK, 2 * TOK), pl.ds(t * 128, 128)].astype(F32).T.astype(BF16)
            )

    def forward(n, j):
        got(1 + 2 * j, agb.at[1, j, c])
        send(5 + 2 * j, agb.at[1, j, c, pl.ds(0, CUT)], agb.at[3, j, c, pl.ds(0, CUT)], to_xp)
        send(n, agb.at[1, j, c], agb.at[1, j, c], to_sib)
        got(2 + 2 * j, agb.at[2, j, c])
        send(6 + 2 * j, agb.at[2, j, c, pl.ds(CUT, BLK - CUT)],
             agb.at[3, j, c, pl.ds(CUT, BLK - CUT)], to_xm)
        send(n + 1, agb.at[2, j, c], agb.at[2, j, c], to_sib)

    got(0, agb.at[0, 1, c])
    send(3, agb.at[0, 1, c], agb.at[1, 1, c], to_xp)
    send(4, agb.at[0, 1, c], agb.at[2, 1, c], to_xm)
    send(9, agb.at[0, 1, c], agb.at[0, 1, c], to_sib)
    forward(10, 0)
    got(9, agb.at[0, 1, sib])
    attend_pair(0)
    forward(12, 1)
    got(10, agb.at[1, 0, sib])
    got(12, agb.at[1, 1, sib])
    attend_pair(1)
    for j in range(2):
        got(5 + 2 * j, agb.at[3, j, c, pl.ds(0, CUT)])
        got(6 + 2 * j, agb.at[3, j, c, pl.ds(CUT, BLK - CUT)])
        send(14 + j, agb.at[3, j, c], agb.at[3, j, c], to_sib)
    got(11, agb.at[2, 0, sib])
    got(13, agb.at[2, 1, sib])
    attend_pair(2)
    got(14, agb.at[3, 0, sib])
    got(15, agb.at[3, 1, sib])
    attend_pair(3)

    top = mb[0]
    for b in range(1, 8):
        top = jnp.maximum(top, mb[b])
    total = jnp.zeros_like(top)
    for b in range(8):
        share = jnp.exp(mb[b] - top)
        mb[b] = share
        total = total + lb[b] * share
    inv = 1.0 / total
    for b in range(8):
        w = st[b] * (mb[b] * inv)[:1]
        st[b] = w
        wt[pl.ds(b * TOK, TOK), :] = w.astype(BF16)

    dots = jnp.zeros((1, ROWS), F32)
    for t in range(4):
        part = dot(lxt[pl.ds(t * 128, 128), :], wt[...])
        dots = dots + jnp.sum(
            gxt[pl.ds(t * 128, 128), :].astype(F32) * part, axis=0, keepdims=True
        )
        lot[pl.ds(t * 128, 128), :] = part.astype(BF16)

    def ring_first(n, buf, halves, dst):
        lo, hi = halves
        send(n, buf.at[x2].at[lo], dst[0], to_xp)
        send(n + 1, buf.at[x2].at[hi], dst[1], to_xm)
        send(n + 2, buf.at[xp].at[hi], dst[2], to_xp)
        send(n + 3, buf.at[xm].at[lo], dst[4], to_xm)

    def ring_second(n, buf, halves, dst, keep):
        lo, hi = halves
        got(n, dst[0])
        keep[0] = (buf[xp, lo].astype(F32) + dst[0][...].astype(F32)).astype(BF16)
        send(n + 4, keep.at[0], dst[3], to_xp)
        got(n + 1, dst[1])
        keep[1] = (buf[xm, hi].astype(F32) + dst[1][...].astype(F32)).astype(BF16)
        send(n + 5, keep.at[1], dst[5], to_xm)

    def ring_last(n, own_lo, own_hi, dst):
        got(n + 2, dst[2])
        got(n + 3, dst[4])
        got(n + 4, dst[3])
        got(n + 5, dst[5])
        low = own_lo.astype(F32) + dst[3][...].astype(F32) + dst[4][...].astype(F32)
        high = own_hi.astype(F32) + dst[2][...].astype(F32) + dst[5][...].astype(F32)
        return low, high

    v_part = dot(gotx[...], lot[...], 1, 1).astype(BF16)
    for a in range(8):
        for h in range(2):
            vb[a // 4, a % 4, pl.ds(16 * h, 16), :] = v_part[DN * h + 16 * a:DN * h + 16 * a + 16]
    send(41, vb.at[1 - yl], vry, to_y)

    for b in range(8):
        gst[pl.ds(b * TOK, TOK), :] = (st[b] * (gw[b] - dots) * scale).astype(BF16)
    rope_rows = None
    for t in range(5):
        part = dot(lxt[pl.ds(t * 128, 128), :], gst[...])
        if t < 4:
            gat[pl.ds(t * 128, 128), :] = part.astype(BF16)
        else:
            rope_rows = (part[:DR] + part[DR:]).astype(BF16)
    gr_ref[0] = rope_rows[:, :TOK]
    gr_ref[1] = rope_rows[:, TOK:]

    k_part = dot(qtx[...], gat[...], 1, 1).astype(BF16)
    for a in range(8):
        for h in range(2):
            kb[a // 2, a % 2, pl.ds(16 * h, 16), :] = k_part[DN * h + 16 * a:DN * h + 16 * a + 16]
    k_dst = (kr2p, kr2m, kra1, kra2, krb1, krb2)
    k_half = (0, 1)
    ring_first(53, kb, k_half, k_dst)

    def terms(k, j):
        start = pl.multiple_of((2 * k + j) * TOK, TOK)
        g = gst[pl.ds(start, TOK), :]
        full = dot(g, ax[...])
        lat = full[:, :DL] + dot(wt[pl.ds(start, TOK), :], gx[...])
        rope = jnp.where(low_lane, full[:HALF, DL:], full[HALF:, DL:])
        return lat, rope

    def put_terms(lat, rope, dst):
        for i in range(NZ):
            dst[pl.ds(96 * i, 96), :] = jnp.concatenate(
                [lat[24 * i:24 * i + 24, 128 * t:128 * t + 128] for t in range(4)], axis=0
            ).astype(dst.dtype)
        dst[pl.ds(96 * NZ, 96), :] = rope.astype(dst.dtype)

    def both_cores(k, dst):
        got(16 + k, crecv.at[k])
        dst[...] = (cown[k] + crecv[k].astype(F32)).astype(dst.dtype)

    x_dst = (r2p, r2m, ra1, ra2, rb1, rb2)
    low_rows, high_rows = pl.ds(0, CHH), pl.ds(CHH, CHH)

    for n, k in enumerate((3, 2, 1, 0)):
        put_terms(*terms(k, sib), csend.at[k])
        send(16 + k, csend.at[k], crecv.at[k], to_sib)
        put_terms(*terms(k, c), cown.at[k])
        if n == 1:
            both_cores(3, xs.at[3])
            send(20, xs.at[3, low_rows], r2p, to_xp)
            send(21, xs.at[3, high_rows], r2m, to_xm)
        if n == 2:
            both_cores(2, xs.at[2])
            send(22, xs.at[2, high_rows], ra1, to_xp)
        if n == 3:
            both_cores(1, xs.at[1])
            send(23, xs.at[1, low_rows], rb1, to_xm)
    got(20, r2p)
    xs[0, low_rows] = (xs[2, low_rows].astype(F32) + r2p[...].astype(F32)).astype(BF16)
    send(24, xs.at[0, low_rows], ra2, to_xp)
    got(21, r2m)
    xs[0, high_rows] = (xs[1, high_rows].astype(F32) + r2m[...].astype(F32)).astype(BF16)
    send(25, xs.at[0, high_rows], rb2, to_xm)
    both_cores(0, xsum)

    got(41, vry)
    vs[...] = (vb[yl].astype(F32) + vry[...].astype(F32)).astype(BF16)
    v_dst = (vr2p, vr2m, vra1, vra2, vrb1, vrb2)
    v_half = (pl.ds(0, 16), pl.ds(16, 16))
    ring_first(42, vs, v_half, v_dst)
    ring_second(53, kb, k_half, k_dst, kkeep)

    grad_nope = dot(gat[...], kup2, 0, 1)
    gn_ref[0] = grad_nope[:TOK, :DN].astype(BF16)
    gn_ref[1] = grad_nope[TOK:, DN:].astype(BF16)

    ring_second(42, vs, v_half, v_dst, vkeep)

    got(22, ra1)
    got(23, rb1)
    got(24, ra2)
    got(25, rb2)
    xsum[low_rows] = xsum[low_rows] + ra2[...].astype(F32) + rb1[...].astype(F32)
    xsum[high_rows] = xsum[high_rows] + ra1[...].astype(F32) + rb2[...].astype(F32)
    pad = jnp.zeros((8, 128), F32)
    for i in range(NZ):
        zs[i] = jnp.concatenate(
            [xsum[pl.ds(96 * i, 96)], xsum[pl.ds(96 * NZ + 24 * (i % 4), 24)], pad], axis=0
        ).astype(BF16)
    for d in range(1, NZ):
        far = (z + d) % NZ
        send(25 + d, zs.at[far], zrecv.at[d], device(z_=far))

    low, high = ring_last(53, kb[x, 0], kb[x, 1], k_dst)
    kx[0] = low.astype(BF16)
    kx[1] = high.astype(BF16)
    send(59, kx.at[1 - yl], kry, to_y)
    low, high = ring_last(42, vs[x, pl.ds(0, 16)], vs[x, pl.ds(16, 16)], v_dst)
    vfin[yl, x, pl.ds(0, 16)] = low.astype(BF16)
    vfin[yl, x, pl.ds(16, 16)] = high.astype(BF16)
    send(48, vfin.at[yl, x], vfin.at[yl, x], to_xp)
    send(49, vfin.at[yl, x], vfin.at[yl, x], to_xm)
    got(59, kry)
    kfin[x, yl] = (kx[yl].astype(F32) + kry[...].astype(F32)).astype(BF16)
    send(60, kfin.at[x, yl], kfin.at[x, yl], to_y)
    got(48, vfin.at[yl, xm])
    send(50, vfin.at[yl, xm, pl.ds(0, 16)], vfin.at[yl, xm, pl.ds(0, 16)], to_xp)
    got(49, vfin.at[yl, xp])
    send(51, vfin.at[yl, xp, pl.ds(16, 16)], vfin.at[yl, xp, pl.ds(16, 16)], to_xm)
    got(60, kfin.at[x, 1 - yl])
    send(61, kfin.at[x], kfin.at[x], to_xp)
    send(62, kfin.at[x], kfin.at[x], to_xm)
    got(50, vfin.at[yl, x2, pl.ds(0, 16)])
    got(51, vfin.at[yl, x2, pl.ds(16, 16)])
    send(52, vfin.at[yl], vfin.at[yl], to_y)

    zsum = zs[z].astype(F32)
    for d in range(1, NZ):
        got(25 + d, zrecv.at[d])
        zsum = zsum + zrecv[d].astype(F32)
    out_row, in_row = iota((128, 128), 0), iota((128, 128), 1)
    owner, place = out_row // 16, out_row % 16
    source = 24 * third(place) + 3 * owner + (place - 3 * third(place))
    order = jnp.where((source == in_row) & (place < 15), 1.0, 0.0).astype(BF16)
    sorted_rows = dot(order, zsum.astype(BF16)).astype(BF16)
    for i in range(8):
        ys[i] = sorted_rows[16 * i:16 * i + 16]

    def to_owner(d, e):
        far = (yh + d) % NYH
        return pltpu.make_async_remote_copy(
            src_ref=ys.at[far * 2 + e], dst_ref=yrecv.at[d, c],
            send_sem=ss.at[33 + 2 * d + e], recv_sem=rs.at[33 + 2 * d + c],
            device_id=device(yh_=far, yl_=(yl + c) % 2, c_=e), device_id_type=MESH,
        )

    for d in range(NYH):
        for e in range(2):
            if d == 0 and e == 0:
                @pl.when(c == 0)
                def _():
                    yrecv[0, 0] = ys[yh * 2]

                @pl.when(c == 1)
                def _():
                    to_owner(0, 0).start()
            else:
                to_owner(d, e).start()

    got(61, kfin.at[xm])
    send(63, kfin.at[xm, 0], kfin.at[xm, 0], to_xp)
    got(62, kfin.at[xp])
    send(64, kfin.at[xp, 1], kfin.at[xp, 1], to_xm)

    total = jnp.zeros((16, 128), F32)
    for d in range(NYH):
        for e in range(2):
            if d == 0 and e == 0:
                @pl.when(c == 1)
                def _():
                    got(33, yrecv.at[0, 0])
            else:
                got(33 + 2 * d + e, yrecv.at[d, e])
    for d in range(NYH):
        for e in range(2):
            total = total + yrecv[d, e].astype(F32)
    ol_ref[...] = jnp.concatenate([total[3 * t:3 * t + 3] for t in range(4)], axis=1).astype(BF16)
    rope = total[12:15]
    or_ref[...] = jnp.where(z >= NZ // 2, rope[:, DR:], rope[:, :DR]).astype(BF16)

    got(52, vfin.at[1 - yl])
    for a in range(8):
        for h in range(2):
            gv_ref[h, pl.ds(16 * a, 16), :] = vfin[a // 4, a % 4, pl.ds(16 * h, 16), :].astype(F32)
    got(63, kfin.at[x2, 0])
    got(64, kfin.at[x2, 1])
    for a in range(8):
        for h in range(2):
            gk_ref[h, pl.ds(16 * a, 16), :] = kfin[a // 2, a % 2, pl.ds(16 * h, 16), :].astype(F32)

    for copy in sent:
        copy.wait_send()
    for d in range(NYH):
        for e in range(2):
            if d == 0 and e == 0:
                @pl.when(c == 1)
                def _():
                    to_owner(0, 0).wait_send()
            else:
                to_owner(d, e).wait_send()


def on_device(query_nope, query_rope, grad_output, latents, key_rope, key_up, value_up, pair_order):
    scratch = [
        ((2, TOK, DN), BF16), ((2, DR, TOK), BF16), ((2, TOK, DN), BF16), ((DR, TOK), BF16),
        ((2, DN, DL), BF16), ((2, DN, DL), BF16), ((1, PAIRS), jnp.int32),
        ((4, 2, 2, BLK, 128), BF16), ((NX * 2 * TOK, EXT), BF16), ((EXT, NX * 2 * TOK), BF16),
        ((ROWS, EXT), BF16), ((EXT, ROWS), BF16), ((ROWS, DL), BF16), ((DL, ROWS), BF16),
        ((2 * DN, ROWS), BF16), ((2 * DN, ROWS), BF16),
        ((8, TOK, 128), F32), ((8, ROWS), F32), ((8, TOK, ROWS), F32), ((8, TOK, ROWS), F32),
        ((8, 8, ROWS), F32), ((8, 8, ROWS), F32),
        ((8 * TOK, ROWS), BF16), ((8 * TOK, ROWS), BF16), ((DL, ROWS), BF16), ((DL, ROWS), BF16),
        ((4, CH, 128), BF16), ((4, CH, 128), BF16), ((4, CH, 128), F32), ((4, CH, 128), BF16),
        ((CH, 128), F32),
        ((CHH, 128), BF16), ((CHH, 128), BF16), ((CHH, 128), BF16), ((CHH, 128), BF16),
        ((CHH, 128), BF16), ((CHH, 128), BF16),
        ((8, 128, 128), BF16), ((8, 128, 128), BF16), ((8, 16, 128), BF16), ((4, 2, 16, 128), BF16),
        ((2, 4, 32, DL), BF16), ((4, 32, DL), BF16), ((4, 32, DL), BF16),
    ] + [((16, DL), BF16)] * 6 + [((2, 4, 32, DL), BF16), ((2, 16, DL), BF16), ((4, 2, 32, DL), BF16)] + [
        ((32, DL), BF16)] * 6 + [
        ((2, 32, DL), BF16), ((2, 32, DL), BF16), ((32, DL), BF16), ((4, 2, 32, DL), BF16),
    ]
    outs = (
        ((2, TOK, DN), BF16), ((2, DR, TOK), BF16), ((3, DL), BF16), ((3, DR), BF16),
        ((2, DN, DL), F32), ((2, DN, DL), F32),
    )
    any_spec = pl.BlockSpec(memory_space=pl.ANY)
    vmem_spec = pl.BlockSpec(memory_space=pltpu.VMEM)
    grad_nope, grad_rope, own_lat, own_rope, grad_kup, grad_vup = pl.pallas_call(
        kernel,
        out_shape=[jax.ShapeDtypeStruct(s, t) for s, t in outs],
        in_specs=[any_spec] * 8,
        out_specs=[vmem_spec] * 6,
        scratch_shapes=[pltpu.VMEM(s, t) for s, t in scratch] + [
            pltpu.SemaphoreType.DMA((15,)),
            pltpu.SemaphoreType.DMA((N_SEM,)),
            pltpu.SemaphoreType.DMA((N_SEM,)),
        ],
        compiler_params=pltpu.CompilerParams(
            collective_id=0, has_side_effects=True, vmem_limit_bytes=60 * 1024 * 1024
        ),
        name="mla_backward",
    )(
        jnp.transpose(query_nope, (1, 0, 2)),
        jnp.transpose(query_rope, (1, 2, 0)),
        jnp.transpose(grad_output, (1, 0, 2)),
        latents,
        key_rope.T,
        key_up,
        value_up,
        pair_order.reshape(1, -1),
    )
    return (
        jnp.transpose(grad_nope, (1, 0, 2)),
        jnp.transpose(grad_rope, (2, 0, 1)),
        own_lat,
        own_rope,
        grad_kup,
        grad_vup,
    )


def solution(mesh):
    placed = (
        P("dp", "ctx", None),
        P("dp", "ctx", None),
        P("dp", "ctx", None),
        P("dp", None),
        P("dp", None),
        P("ctx", None, None),
        P("ctx", None, None),
        P(),
    )
    return jax.shard_map(
        on_device,
        mesh=mesh,
        in_specs=placed,
        out_specs=(
            P("dp", "ctx", None),
            P("dp", "ctx", None),
            P(("dp", "ctx"), None),
            P(("dp", "ctx"), None),
            P("ctx", None, None),
            P("ctx", None, None),
        ),
        check_vma=False,
    )
```

```python
import functools
import math

import jax
import jax.numpy as jnp
from jax import lax
from jax.experimental import pallas as pl
from jax.experimental.pallas import tpu as pltpu
from jax.sharding import PartitionSpec as P

MESH = pl.DeviceIdType.MESH
F32 = jnp.float32
BF16 = jnp.bfloat16
NEG = -1e30

NX, NYL, NZ, NYH = 4, 2, 8, 4
TOK = 192
HALF = TOK // 2
DL, DR, DN = 512, 64, 128
ROWS = 2 * TOK
EXT = DL + 2 * DR
PAIRS = 256
PER_DEV = 32
BLK = 4 * HALF + 48
CUT = 224
CH = NZ * 96 + 96
CHH = CH // 2

REL = (0, 3, 1, 2)

N_SEM = 65


def dot(a, b, ca=1, cb=0):
    return lax.dot_general(a, b, (((ca,), (cb,)), ((), ())), preferred_element_type=F32)


def iota(shape, axis):
    return lax.broadcasted_iota(jnp.int32, shape, axis)


def third(v):
    return (v * 43691) >> 17


def kernel(
    q_hbm, qr_hbm, go_hbm, lat_hbm, kr_hbm, kup_hbm, vup_hbm, po_hbm,
    gn_ref, gr_ref, ol_ref, or_ref, kfin, vfin,
    q_v, qr_v, go_v, kr_v, kup_v, vup_v, po_v,
    agb, lx_s, lxt, ax, axt, gx, gxt, qtx, gotx,
    pcol, prow, st, gw, mb, lb, wt, gst, lot, gat,
    csend, crecv, cown, xs, xsum, r2p, r2m, ra1, ra2, rb1, rb2,
    zs, zrecv, ys, yrecv,
    vb, vry, vs, vr2p, vr2m, vra1, vra2, vrb1, vrb2,
    vkeep, kb, kr2p, kr2m, kra1, kra2, krb1, krb2, kkeep, kx, kry,
    lsem, ss, rs,
):
    dp, ctx = lax.axis_index("dp"), lax.axis_index("ctx")
    x, yl = dp // NYL, dp % NYL
    z, yh, c = ctx // (NYH * 2), (ctx // 2) % NYH, ctx % 2
    sib = 1 - c
    xp, xm, x2 = (x + 1) % NX, (x + 3) % NX, (x + 2) % NX

    def device(x_=None, yl_=None, z_=None, yh_=None, c_=None):
        x_, yl_ = x if x_ is None else x_, yl if yl_ is None else yl_
        z_, yh_, c_ = z if z_ is None else z_, yh if yh_ is None else yh_, c if c_ is None else c_
        return {"dp": x_ * NYL + yl_, "ctx": (z_ * NYH + yh_) * 2 + c_}

    to_sib = device(c_=sib)
    to_y = device(yl_=1 - yl)
    to_xp, to_xm = device(x_=xp), device(x_=xm)

    def remote(n, src, dst, dev):
        return pltpu.make_async_remote_copy(
            src_ref=src, dst_ref=dst, send_sem=ss.at[n], recv_sem=rs.at[n],
            device_id=dev, device_id_type=MESH,
        )

    sent = []

    def send(n, src, dst, dev):
        copy = remote(n, src, dst, dev)
        copy.start()
        sent.append(copy)

    def got(n, dst):
        remote(n, dst, dst, to_sib).wait_recv()

    barrier = pltpu.get_barrier_semaphore()

    def greet(dev):
        pl.semaphore_signal(barrier, inc=1, device_id=dev, device_id_type=MESH)

    greet(to_xp)
    greet(to_xm)
    greet(device(yl_=1 - yl))
    for d in range(NYH):
        far = (yh + d) % NYH
        greet(device(yh_=far, c_=sib))
        greet(device(yh_=far, yl_=1 - yl, c_=sib))
        if d:
            greet(device(yh_=far, yl_=(yl + c) % 2, c_=c))
    for d in range(1, NZ):
        greet(device(z_=(z + d) % NZ))

    local = []

    def fetch(src, dst):
        copy = pltpu.make_async_copy(src, dst, lsem.at[len(local)])
        copy.start()
        local.append(copy)
        return copy

    kr_in = fetch(kr_hbm, kr_v)
    lat_in = []
    for h in range(2):
        for t in range(4):
            lat_in.append(fetch(
                lat_hbm.at[pl.ds(h * HALF, HALF), pl.ds(t * 128, 128)],
                agb.at[0, 0, h, pl.ds(t * HALF, HALF)],
            ))
    q_in, kup_in = fetch(q_hbm, q_v), fetch(kup_hbm, kup_v)
    go_in, vup_in = fetch(go_hbm, go_v), fetch(vup_hbm, vup_v)
    qr_in, po_in = fetch(qr_hbm, qr_v), fetch(po_hbm, po_v)

    kr_in.wait()
    kr_own = kr_v[...].astype(F32).T
    krp = jnp.concatenate([kr_own[:HALF], kr_own[HALF:]], axis=1).astype(BF16)
    agb[0, 0, 0, pl.ds(4 * HALF, 48)] = krp[:48]
    agb[0, 0, 1, pl.ds(4 * HALF, 48)] = krp[48:]
    for copy in lat_in:
        copy.wait()

    pl.semaphore_wait(barrier, 21)

    send(0, agb.at[0, 0, c], agb.at[0, 1, c], to_y)
    send(1, agb.at[0, 0, c], agb.at[1, 0, c], to_xp)
    send(2, agb.at[0, 0, c], agb.at[2, 0, c], to_xm)

    q_in.wait()
    go_in.wait()
    kup_in.wait()
    vup_in.wait()
    qr_in.wait()
    po_in.wait()
    blank = jnp.zeros((TOK, DN), F32)

    def block_diagonal(ref):
        both = ref[...].astype(F32)
        top = jnp.concatenate([both[:, 0, :], blank], axis=1)
        low = jnp.concatenate([blank, both[:, 1, :]], axis=1)
        return jnp.concatenate([top, low], axis=0)

    qx = block_diagonal(q_v)
    gox = block_diagonal(go_v)
    qtx[...] = qx.T.astype(BF16)
    gotx[...] = gox.T.astype(BF16)
    kup2 = kup_v[...].reshape(2 * DN, DL)
    vup2 = vup_v[...].reshape(2 * DN, DL)
    absorbed = dot(qx.astype(BF16), kup2)
    grad_lat = dot(gox.astype(BF16), vup2)
    qr_rows = jnp.concatenate([qr_v[0].astype(F32).T, qr_v[1].astype(F32).T], axis=0)
    qr2 = jnp.concatenate([qr_rows, qr_rows], axis=1)
    ax[:, :DL] = absorbed.astype(BF16)
    ax[:, DL:] = qr2.astype(BF16)
    axt[:DL, :] = absorbed.T.astype(BF16)
    axt[DL:, :] = qr2.T.astype(BF16)
    gx[...] = grad_lat.astype(BF16)
    gxt[...] = grad_lat.T.astype(BF16)

    po_row = jnp.broadcast_to(po_v[...].astype(F32), (8, PAIRS))
    slot_t = third(iota((PAIRS, ROWS), 1) % HALF)
    pick = jnp.where(iota((PAIRS, ROWS), 0) == dp * PER_DEV + slot_t, 1.0, 0.0).astype(BF16)
    pid_row = dot(po_row.astype(BF16), pick)
    within = iota((8, ROWS), 1)
    in_half = within % HALF
    late = (within % TOK) >= HALF
    group = jnp.where(late, 2.0 * PAIRS - 1.0 - pid_row, pid_row)
    prow[...] = group * 3.0 + (in_half - 3 * third(in_half)).astype(F32)

    po_col = jnp.broadcast_to(po_row[:1], (128, PAIRS)).T.astype(BF16)
    half_of = iota((TOK, PER_DEV), 0) % HALF
    expand = jnp.where(third(half_of) == iota((TOK, PER_DEV), 1), 1.0, 0.0).astype(BF16)
    row_no = iota((TOK, 128), 0)
    row_half = row_no % HALF
    for b in range(NX * NYL):
        pid = dot(expand, po_col[b * PER_DEV:(b + 1) * PER_DEV])
        grp = jnp.where(row_no >= HALF, 2.0 * PAIRS - 1.0 - pid, pid)
        pcol[b] = grp * 3.0 + (row_half - 3 * third(row_half)).astype(F32)

    scale = 1.0 / math.sqrt(DN + DR)
    low_lane = iota((HALF, 128), 1) < DR

    def attend(k, j):
        b = 2 * k + j
        key_dev = ((x + REL[k]) % NX) * NYL + (yl + j) % 2
        halves = []
        krp = jnp.concatenate(
            [agb[k, j, 0, pl.ds(4 * HALF, 48)], agb[k, j, 1, pl.ds(4 * HALF, 48)]], axis=0
        )
        zero = jnp.zeros((HALF, 128), BF16)
        for h in range(2):
            tiles = [agb[k, j, h, pl.ds(t * HALF, HALF)] for t in range(4)]
            tiles.append(jnp.where(low_lane, krp, zero) if h == 0 else jnp.where(low_lane, zero, krp))
            halves.append(jnp.concatenate(tiles, axis=1))
        lx = jnp.concatenate(halves, axis=0)
        lx_s[pl.ds(b * TOK, TOK), :] = lx
        s = dot(lx, axt[...]) * scale
        gw[b] = dot(lx[:, :DL], gxt[...])
        key_pos = pcol[key_dev]
        allowed = jnp.concatenate([key_pos] * 3, axis=1) <= prow[0:1]
        s = jnp.where(allowed, s, NEG)
        m = jnp.max(s, axis=0, keepdims=True)
        p = jnp.where(allowed, jnp.exp(s - m), 0.0)
        st[b] = p
        mb[b] = jnp.broadcast_to(m, (8, ROWS))
        lb[b] = jnp.broadcast_to(jnp.sum(p, axis=0, keepdims=True), (8, ROWS))

    def attend_pair(k):
        attend(k, 0)
        attend(k, 1)
        for t in range(EXT // 128):
            lxt[pl.ds(t * 128, 128), pl.ds(k * 2 * TOK, 2 * TOK)] = (
                lx_s[pl.ds(k * 2 * TOK, 2 * TOK), pl.ds(t * 128, 128)].astype(F32).T.astype(BF16)
            )

    def forward(n, j):
        got(1 + 2 * j, agb.at[1, j, c])
        send(5 + 2 * j, agb.at[1, j, c, pl.ds(0, CUT)], agb.at[3, j, c, pl.ds(0, CUT)], to_xp)
        send(n, agb.at[1, j, c], agb.at[1, j, c], to_sib)
        got(2 + 2 * j, agb.at[2, j, c])
        send(6 + 2 * j, agb.at[2, j, c, pl.ds(CUT, BLK - CUT)],
             agb.at[3, j, c, pl.ds(CUT, BLK - CUT)], to_xm)
        send(n + 1, agb.at[2, j, c], agb.at[2, j, c], to_sib)

    got(0, agb.at[0, 1, c])
    send(3, agb.at[0, 1, c], agb.at[1, 1, c], to_xp)
    send(4, agb.at[0, 1, c], agb.at[2, 1, c], to_xm)
    send(9, agb.at[0, 1, c], agb.at[0, 1, c], to_sib)
    forward(10, 0)
    got(9, agb.at[0, 1, sib])
    attend_pair(0)
    forward(12, 1)
    got(10, agb.at[1, 0, sib])
    got(12, agb.at[1, 1, sib])
    attend_pair(1)
    for j in range(2):
        got(5 + 2 * j, agb.at[3, j, c, pl.ds(0, CUT)])
        got(6 + 2 * j, agb.at[3, j, c, pl.ds(CUT, BLK - CUT)])
        send(14 + j, agb.at[3, j, c], agb.at[3, j, c], to_sib)
    got(11, agb.at[2, 0, sib])
    got(13, agb.at[2, 1, sib])
    attend_pair(2)
    got(14, agb.at[3, 0, sib])
    got(15, agb.at[3, 1, sib])
    attend_pair(3)

    top = mb[0]
    for b in range(1, 8):
        top = jnp.maximum(top, mb[b])
    total = jnp.zeros_like(top)
    for b in range(8):
        share = jnp.exp(mb[b] - top)
        mb[b] = share
        total = total + lb[b] * share
    inv = 1.0 / total
    for b in range(8):
        w = st[b] * (mb[b] * inv)[:1]
        st[b] = w
        wt[pl.ds(b * TOK, TOK), :] = w.astype(BF16)

    dots = jnp.zeros((1, ROWS), F32)
    for t in range(4):
        part = dot(lxt[pl.ds(t * 128, 128), :], wt[...])
        dots = dots + jnp.sum(
            gxt[pl.ds(t * 128, 128), :].astype(F32) * part, axis=0, keepdims=True
        )
        lot[pl.ds(t * 128, 128), :] = part.astype(BF16)

    def ring_first(n, buf, halves, dst):
        lo, hi = halves
        send(n, buf.at[x2].at[lo], dst[0], to_xp)
        send(n + 1, buf.at[x2].at[hi], dst[1], to_xm)
        send(n + 2, buf.at[xp].at[hi], dst[2], to_xp)
        send(n + 3, buf.at[xm].at[lo], dst[4], to_xm)

    def ring_second(n, buf, halves, dst, keep):
        lo, hi = halves
        got(n, dst[0])
        keep[0] = (buf[xp, lo].astype(F32) + dst[0][...].astype(F32)).astype(BF16)
        send(n + 4, keep.at[0], dst[3], to_xp)
        got(n + 1, dst[1])
        keep[1] = (buf[xm, hi].astype(F32) + dst[1][...].astype(F32)).astype(BF16)
        send(n + 5, keep.at[1], dst[5], to_xm)

    def ring_last(n, own_lo, own_hi, dst):
        got(n + 2, dst[2])
        got(n + 3, dst[4])
        got(n + 4, dst[3])
        got(n + 5, dst[5])
        low = own_lo.astype(F32) + dst[3][...].astype(F32) + dst[4][...].astype(F32)
        high = own_hi.astype(F32) + dst[2][...].astype(F32) + dst[5][...].astype(F32)
        return low, high

    v_part = dot(gotx[...], lot[...], 1, 1).astype(BF16)
    for a in range(8):
        for h in range(2):
            vb[a // 4, a % 4, pl.ds(16 * h, 16), :] = v_part[DN * h + 16 * a:DN * h + 16 * a + 16]
    send(41, vb.at[1 - yl], vry, to_y)

    for b in range(8):
        gst[pl.ds(b * TOK, TOK), :] = (st[b] * (gw[b] - dots) * scale).astype(BF16)
    rope_rows = None
    for t in range(5):
        part = dot(lxt[pl.ds(t * 128, 128), :], gst[...])
        if t < 4:
            gat[pl.ds(t * 128, 128), :] = part.astype(BF16)
        else:
            rope_rows = (part[:DR] + part[DR:]).astype(BF16)
    gr_ref[0] = rope_rows[:, :TOK]
    gr_ref[1] = rope_rows[:, TOK:]

    k_part = dot(qtx[...], gat[...], 1, 1).astype(BF16)
    for a in range(8):
        for h in range(2):
            kb[a // 2, a % 2, pl.ds(16 * h, 16), :] = k_part[DN * h + 16 * a:DN * h + 16 * a + 16]
    k_dst = (kr2p, kr2m, kra1, kra2, krb1, krb2)
    k_half = (0, 1)
    ring_first(53, kb, k_half, k_dst)

    def terms(k, j):
        start = pl.multiple_of((2 * k + j) * TOK, TOK)
        g = gst[pl.ds(start, TOK), :]
        full = dot(g, ax[...])
        lat = full[:, :DL] + dot(wt[pl.ds(start, TOK), :], gx[...])
        rope = jnp.where(low_lane, full[:HALF, DL:], full[HALF:, DL:])
        return lat, rope

    def put_terms(lat, rope, dst):
        for i in range(NZ):
            dst[pl.ds(96 * i, 96), :] = jnp.concatenate(
                [lat[24 * i:24 * i + 24, 128 * t:128 * t + 128] for t in range(4)], axis=0
            ).astype(dst.dtype)
        dst[pl.ds(96 * NZ, 96), :] = rope.astype(dst.dtype)

    def both_cores(k, dst):
        got(16 + k, crecv.at[k])
        dst[...] = (cown[k] + crecv[k].astype(F32)).astype(dst.dtype)

    x_dst = (r2p, r2m, ra1, ra2, rb1, rb2)
    low_rows, high_rows = pl.ds(0, CHH), pl.ds(CHH, CHH)

    for n, k in enumerate((3, 2, 1, 0)):
        put_terms(*terms(k, sib), csend.at[k])
        send(16 + k, csend.at[k], crecv.at[k], to_sib)
        put_terms(*terms(k, c), cown.at[k])
        if n == 1:
            both_cores(3, xs.at[3])
            send(20, xs.at[3, low_rows], r2p, to_xp)
            send(21, xs.at[3, high_rows], r2m, to_xm)
        if n == 2:
            both_cores(2, xs.at[2])
            send(22, xs.at[2, high_rows], ra1, to_xp)
        if n == 3:
            both_cores(1, xs.at[1])
            send(23, xs.at[1, low_rows], rb1, to_xm)
    got(20, r2p)
    xs[0, low_rows] = (xs[2, low_rows].astype(F32) + r2p[...].astype(F32)).astype(BF16)
    send(24, xs.at[0, low_rows], ra2, to_xp)
    got(21, r2m)
    xs[0, high_rows] = (xs[1, high_rows].astype(F32) + r2m[...].astype(F32)).astype(BF16)
    send(25, xs.at[0, high_rows], rb2, to_xm)
    both_cores(0, xsum)

    got(41, vry)
    vs[...] = (vb[yl].astype(F32) + vry[...].astype(F32)).astype(BF16)
    v_dst = (vr2p, vr2m, vra1, vra2, vrb1, vrb2)
    v_half = (pl.ds(0, 16), pl.ds(16, 16))
    ring_first(42, vs, v_half, v_dst)
    ring_second(53, kb, k_half, k_dst, kkeep)

    grad_nope = dot(gat[...], kup2, 0, 1)
    gn_ref[0] = grad_nope[:TOK, :DN].astype(BF16)
    gn_ref[1] = grad_nope[TOK:, DN:].astype(BF16)

    ring_second(42, vs, v_half, v_dst, vkeep)

    got(22, ra1)
    got(23, rb1)
    got(24, ra2)
    got(25, rb2)
    xsum[low_rows] = xsum[low_rows] + ra2[...].astype(F32) + rb1[...].astype(F32)
    xsum[high_rows] = xsum[high_rows] + ra1[...].astype(F32) + rb2[...].astype(F32)
    pad = jnp.zeros((8, 128), F32)
    for i in range(NZ):
        zs[i] = jnp.concatenate(
            [xsum[pl.ds(96 * i, 96)], xsum[pl.ds(96 * NZ + 24 * (i % 4), 24)], pad], axis=0
        ).astype(BF16)
    for d in range(1, NZ):
        far = (z + d) % NZ
        send(25 + d, zs.at[far], zrecv.at[d], device(z_=far))

    low, high = ring_last(53, kb[x, 0], kb[x, 1], k_dst)
    kx[0] = low.astype(BF16)
    kx[1] = high.astype(BF16)
    send(59, kx.at[1 - yl], kry, to_y)
    low, high = ring_last(42, vs[x, pl.ds(0, 16)], vs[x, pl.ds(16, 16)], v_dst)
    vfin[yl, x, pl.ds(0, 16)] = low.astype(BF16)
    vfin[yl, x, pl.ds(16, 16)] = high.astype(BF16)
    send(48, vfin.at[yl, x], vfin.at[yl, x], to_xp)
    send(49, vfin.at[yl, x], vfin.at[yl, x], to_xm)
    got(59, kry)
    kfin[x, yl] = (kx[yl].astype(F32) + kry[...].astype(F32)).astype(BF16)
    send(60, kfin.at[x, yl], kfin.at[x, yl], to_y)
    got(48, vfin.at[yl, xm])
    send(50, vfin.at[yl, xm, pl.ds(0, 16)], vfin.at[yl, xm, pl.ds(0, 16)], to_xp)
    got(49, vfin.at[yl, xp])
    send(51, vfin.at[yl, xp, pl.ds(16, 16)], vfin.at[yl, xp, pl.ds(16, 16)], to_xm)
    got(60, kfin.at[x, 1 - yl])
    send(61, kfin.at[x], kfin.at[x], to_xp)
    send(62, kfin.at[x], kfin.at[x], to_xm)
    got(50, vfin.at[yl, x2, pl.ds(0, 16)])
    got(51, vfin.at[yl, x2, pl.ds(16, 16)])
    send(52, vfin.at[yl], vfin.at[yl], to_y)

    zsum = zs[z].astype(F32)
    for d in range(1, NZ):
        got(25 + d, zrecv.at[d])
        zsum = zsum + zrecv[d].astype(F32)
    out_row, in_row = iota((128, 128), 0), iota((128, 128), 1)
    owner, place = out_row // 16, out_row % 16
    source = 24 * third(place) + 3 * owner + (place - 3 * third(place))
    order = jnp.where((source == in_row) & (place < 15), 1.0, 0.0).astype(BF16)
    sorted_rows = dot(order, zsum.astype(BF16)).astype(BF16)
    for i in range(8):
        ys[i] = sorted_rows[16 * i:16 * i + 16]

    def to_owner(d, e):
        far = (yh + d) % NYH
        return pltpu.make_async_remote_copy(
            src_ref=ys.at[far * 2 + e], dst_ref=yrecv.at[d, c],
            send_sem=ss.at[33 + 2 * d + e], recv_sem=rs.at[33 + 2 * d + c],
            device_id=device(yh_=far, yl_=(yl + c) % 2, c_=e), device_id_type=MESH,
        )

    for d in range(NYH):
        for e in range(2):
            if d == 0 and e == 0:
                @pl.when(c == 0)
                def _():
                    yrecv[0, 0] = ys[yh * 2]

                @pl.when(c == 1)
                def _():
                    to_owner(0, 0).start()
            else:
                to_owner(d, e).start()

    got(61, kfin.at[xm])
    send(63, kfin.at[xm, 0], kfin.at[xm, 0], to_xp)
    got(62, kfin.at[xp])
    send(64, kfin.at[xp, 1], kfin.at[xp, 1], to_xm)

    total = jnp.zeros((16, 128), F32)
    for d in range(NYH):
        for e in range(2):
            if d == 0 and e == 0:
                @pl.when(c == 1)
                def _():
                    got(33, yrecv.at[0, 0])
            else:
                got(33 + 2 * d + e, yrecv.at[d, e])
    for d in range(NYH):
        for e in range(2):
            total = total + yrecv[d, e].astype(F32)
    ol_ref[...] = jnp.concatenate([total[3 * t:3 * t + 3] for t in range(4)], axis=1).astype(BF16)
    rope = total[12:15]
    or_ref[...] = jnp.where(z >= NZ // 2, rope[:, DR:], rope[:, :DR]).astype(BF16)

    got(52, vfin.at[1 - yl])
    got(63, kfin.at[x2, 0])
    got(64, kfin.at[x2, 1])
    for copy in sent:
        copy.wait_send()
    for d in range(NYH):
        for e in range(2):
            if d == 0 and e == 0:
                @pl.when(c == 1)
                def _():
                    to_owner(0, 0).wait_send()
            else:
                to_owner(d, e).wait_send()


def finish(gn_in, gr_in, ol_in, or_in, kfin, vfin, gn_ref, gr_ref, ol_ref, or_ref, gk_ref, gv_ref):
    gr_ref[...] = gr_in[...]
    ol_ref[...] = ol_in[...]
    or_ref[...] = or_in[...]
    for a in range(8):
        for h in range(2):
            gk_ref[h, pl.ds(16 * a, 16), :] = kfin[a // 2, a % 2, pl.ds(16 * h, 16), :].astype(F32)
            gv_ref[h, pl.ds(16 * a, 16), :] = vfin[a // 4, a % 4, pl.ds(16 * h, 16), :].astype(F32)
    gn_ref[...] = jnp.stack([gn_in[0].astype(F32), gn_in[1].astype(F32)], axis=1).astype(BF16)


def on_device(query_nope, query_rope, grad_output, latents, key_rope, key_up, value_up, pair_order):
    scratch = [
        ((TOK, 2, DN), BF16), ((2, DR, TOK), BF16), ((TOK, 2, DN), BF16), ((DR, TOK), BF16),
        ((2, DN, DL), BF16), ((2, DN, DL), BF16), ((1, PAIRS), jnp.int32),
        ((4, 2, 2, BLK, 128), BF16), ((NX * 2 * TOK, EXT), BF16), ((EXT, NX * 2 * TOK), BF16),
        ((ROWS, EXT), BF16), ((EXT, ROWS), BF16), ((ROWS, DL), BF16), ((DL, ROWS), BF16),
        ((2 * DN, ROWS), BF16), ((2 * DN, ROWS), BF16),
        ((8, TOK, 128), F32), ((8, ROWS), F32), ((8, TOK, ROWS), F32), ((8, TOK, ROWS), F32),
        ((8, 8, ROWS), F32), ((8, 8, ROWS), F32),
        ((8 * TOK, ROWS), BF16), ((8 * TOK, ROWS), BF16), ((DL, ROWS), BF16), ((DL, ROWS), BF16),
        ((4, CH, 128), BF16), ((4, CH, 128), BF16), ((4, CH, 128), F32), ((4, CH, 128), BF16),
        ((CH, 128), F32),
        ((CHH, 128), BF16), ((CHH, 128), BF16), ((CHH, 128), BF16), ((CHH, 128), BF16),
        ((CHH, 128), BF16), ((CHH, 128), BF16),
        ((8, 128, 128), BF16), ((8, 128, 128), BF16), ((8, 16, 128), BF16), ((4, 2, 16, 128), BF16),
        ((2, 4, 32, DL), BF16), ((4, 32, DL), BF16), ((4, 32, DL), BF16),
    ] + [((16, DL), BF16)] * 6 + [((2, 16, DL), BF16), ((4, 2, 32, DL), BF16)] + [
        ((32, DL), BF16)] * 6 + [
        ((2, 32, DL), BF16), ((2, 32, DL), BF16), ((32, DL), BF16),
    ]
    outs = (
        ((2, TOK, DN), BF16), ((2, DR, TOK), BF16), ((3, DL), BF16), ((3, DR), BF16),
        ((4, 2, 32, DL), BF16), ((2, 4, 32, DL), BF16),
    )
    any_spec = pl.BlockSpec(memory_space=pl.ANY)
    vmem_spec = pl.BlockSpec(memory_space=pltpu.VMEM)
    raw = pl.pallas_call(
        kernel,
        out_shape=[jax.ShapeDtypeStruct(s, t) for s, t in outs],
        in_specs=[any_spec] * 8,
        out_specs=[vmem_spec] * 6,
        scratch_shapes=[pltpu.VMEM(s, t) for s, t in scratch] + [
            pltpu.SemaphoreType.DMA((15,)),
            pltpu.SemaphoreType.DMA((N_SEM,)),
            pltpu.SemaphoreType.DMA((N_SEM,)),
        ],
        compiler_params=pltpu.CompilerParams(
            collective_id=0, has_side_effects=True, vmem_limit_bytes=60 * 1024 * 1024
        ),
        name="mla_backward",
    )(
        query_nope,
        jnp.transpose(query_rope, (1, 2, 0)),
        grad_output,
        latents,
        key_rope.T,
        key_up,
        value_up,
        pair_order.reshape(1, -1),
    )
    results = (
        ((TOK, 2, DN), BF16), ((2, DR, TOK), BF16), ((3, DL), BF16), ((3, DR), BF16),
        ((2, DN, DL), F32), ((2, DN, DL), F32),
    )
    grad_nope, grad_rope, own_lat, own_rope, grad_kup, grad_vup = pl.pallas_call(
        finish,
        out_shape=[jax.ShapeDtypeStruct(s, t) for s, t in results],
        in_specs=[vmem_spec] * 6,
        out_specs=[vmem_spec] * 6,
        name="finish",
    )(*raw)
    return grad_nope, jnp.transpose(grad_rope, (2, 0, 1)), own_lat, own_rope, grad_kup, grad_vup


def solution(mesh):
    placed = (
        P("dp", "ctx", None),
        P("dp", "ctx", None),
        P("dp", "ctx", None),
        P("dp", None),
        P("dp", None),
        P("ctx", None, None),
        P("ctx", None, None),
        P(),
    )
    return jax.shard_map(
        on_device,
        mesh=mesh,
        in_specs=placed,
        out_specs=(
            P("dp", "ctx", None),
            P("dp", "ctx", None),
            P(("dp", "ctx"), None),
            P(("dp", "ctx"), None),
            P("ctx", None, None),
            P("ctx", None, None),
        ),
        check_vma=False,
    )
```

```python
import functools
import math

import jax
import jax.numpy as jnp
from jax import lax
from jax.experimental import pallas as pl
from jax.experimental.pallas import tpu as pltpu
from jax.sharding import PartitionSpec as P

MESH = pl.DeviceIdType.MESH
F32 = jnp.float32
BF16 = jnp.bfloat16
NEG = -1e30

NX, NYL, NZ, NYH = 4, 2, 8, 4
TOK = 192
HALF = TOK // 2
DL, DR, DN = 512, 64, 128
ROWS = 2 * TOK
EXT = DL + 2 * DR
PAIRS = 256
PER_DEV = 32
BLK = 4 * HALF + 48
CUT = 224
CH = NZ * 96 + 96
CHH = CH // 2

REL = (0, 3, 1, 2)

N_SEM = 69


def dot(a, b, ca=1, cb=0):
    return lax.dot_general(a, b, (((ca,), (cb,)), ((), ())), preferred_element_type=F32)


def iota(shape, axis):
    return lax.broadcasted_iota(jnp.int32, shape, axis)


def third(v):
    return (v * 43691) >> 17


def kernel(
    q_hbm, qr_hbm, go_hbm, lat_hbm, kr_hbm, kup_hbm, vup_hbm, po_hbm,
    gn_ref, gr_ref, ol_ref, or_ref, kfin, vfin,
    q_v, qr_v, go_v, kr_v, kup_v, vup_v, po_v,
    agb, lx_s, lxt, ax, axt, gx, gxt, qtx, gotx,
    pcol, prow, st, gw, mb, lb, wt, gst, lot, gat,
    csend, crecv, cown, xs, xsum, r2p, r2m, ra1, ra2, rb1, rb2,
    zs, zrecv, ys, yrecv,
    vb, vry, vs, vr2p, vr2m, vra1, vra2, vrb1, vrb2, vkeep,
    kb, kry, ks, kr2p, kr2m, kra1, kra2, krb1, krb2, kkeep,
    lsem, ss, rs, known,
):
    dp, ctx = lax.axis_index("dp"), lax.axis_index("ctx")
    x, yl = dp // NYL, dp % NYL
    z, yh, c = ctx // (NYH * 2), (ctx // 2) % NYH, ctx % 2
    sib = 1 - c
    xp, xm, x2 = (x + 1) % NX, (x + 3) % NX, (x + 2) % NX

    def device(x_=None, yl_=None, z_=None, yh_=None, c_=None):
        x_, yl_ = x if x_ is None else x_, yl if yl_ is None else yl_
        z_, yh_, c_ = z if z_ is None else z_, yh if yh_ is None else yh_, c if c_ is None else c_
        return {"dp": x_ * NYL + yl_, "ctx": (z_ * NYH + yh_) * 2 + c_}

    to_sib = device(c_=sib)
    to_y = device(yl_=1 - yl)
    to_xp, to_xm = device(x_=xp), device(x_=xm)

    def remote(n, src, dst, dev):
        return pltpu.make_async_remote_copy(
            src_ref=src, dst_ref=dst, send_sem=ss.at[n], recv_sem=rs.at[n],
            device_id=dev, device_id_type=MESH,
        )

    sent = []

    def send(n, src, dst, dev):
        copy = remote(n, src, dst, dev)
        copy.start()
        sent.append(copy)

    def got(n, dst):
        remote(n, dst, dst, to_sib).wait_recv()

    barrier = pltpu.get_barrier_semaphore()

    row = yh * 2 + yl
    along_y = []
    for step in (1, 7):
        far = (row + step) % (2 * NYH)
        along_y.append(device(yl_=far % 2, yh_=far // 2))
    along_z = [device(z_=(z + step) % NZ) for step in (1, NZ - 1)]
    for dev in [to_sib, to_xp, to_xm] + along_y + along_z:
        pl.semaphore_signal(barrier, inc=1, device_id=dev, device_id_type=MESH)

    def tell(n):
        for dev in along_y + along_z:
            pl.semaphore_signal(known.at[n], inc=1, device_id=dev, device_id_type=MESH)

    def heard(n):
        pl.semaphore_wait(known.at[n], 4)

    local = []

    def fetch(src, dst):
        copy = pltpu.make_async_copy(src, dst, lsem.at[len(local)])
        copy.start()
        local.append(copy)
        return copy

    kr_in = fetch(kr_hbm, kr_v)
    lat_in = []
    for h in range(2):
        for t in range(4):
            lat_in.append(fetch(
                lat_hbm.at[pl.ds(h * HALF, HALF), pl.ds(t * 128, 128)],
                agb.at[0, 0, h, pl.ds(t * HALF, HALF)],
            ))
    q_in, kup_in = fetch(q_hbm, q_v), fetch(kup_hbm, kup_v)
    go_in, vup_in = fetch(go_hbm, go_v), fetch(vup_hbm, vup_v)
    qr_in, po_in = fetch(qr_hbm, qr_v), fetch(po_hbm, po_v)

    kr_in.wait()
    kr_own = kr_v[...].astype(F32).T
    krp = jnp.concatenate([kr_own[:HALF], kr_own[HALF:]], axis=1).astype(BF16)
    agb[0, 0, 0, pl.ds(4 * HALF, 48)] = krp[:48]
    agb[0, 0, 1, pl.ds(4 * HALF, 48)] = krp[48:]
    for copy in lat_in:
        copy.wait()

    pl.semaphore_wait(barrier, 7)

    send(0, agb.at[0, 0, c], agb.at[0, 1, c], to_y)
    send(1, agb.at[0, 0, c], agb.at[1, 0, c], to_xp)
    send(2, agb.at[0, 0, c], agb.at[2, 0, c], to_xm)
    tell(0)

    q_in.wait()
    go_in.wait()
    kup_in.wait()
    vup_in.wait()
    qr_in.wait()
    po_in.wait()
    blank = jnp.zeros((TOK, DN), F32)

    def block_diagonal(ref):
        both = ref[...].astype(F32)
        top = jnp.concatenate([both[:, 0, :], blank], axis=1)
        low = jnp.concatenate([blank, both[:, 1, :]], axis=1)
        return jnp.concatenate([top, low], axis=0)

    qx = block_diagonal(q_v)
    gox = block_diagonal(go_v)
    qtx[...] = qx.T.astype(BF16)
    gotx[...] = gox.T.astype(BF16)
    kup2 = kup_v[...].reshape(2 * DN, DL)
    vup2 = vup_v[...].reshape(2 * DN, DL)
    absorbed = dot(qx.astype(BF16), kup2)
    grad_lat = dot(gox.astype(BF16), vup2)
    qr_rows = jnp.concatenate([qr_v[0].astype(F32).T, qr_v[1].astype(F32).T], axis=0)
    qr2 = jnp.concatenate([qr_rows, qr_rows], axis=1)
    ax[:, :DL] = absorbed.astype(BF16)
    ax[:, DL:] = qr2.astype(BF16)
    axt[:DL, :] = absorbed.T.astype(BF16)
    axt[DL:, :] = qr2.T.astype(BF16)
    gx[...] = grad_lat.astype(BF16)
    gxt[...] = grad_lat.T.astype(BF16)

    po_row = jnp.broadcast_to(po_v[...].astype(F32), (8, PAIRS))
    slot_t = third(iota((PAIRS, ROWS), 1) % HALF)
    pick = jnp.where(iota((PAIRS, ROWS), 0) == dp * PER_DEV + slot_t, 1.0, 0.0).astype(BF16)
    pid_row = dot(po_row.astype(BF16), pick)
    within = iota((8, ROWS), 1)
    in_half = within % HALF
    late = (within % TOK) >= HALF
    group = jnp.where(late, 2.0 * PAIRS - 1.0 - pid_row, pid_row)
    prow[...] = group * 3.0 + (in_half - 3 * third(in_half)).astype(F32)

    po_col = jnp.broadcast_to(po_row[:1], (128, PAIRS)).T.astype(BF16)
    half_of = iota((TOK, PER_DEV), 0) % HALF
    expand = jnp.where(third(half_of) == iota((TOK, PER_DEV), 1), 1.0, 0.0).astype(BF16)
    row_no = iota((TOK, 128), 0)
    row_half = row_no % HALF
    for b in range(NX * NYL):
        pid = dot(expand, po_col[b * PER_DEV:(b + 1) * PER_DEV])
        grp = jnp.where(row_no >= HALF, 2.0 * PAIRS - 1.0 - pid, pid)
        pcol[b] = grp * 3.0 + (row_half - 3 * third(row_half)).astype(F32)

    scale = 1.0 / math.sqrt(DN + DR)
    low_lane = iota((HALF, 128), 1) < DR

    def attend(k, j):
        b = 2 * k + j
        key_dev = ((x + REL[k]) % NX) * NYL + (yl + j) % 2
        halves = []
        krp = jnp.concatenate(
            [agb[k, j, 0, pl.ds(4 * HALF, 48)], agb[k, j, 1, pl.ds(4 * HALF, 48)]], axis=0
        )
        zero = jnp.zeros((HALF, 128), BF16)
        for h in range(2):
            tiles = [agb[k, j, h, pl.ds(t * HALF, HALF)] for t in range(4)]
            tiles.append(jnp.where(low_lane, krp, zero) if h == 0 else jnp.where(low_lane, zero, krp))
            halves.append(jnp.concatenate(tiles, axis=1))
        lx = jnp.concatenate(halves, axis=0)
        lx_s[pl.ds(b * TOK, TOK), :] = lx
        s = dot(lx, axt[...]) * scale
        gw[b] = dot(lx[:, :DL], gxt[...])
        key_pos = pcol[key_dev]
        allowed = jnp.concatenate([key_pos] * 3, axis=1) <= prow[0:1]
        s = jnp.where(allowed, s, NEG)
        m = jnp.max(s, axis=0, keepdims=True)
        p = jnp.where(allowed, jnp.exp(s - m), 0.0)
        st[b] = p
        mb[b] = jnp.broadcast_to(m, (8, ROWS))
        lb[b] = jnp.broadcast_to(jnp.sum(p, axis=0, keepdims=True), (8, ROWS))

    def attend_pair(k):
        attend(k, 0)
        attend(k, 1)
        for t in range(EXT // 128):
            lxt[pl.ds(t * 128, 128), pl.ds(k * 2 * TOK, 2 * TOK)] = (
                lx_s[pl.ds(k * 2 * TOK, 2 * TOK), pl.ds(t * 128, 128)].astype(F32).T.astype(BF16)
            )

    def forward(n, j):
        got(1 + 2 * j, agb.at[1, j, c])
        send(5 + 2 * j, agb.at[1, j, c, pl.ds(0, CUT)], agb.at[3, j, c, pl.ds(0, CUT)], to_xp)
        send(n, agb.at[1, j, c], agb.at[1, j, c], to_sib)
        got(2 + 2 * j, agb.at[2, j, c])
        send(6 + 2 * j, agb.at[2, j, c, pl.ds(CUT, BLK - CUT)],
             agb.at[3, j, c, pl.ds(CUT, BLK - CUT)], to_xm)
        send(n + 1, agb.at[2, j, c], agb.at[2, j, c], to_sib)

    heard(0)
    tell(1)
    got(0, agb.at[0, 1, c])
    send(3, agb.at[0, 1, c], agb.at[1, 1, c], to_xp)
    send(4, agb.at[0, 1, c], agb.at[2, 1, c], to_xm)
    send(9, agb.at[0, 1, c], agb.at[0, 1, c], to_sib)
    forward(10, 0)
    heard(1)
    tell(2)
    got(9, agb.at[0, 1, sib])
    attend_pair(0)
    forward(12, 1)
    heard(2)
    tell(3)
    got(10, agb.at[1, 0, sib])
    got(12, agb.at[1, 1, sib])
    attend_pair(1)
    for j in range(2):
        got(5 + 2 * j, agb.at[3, j, c, pl.ds(0, CUT)])
        got(6 + 2 * j, agb.at[3, j, c, pl.ds(CUT, BLK - CUT)])
        send(14 + j, agb.at[3, j, c], agb.at[3, j, c], to_sib)
    got(11, agb.at[2, 0, sib])
    got(13, agb.at[2, 1, sib])
    attend_pair(2)
    got(14, agb.at[3, 0, sib])
    got(15, agb.at[3, 1, sib])
    attend_pair(3)
    heard(3)

    top = mb[0]
    for b in range(1, 8):
        top = jnp.maximum(top, mb[b])
    total = jnp.zeros_like(top)
    for b in range(8):
        share = jnp.exp(mb[b] - top)
        mb[b] = share
        total = total + lb[b] * share
    inv = 1.0 / total
    for b in range(8):
        w = st[b] * (mb[b] * inv)[:1]
        st[b] = w
        wt[pl.ds(b * TOK, TOK), :] = w.astype(BF16)

    dots = jnp.zeros((1, ROWS), F32)
    for t in range(4):
        part = dot(lxt[pl.ds(t * 128, 128), :], wt[...])
        dots = dots + jnp.sum(
            gxt[pl.ds(t * 128, 128), :].astype(F32) * part, axis=0, keepdims=True
        )
        lot[pl.ds(t * 128, 128), :] = part.astype(BF16)

    def ring_first(n, buf, halves, dst):
        lo, hi = halves
        send(n, buf.at[x2].at[lo], dst[0], to_xp)
        send(n + 1, buf.at[x2].at[hi], dst[1], to_xm)
        send(n + 2, buf.at[xp].at[hi], dst[2], to_xp)
        send(n + 3, buf.at[xm].at[lo], dst[4], to_xm)

    def ring_second(n, buf, halves, dst, keep):
        lo, hi = halves
        got(n, dst[0])
        keep[0] = (buf[xp, lo].astype(F32) + dst[0][...].astype(F32)).astype(BF16)
        send(n + 4, keep.at[0], dst[3], to_xp)
        got(n + 1, dst[1])
        keep[1] = (buf[xm, hi].astype(F32) + dst[1][...].astype(F32)).astype(BF16)
        send(n + 5, keep.at[1], dst[5], to_xm)

    def ring_last(n, buf, halves, dst, fin):
        got(n + 2, dst[2])
        got(n + 3, dst[4])
        got(n + 4, dst[3])
        got(n + 5, dst[5])
        for half, one, two in zip(halves, dst[3:1:-1], dst[4:6]):
            fin[yl, x, half] = (
                buf[x, half].astype(F32) + one[...].astype(F32) + two[...].astype(F32)
            ).astype(BF16)

    halves = (pl.ds(0, 16), pl.ds(16, 16))
    v_dst = (vr2p, vr2m, vra1, vra2, vrb1, vrb2)
    k_dst = (kr2p, kr2m, kra1, kra2, krb1, krb2)

    def to_pair(n, part, buf, dst):
        for a in range(8):
            for h in range(2):
                buf[a // 4, a % 4, pl.ds(16 * h, 16), :] = part[DN * h + 16 * a:DN * h + 16 * a + 16]
        send(n, buf.at[1 - yl], dst, to_y)

    def from_pair(n, buf, other, total):
        got(n, other)
        total[...] = (buf[yl].astype(F32) + other[...].astype(F32)).astype(BF16)

    def peers():
        for n, (dx, dy) in enumerate(((1, 0), (3, 0), (0, 1), (2, 0), (1, 1), (3, 1), (2, 1))):
            yield n, (x + dx) % NX, (x + NX - dx) % NX, (yl + dy) % 2

    def spread(n, fin):
        for i, to_x, _, side in peers():
            send(n + i, fin.at[yl, x], fin.at[yl, x], device(x_=to_x, yl_=side))

    def spread_got(n, fin):
        for i, _, from_x, side in peers():
            got(n + i, fin.at[side, from_x])

    for b in range(8):
        gst[pl.ds(b * TOK, TOK), :] = (st[b] * (gw[b] - dots) * scale).astype(BF16)

    def terms(k, j):
        start = pl.multiple_of((2 * k + j) * TOK, TOK)
        g = gst[pl.ds(start, TOK), :]
        full = dot(g, ax[...])
        lat = full[:, :DL] + dot(wt[pl.ds(start, TOK), :], gx[...])
        rope = jnp.where(low_lane, full[:HALF, DL:], full[HALF:, DL:])
        return lat, rope

    def put_terms(lat, rope, dst):
        for i in range(NZ):
            dst[pl.ds(96 * i, 96), :] = jnp.concatenate(
                [lat[24 * i:24 * i + 24, 128 * t:128 * t + 128] for t in range(4)], axis=0
            ).astype(dst.dtype)
        dst[pl.ds(96 * NZ, 96), :] = rope.astype(dst.dtype)

    def both_cores(k, dst):
        got(16 + k, crecv.at[k])
        dst[...] = (cown[k] + crecv[k].astype(F32)).astype(dst.dtype)

    low_rows, high_rows = pl.ds(0, CHH), pl.ds(CHH, CHH)

    def chunk(k):
        put_terms(*terms(k, sib), csend.at[k])
        send(16 + k, csend.at[k], crecv.at[k], to_sib)
        put_terms(*terms(k, c), cown.at[k])

    chunk(3)
    to_pair(41, dot(gotx[...], lot[...], 1, 1).astype(BF16), vb, vry)
    chunk(2)
    both_cores(3, xs.at[3])
    send(20, xs.at[3, low_rows], r2p, to_xp)
    send(21, xs.at[3, high_rows], r2m, to_xm)
    chunk(1)
    both_cores(2, xs.at[2])
    send(22, xs.at[2, high_rows], ra1, to_xp)
    chunk(0)
    both_cores(1, xs.at[1])
    send(23, xs.at[1, low_rows], rb1, to_xm)

    gat[...] = dot(lxt[:DL, :], gst[...]).astype(BF16)
    to_pair(48, dot(qtx[...], gat[...], 1, 1).astype(BF16), kb, kry)

    got(20, r2p)
    xs[0, low_rows] = (xs[2, low_rows].astype(F32) + r2p[...].astype(F32)).astype(BF16)
    send(24, xs.at[0, low_rows], ra2, to_xp)
    got(21, r2m)
    xs[0, high_rows] = (xs[1, high_rows].astype(F32) + r2m[...].astype(F32)).astype(BF16)
    send(25, xs.at[0, high_rows], rb2, to_xm)
    both_cores(0, xsum)

    from_pair(41, vb, vry, vs)
    ring_first(42, vs, halves, v_dst)

    rope2 = dot(lxt[DL:, :], gst[...])
    rope_rows = (rope2[:DR] + rope2[DR:]).astype(BF16)
    gr_ref[0] = rope_rows[:, :TOK]
    gr_ref[1] = rope_rows[:, TOK:]
    grad_nope = dot(gat[...], kup2, 0, 1)
    gn_ref[0] = grad_nope[:TOK, :DN].astype(BF16)
    gn_ref[1] = grad_nope[TOK:, DN:].astype(BF16)

    from_pair(48, kb, kry, ks)
    ring_first(49, ks, halves, k_dst)
    ring_second(42, vs, halves, v_dst, vkeep)

    got(22, ra1)
    got(23, rb1)
    got(24, ra2)
    got(25, rb2)
    xsum[low_rows] = xsum[low_rows] + ra2[...].astype(F32) + rb1[...].astype(F32)
    xsum[high_rows] = xsum[high_rows] + ra1[...].astype(F32) + rb2[...].astype(F32)
    pad = jnp.zeros((8, 128), F32)
    for i in range(NZ):
        zs[i] = jnp.concatenate(
            [xsum[pl.ds(96 * i, 96)], xsum[pl.ds(96 * NZ + 24 * (i % 4), 24)], pad], axis=0
        ).astype(BF16)
    for d in (4, 3, 5, 2, 6, 1, 7):
        far = (z + d) % NZ
        send(25 + d, zs.at[far], zrecv.at[d], device(z_=far))

    ring_last(42, vs, halves, v_dst, vfin)
    spread(55, vfin)
    ring_second(49, ks, halves, k_dst, kkeep)
    ring_last(49, ks, halves, k_dst, kfin)
    spread(62, kfin)

    out_row, in_row = iota((128, 128), 0), iota((128, 128), 1)
    owner, place = out_row // 16, out_row % 16
    source = 24 * third(place) + 3 * owner + (place - 3 * third(place))
    order = jnp.where((source == in_row) & (place < 15), 1.0, 0.0).astype(BF16)
    zsum = zs[z].astype(F32)
    for d in (1, 7, 2, 6, 3, 5, 4):
        got(25 + d, zrecv.at[d])
        zsum = zsum + zrecv[d].astype(F32)
    sorted_rows = dot(order, zsum.astype(BF16)).astype(BF16)
    for i in range(8):
        ys[i] = sorted_rows[16 * i:16 * i + 16]

    def to_owner(d, e):
        far = (yh + d) % NYH
        return pltpu.make_async_remote_copy(
            src_ref=ys.at[far * 2 + e], dst_ref=yrecv.at[d, c],
            send_sem=ss.at[33 + 2 * d + e], recv_sem=rs.at[33 + 2 * d + c],
            device_id=device(yh_=far, yl_=(yl + c) % 2, c_=e), device_id_type=MESH,
        )

    for d in range(NYH):
        for e in range(2):
            if d == 0 and e == 0:
                @pl.when(c == 0)
                def _():
                    yrecv[0, 0] = ys[yh * 2]

                @pl.when(c == 1)
                def _():
                    to_owner(0, 0).start()
            else:
                to_owner(d, e).start()

    spread_got(55, vfin)
    spread_got(62, kfin)

    total = jnp.zeros((16, 128), F32)
    for d in range(NYH):
        for e in range(2):
            if d == 0 and e == 0:
                @pl.when(c == 1)
                def _():
                    got(33, yrecv.at[0, 0])
            else:
                got(33 + 2 * d + e, yrecv.at[d, e])
    for d in range(NYH):
        for e in range(2):
            total = total + yrecv[d, e].astype(F32)
    ol_ref[...] = jnp.concatenate([total[3 * t:3 * t + 3] for t in range(4)], axis=1).astype(BF16)
    rope = total[12:15]
    or_ref[...] = jnp.where(z >= NZ // 2, rope[:, DR:], rope[:, :DR]).astype(BF16)

    for copy in sent:
        copy.wait_send()
    for d in range(NYH):
        for e in range(2):
            if d == 0 and e == 0:
                @pl.when(c == 1)
                def _():
                    to_owner(0, 0).wait_send()
            else:
                to_owner(d, e).wait_send()


def finish(gn_in, gr_in, ol_in, or_in, kfin, vfin, gn_ref, gr_ref, ol_ref, or_ref, gk_ref, gv_ref):
    gr_ref[...] = gr_in[...]
    ol_ref[...] = ol_in[...]
    or_ref[...] = or_in[...]
    for a in range(8):
        for h in range(2):
            gk_ref[h, pl.ds(16 * a, 16), :] = kfin[a // 4, a % 4, pl.ds(16 * h, 16), :].astype(F32)
            gv_ref[h, pl.ds(16 * a, 16), :] = vfin[a // 4, a % 4, pl.ds(16 * h, 16), :].astype(F32)
    gn_ref[...] = jnp.stack([gn_in[0].astype(F32), gn_in[1].astype(F32)], axis=1).astype(BF16)


def on_device(query_nope, query_rope, grad_output, latents, key_rope, key_up, value_up, pair_order):
    scratch = [
        ((TOK, 2, DN), BF16), ((2, DR, TOK), BF16), ((TOK, 2, DN), BF16), ((DR, TOK), BF16),
        ((2, DN, DL), BF16), ((2, DN, DL), BF16), ((1, PAIRS), jnp.int32),
        ((4, 2, 2, BLK, 128), BF16), ((NX * 2 * TOK, EXT), BF16), ((EXT, NX * 2 * TOK), BF16),
        ((ROWS, EXT), BF16), ((EXT, ROWS), BF16), ((ROWS, DL), BF16), ((DL, ROWS), BF16),
        ((2 * DN, ROWS), BF16), ((2 * DN, ROWS), BF16),
        ((8, TOK, 128), F32), ((8, ROWS), F32), ((8, TOK, ROWS), F32), ((8, TOK, ROWS), F32),
        ((8, 8, ROWS), F32), ((8, 8, ROWS), F32),
        ((8 * TOK, ROWS), BF16), ((8 * TOK, ROWS), BF16), ((DL, ROWS), BF16), ((DL, ROWS), BF16),
        ((4, CH, 128), BF16), ((4, CH, 128), BF16), ((4, CH, 128), F32), ((4, CH, 128), BF16),
        ((CH, 128), F32),
        ((CHH, 128), BF16), ((CHH, 128), BF16), ((CHH, 128), BF16), ((CHH, 128), BF16),
        ((CHH, 128), BF16), ((CHH, 128), BF16),
        ((8, 128, 128), BF16), ((8, 128, 128), BF16), ((8, 16, 128), BF16), ((4, 2, 16, 128), BF16),
    ] + (
        [((2, 4, 32, DL), BF16)] + [((4, 32, DL), BF16)] * 2 + [((16, DL), BF16)] * 6 + [((2, 16, DL), BF16)]
    ) * 2
    outs = (
        ((2, TOK, DN), BF16), ((2, DR, TOK), BF16), ((3, DL), BF16), ((3, DR), BF16),
        ((2, 4, 32, DL), BF16), ((2, 4, 32, DL), BF16),
    )
    any_spec = pl.BlockSpec(memory_space=pl.ANY)
    vmem_spec = pl.BlockSpec(memory_space=pltpu.VMEM)
    raw = pl.pallas_call(
        kernel,
        out_shape=[jax.ShapeDtypeStruct(s, t) for s, t in outs],
        in_specs=[any_spec] * 8,
        out_specs=[vmem_spec] * 6,
        scratch_shapes=[pltpu.VMEM(s, t) for s, t in scratch] + [
            pltpu.SemaphoreType.DMA((15,)),
            pltpu.SemaphoreType.DMA((N_SEM,)),
            pltpu.SemaphoreType.DMA((N_SEM,)),
            pltpu.SemaphoreType.REGULAR((4,)),
        ],
        compiler_params=pltpu.CompilerParams(
            collective_id=0, has_side_effects=True, vmem_limit_bytes=60 * 1024 * 1024
        ),
        name="mla_backward",
    )(
        query_nope,
        jnp.transpose(query_rope, (1, 2, 0)),
        grad_output,
        latents,
        key_rope.T,
        key_up,
        value_up,
        pair_order.reshape(1, -1),
    )
    results = (
        ((TOK, 2, DN), BF16), ((2, DR, TOK), BF16), ((3, DL), BF16), ((3, DR), BF16),
        ((2, DN, DL), F32), ((2, DN, DL), F32),
    )
    grad_nope, grad_rope, own_lat, own_rope, grad_kup, grad_vup = pl.pallas_call(
        finish,
        out_shape=[jax.ShapeDtypeStruct(s, t) for s, t in results],
        in_specs=[vmem_spec] * 6,
        out_specs=[vmem_spec] * 6,
        name="finish",
    )(*raw)
    return grad_nope, jnp.transpose(grad_rope, (2, 0, 1)), own_lat, own_rope, grad_kup, grad_vup


def solution(mesh):
    placed = (
        P("dp", "ctx", None),
        P("dp", "ctx", None),
        P("dp", "ctx", None),
        P("dp", None),
        P("dp", None),
        P("ctx", None, None),
        P("ctx", None, None),
        P(),
    )
    return jax.shard_map(
        on_device,
        mesh=mesh,
        in_specs=placed,
        out_specs=(
            P("dp", "ctx", None),
            P("dp", "ctx", None),
            P(("dp", "ctx"), None),
            P(("dp", "ctx"), None),
            P("ctx", None, None),
            P("ctx", None, None),
        ),
        check_vma=False,
    )
```

```python
import functools
import math

import jax
import jax.numpy as jnp
from jax import lax
from jax.experimental import pallas as pl
from jax.experimental.pallas import tpu as pltpu
from jax.sharding import PartitionSpec as P

MESH = pl.DeviceIdType.MESH
F32 = jnp.float32
BF16 = jnp.bfloat16
NEG = -1e30

NX, NYL, NZ, NYH = 4, 2, 8, 4
TOK = 192
HALF = TOK // 2
DL, DR, DN = 512, 64, 128
ROWS = 2 * TOK
EXT = DL + 2 * DR
PAIRS = 256
PER_DEV = 32
BLK = 4 * HALF + 48
CUT = 224
CH = NZ * 96 + 96
CHH = CH // 2

REL = (0, 3, 1, 2)

N_SEM = 101


def dot(a, b, ca=1, cb=0):
    return lax.dot_general(a, b, (((ca,), (cb,)), ((), ())), preferred_element_type=F32)


def iota(shape, axis):
    return lax.broadcasted_iota(jnp.int32, shape, axis)


def third(v):
    return (v * 43691) >> 17


def kernel(
    q_hbm, qr_hbm, go_hbm, lat_hbm, kr_hbm, kup_hbm, vup_hbm, po_hbm,
    gn_ref, gr_ref, ol_ref, or_ref, kfin, vfin,
    q_v, qr_v, go_v, kr_v, kup_v, vup_v, po_v,
    agb, lx_s, lxt, ax, axt, gx, gxt, qtx, gotx,
    pcol, prow, st, gw, mb, lb, wt, gst, lot, gat,
    csend, crecv, cown, xs, xsum, r2p, r2m, ra1, ra2, rb1, rb2,
    zs, zrecv, ys, yrecv,
    vb, vry, vs, vr2p, vr2m, vra1, vra2, vrb1, vrb2, vkeep,
    kb, kry, ks, kr2p, kr2m, kra1, kra2, krb1, krb2, kkeep,
    lsem, ss, rs, known,
):
    dp, ctx = lax.axis_index("dp"), lax.axis_index("ctx")
    x, yl = dp // NYL, dp % NYL
    z, yh, c = ctx // (NYH * 2), (ctx // 2) % NYH, ctx % 2
    sib = 1 - c
    xp, xm, x2 = (x + 1) % NX, (x + 3) % NX, (x + 2) % NX

    def device(x_=None, yl_=None, z_=None, yh_=None, c_=None):
        x_, yl_ = x if x_ is None else x_, yl if yl_ is None else yl_
        z_, yh_, c_ = z if z_ is None else z_, yh if yh_ is None else yh_, c if c_ is None else c_
        return {"dp": x_ * NYL + yl_, "ctx": (z_ * NYH + yh_) * 2 + c_}

    to_sib = device(c_=sib)
    to_y = device(yl_=1 - yl)
    to_xp, to_xm = device(x_=xp), device(x_=xm)

    def remote(n, src, dst, dev):
        return pltpu.make_async_remote_copy(
            src_ref=src, dst_ref=dst, send_sem=ss.at[n], recv_sem=rs.at[n],
            device_id=dev, device_id_type=MESH,
        )

    sent = []

    def send(n, src, dst, dev):
        copy = remote(n, src, dst, dev)
        copy.start()
        sent.append(copy)

    def got(n, dst):
        remote(n, dst, dst, to_sib).wait_recv()

    barrier = pltpu.get_barrier_semaphore()

    row = yh * 2 + yl
    along_y = []
    for step in (1, 7):
        far = (row + step) % (2 * NYH)
        along_y.append(device(yl_=far % 2, yh_=far // 2))
    along_z = [device(z_=(z + step) % NZ) for step in (1, NZ - 1)]
    for dev in [to_sib, to_xp, to_xm] + along_y + along_z:
        pl.semaphore_signal(barrier, inc=1, device_id=dev, device_id_type=MESH)

    def tell(n):
        for dev in along_y + along_z:
            pl.semaphore_signal(known.at[n], inc=1, device_id=dev, device_id_type=MESH)

    def heard(n):
        pl.semaphore_wait(known.at[n], 4)

    local = []

    def fetch(src, dst):
        copy = pltpu.make_async_copy(src, dst, lsem.at[len(local)])
        copy.start()
        local.append(copy)
        return copy

    kr_in = fetch(kr_hbm, kr_v)
    lat_in = []
    for h in range(2):
        for t in range(4):
            lat_in.append(fetch(
                lat_hbm.at[pl.ds(h * HALF, HALF), pl.ds(t * 128, 128)],
                agb.at[0, 0, h, pl.ds(t * HALF, HALF)],
            ))
    q_in, kup_in = fetch(q_hbm, q_v), fetch(kup_hbm, kup_v)
    go_in, vup_in = fetch(go_hbm, go_v), fetch(vup_hbm, vup_v)
    qr_in, po_in = fetch(qr_hbm, qr_v), fetch(po_hbm, po_v)

    kr_in.wait()
    kr_own = kr_v[...].astype(F32).T
    krp = jnp.concatenate([kr_own[:HALF], kr_own[HALF:]], axis=1).astype(BF16)
    agb[0, 0, 0, pl.ds(4 * HALF, 48)] = krp[:48]
    agb[0, 0, 1, pl.ds(4 * HALF, 48)] = krp[48:]
    for copy in lat_in:
        copy.wait()

    pl.semaphore_wait(barrier, 7)

    far = (row + 1 + 6 * c) % (2 * NYH)
    to_yg = device(yl_=far % 2, yh_=far // 2)
    pieces = (pl.ds(0, CUT), pl.ds(CUT, BLK - CUT))
    x_id, y_id, sib_id = 0, 16, 32

    def block(k, j, p, core=c):
        return agb.at[k, j, core, pieces[p]]

    def gather_x(k, j, p, source):
        dst = block(k, j, p)
        send(x_id + 4 * k + 2 * j + p, source, dst, to_xp if (k, p) in ((1, 0), (1, 1), (3, 0)) else to_xm)

    def gather_y(k, p):
        send(y_id + 2 * k + p, block(k, 0, p), block(k, 1, p), to_yg)

    def gather_sib(k, j, p):
        send(sib_id + 4 * k + 2 * j + p, block(k, j, p), block(k, j, p), to_sib)

    def from_x(k, j, p):
        got(x_id + 4 * k + 2 * j + p, block(k, j, p))

    def from_y(k, p):
        got(y_id + 2 * k + p, block(k, 1, p))

    def from_sib(k, j):
        for p in range(2):
            got(sib_id + 4 * k + 2 * j + p, block(k, j, p, sib))

    gather_x(1, 0, 0, block(0, 0, 0))
    gather_x(2, 0, 1, block(0, 0, 1))
    gather_y(0, 0)
    gather_x(1, 0, 1, block(0, 0, 1))
    gather_x(2, 0, 0, block(0, 0, 0))
    gather_y(0, 1)
    tell(0)

    q_in.wait()
    go_in.wait()
    kup_in.wait()
    vup_in.wait()
    qr_in.wait()
    po_in.wait()
    blank = jnp.zeros((TOK, DN), F32)

    def block_diagonal(ref):
        both = ref[...].astype(F32)
        top = jnp.concatenate([both[:, 0, :], blank], axis=1)
        low = jnp.concatenate([blank, both[:, 1, :]], axis=1)
        return jnp.concatenate([top, low], axis=0)

    qx = block_diagonal(q_v)
    gox = block_diagonal(go_v)
    qtx[...] = qx.T.astype(BF16)
    gotx[...] = gox.T.astype(BF16)
    kup2 = kup_v[...].reshape(2 * DN, DL)
    vup2 = vup_v[...].reshape(2 * DN, DL)
    absorbed = dot(qx.astype(BF16), kup2)
    grad_lat = dot(gox.astype(BF16), vup2)
    qr_rows = jnp.concatenate([qr_v[0].astype(F32).T, qr_v[1].astype(F32).T], axis=0)
    qr2 = jnp.concatenate([qr_rows, qr_rows], axis=1)
    ax[:, :DL] = absorbed.astype(BF16)
    ax[:, DL:] = qr2.astype(BF16)
    axt[:DL, :] = absorbed.astype(BF16).T
    axt[DL:, :] = qr2.astype(BF16).T
    gx[...] = grad_lat.astype(BF16)
    gxt[...] = grad_lat.astype(BF16).T

    po_row = jnp.broadcast_to(po_v[...].astype(F32), (8, PAIRS))
    slot_t = third(iota((PAIRS, ROWS), 1) % HALF)
    pick = jnp.where(iota((PAIRS, ROWS), 0) == dp * PER_DEV + slot_t, 1.0, 0.0).astype(BF16)
    pid_row = dot(po_row.astype(BF16), pick)
    within = iota((8, ROWS), 1)
    in_half = within % HALF
    late = (within % TOK) >= HALF
    group = jnp.where(late, 2.0 * PAIRS - 1.0 - pid_row, pid_row)
    prow[...] = group * 3.0 + (in_half - 3 * third(in_half)).astype(F32)

    po_col = jnp.broadcast_to(po_row[:1], (128, PAIRS)).T.astype(BF16)
    half_of = iota((TOK, PER_DEV), 0) % HALF
    expand = jnp.where(third(half_of) == iota((TOK, PER_DEV), 1), 1.0, 0.0).astype(BF16)
    row_no = iota((TOK, 128), 0)
    row_half = row_no % HALF
    for b in range(NX * NYL):
        pid = dot(expand, po_col[b * PER_DEV:(b + 1) * PER_DEV])
        grp = jnp.where(row_no >= HALF, 2.0 * PAIRS - 1.0 - pid, pid)
        pcol[b] = grp * 3.0 + (row_half - 3 * third(row_half)).astype(F32)

    scale = 1.0 / math.sqrt(DN + DR)
    low_lane = iota((HALF, 128), 1) < DR

    def attend(k, j):
        b = 2 * k + j
        key_dev = ((x + REL[k]) % NX) * NYL + (yl + j) % 2
        halves = []
        krp = jnp.concatenate(
            [agb[k, j, 0, pl.ds(4 * HALF, 48)], agb[k, j, 1, pl.ds(4 * HALF, 48)]], axis=0
        )
        zero = jnp.zeros((HALF, 128), BF16)
        for h in range(2):
            tiles = [agb[k, j, h, pl.ds(t * HALF, HALF)] for t in range(4)]
            tiles.append(jnp.where(low_lane, krp, zero) if h == 0 else jnp.where(low_lane, zero, krp))
            halves.append(jnp.concatenate(tiles, axis=1))
        lx = jnp.concatenate(halves, axis=0)
        lx_s[pl.ds(b * TOK, TOK), :] = lx
        s = dot(lx, axt[...]) * scale
        gw[b] = dot(lx[:, :DL], gxt[...])
        key_pos = pcol[key_dev]
        allowed = jnp.concatenate([key_pos] * 3, axis=1) <= prow[0:1]
        s = jnp.where(allowed, s, NEG)
        m = jnp.max(s, axis=0, keepdims=True)
        p = jnp.where(allowed, jnp.exp(s - m), 0.0)
        st[b] = p
        mb[b] = jnp.broadcast_to(m, (8, ROWS))
        lb[b] = jnp.broadcast_to(jnp.sum(p, axis=0, keepdims=True), (8, ROWS))

    def turn(k):
        for t in range(EXT // 128):
            lxt[pl.ds(t * 128, 128), pl.ds(k * 2 * TOK, 2 * TOK)] = (
                lx_s[pl.ds(k * 2 * TOK, 2 * TOK), pl.ds(t * 128, 128)].T
            )

    def on_from_x(k, p):
        from_x(k, 0, p)
        if (k, p) in ((1, 0), (2, 1)):
            gather_x(3, 0, p, block(k, 0, p))
        gather_y(k, p)
        gather_sib(k, 0, p)

    def on_from_y(k, p):
        from_y(k, p)
        if (k, p) in ((1, 0), (2, 1)):
            gather_x(3, 1, p, block(k, 1, p))
        gather_sib(k, 1, p)

    def on_far(j):
        for p in range(2):
            from_x(3, j, p)
            gather_sib(3, j, p)

    heard(0)
    tell(1)
    on_from_x(1, 0)
    on_from_x(2, 1)
    on_from_y(0, 0)
    on_from_y(0, 1)
    heard(1)
    tell(2)
    attend(0, 0)
    on_from_x(1, 1)
    on_from_x(2, 0)
    heard(2)
    tell(3)
    from_sib(0, 1)
    attend(0, 1)
    on_from_y(1, 0)
    on_from_y(2, 1)
    turn(0)
    on_far(0)
    from_sib(1, 0)
    attend(1, 0)
    on_from_y(1, 1)
    on_from_y(2, 0)
    from_sib(2, 0)
    attend(2, 0)
    from_sib(3, 0)
    attend(3, 0)
    on_far(1)
    from_sib(1, 1)
    attend(1, 1)
    turn(1)
    from_sib(2, 1)
    attend(2, 1)
    turn(2)
    from_sib(3, 1)
    attend(3, 1)
    turn(3)
    heard(3)

    top = mb[0]
    for b in range(1, 8):
        top = jnp.maximum(top, mb[b])
    total = jnp.zeros_like(top)
    for b in range(8):
        share = jnp.exp(mb[b] - top)
        mb[b] = share
        total = total + lb[b] * share
    inv = 1.0 / total
    for b in range(8):
        w = st[b] * (mb[b] * inv)[:1]
        st[b] = w
        wt[pl.ds(b * TOK, TOK), :] = w.astype(BF16)

    dots = jnp.zeros((1, ROWS), F32)
    for t in range(4):
        part = dot(lxt[pl.ds(t * 128, 128), :], wt[...])
        dots = dots + jnp.sum(
            gxt[pl.ds(t * 128, 128), :].astype(F32) * part, axis=0, keepdims=True
        )
        lot[pl.ds(t * 128, 128), :] = part.astype(BF16)

    def ring_first(n, buf, halves, dst):
        lo, hi = halves
        send(n, buf.at[x2].at[lo], dst[0], to_xp)
        send(n + 1, buf.at[x2].at[hi], dst[1], to_xm)
        send(n + 2, buf.at[xp].at[hi], dst[2], to_xp)
        send(n + 3, buf.at[xm].at[lo], dst[4], to_xm)

    def ring_second(n, buf, halves, dst, keep):
        lo, hi = halves
        got(n, dst[0])
        keep[0] = (buf[xp, lo].astype(F32) + dst[0][...].astype(F32)).astype(BF16)
        send(n + 4, keep.at[0], dst[3], to_xp)
        got(n + 1, dst[1])
        keep[1] = (buf[xm, hi].astype(F32) + dst[1][...].astype(F32)).astype(BF16)
        send(n + 5, keep.at[1], dst[5], to_xm)

    def ring_last(n, buf, halves, dst, fin):
        got(n + 2, dst[2])
        got(n + 3, dst[4])
        got(n + 4, dst[3])
        got(n + 5, dst[5])
        for half, one, two in zip(halves, dst[3:1:-1], dst[4:6]):
            fin[yl, x, half] = (
                buf[x, half].astype(F32) + one[...].astype(F32) + two[...].astype(F32)
            ).astype(BF16)

    halves = (pl.ds(0, 16), pl.ds(16, 16))
    v_dst = (vr2p, vr2m, vra1, vra2, vrb1, vrb2)
    k_dst = (kr2p, kr2m, kra1, kra2, krb1, krb2)

    def to_pair(n, part, buf, dst):
        for a in range(8):
            for h in range(2):
                buf[a // 4, a % 4, pl.ds(16 * h, 16), :] = part[DN * h + 16 * a:DN * h + 16 * a + 16]
        send(n, buf.at[1 - yl], dst, to_y)

    def from_pair(n, buf, other, total):
        got(n, other)
        total[...] = (buf[yl].astype(F32) + other[...].astype(F32)).astype(BF16)

    def peers():
        for n, (dx, dy) in enumerate(((1, 0), (3, 0), (0, 1), (2, 0), (1, 1), (3, 1), (2, 1))):
            yield n, (x + dx) % NX, (x + NX - dx) % NX, (yl + dy) % 2

    def spread(n, fin):
        for i, to_x, _, side in peers():
            send(n + i, fin.at[yl, x], fin.at[yl, x], device(x_=to_x, yl_=side))

    def spread_got(n, fin):
        for i, _, from_x, side in peers():
            got(n + i, fin.at[side, from_x])

    for b in range(8):
        gst[pl.ds(b * TOK, TOK), :] = (st[b] * (gw[b] - dots) * scale).astype(BF16)

    def terms(k, j):
        start = pl.multiple_of((2 * k + j) * TOK, TOK)
        g = gst[pl.ds(start, TOK), :]
        full = dot(g, ax[...])
        lat = full[:, :DL] + dot(wt[pl.ds(start, TOK), :], gx[...])
        rope = jnp.where(low_lane, full[:HALF, DL:], full[HALF:, DL:])
        return lat, rope

    def put_terms(lat, rope, dst):
        for i in range(NZ):
            dst[pl.ds(96 * i, 96), :] = jnp.concatenate(
                [lat[24 * i:24 * i + 24, 128 * t:128 * t + 128] for t in range(4)], axis=0
            ).astype(dst.dtype)
        dst[pl.ds(96 * NZ, 96), :] = rope.astype(dst.dtype)

    def both_cores(k, dst):
        got(48 + k, crecv.at[k])
        dst[...] = (cown[k] + crecv[k].astype(F32)).astype(dst.dtype)

    low_rows, high_rows = pl.ds(0, CHH), pl.ds(CHH, CHH)

    def chunk(k):
        put_terms(*terms(k, sib), csend.at[k])
        send(48 + k, csend.at[k], crecv.at[k], to_sib)
        put_terms(*terms(k, c), cown.at[k])

    chunk(3)
    to_pair(73, dot(gotx[...], lot[...], 1, 1).astype(BF16), vb, vry)
    chunk(2)
    both_cores(3, xs.at[3])
    send(52, xs.at[3, low_rows], r2p, to_xp)
    send(53, xs.at[3, high_rows], r2m, to_xm)
    chunk(1)
    both_cores(2, xs.at[2])
    send(54, xs.at[2, high_rows], ra1, to_xp)
    chunk(0)
    both_cores(1, xs.at[1])
    send(55, xs.at[1, low_rows], rb1, to_xm)

    gat[...] = dot(lxt[:DL, :], gst[...]).astype(BF16)
    to_pair(80, dot(qtx[...], gat[...], 1, 1).astype(BF16), kb, kry)

    got(52, r2p)
    xs[0, low_rows] = (xs[2, low_rows].astype(F32) + r2p[...].astype(F32)).astype(BF16)
    send(56, xs.at[0, low_rows], ra2, to_xp)
    got(53, r2m)
    xs[0, high_rows] = (xs[1, high_rows].astype(F32) + r2m[...].astype(F32)).astype(BF16)
    send(57, xs.at[0, high_rows], rb2, to_xm)
    both_cores(0, xsum)

    from_pair(73, vb, vry, vs)
    ring_first(74, vs, halves, v_dst)

    rope2 = dot(lxt[DL:, :], gst[...])
    rope_rows = (rope2[:DR] + rope2[DR:]).astype(BF16)
    gr_ref[0] = rope_rows[:, :TOK]
    gr_ref[1] = rope_rows[:, TOK:]
    grad_nope = dot(gat[...], kup2, 0, 1)
    gn_ref[0] = grad_nope[:TOK, :DN].astype(BF16)
    gn_ref[1] = grad_nope[TOK:, DN:].astype(BF16)

    from_pair(80, kb, kry, ks)
    ring_first(81, ks, halves, k_dst)

    got(54, ra1)
    got(55, rb1)
    got(56, ra2)
    got(57, rb2)
    xsum[low_rows] = xsum[low_rows] + ra2[...].astype(F32) + rb1[...].astype(F32)
    xsum[high_rows] = xsum[high_rows] + ra1[...].astype(F32) + rb2[...].astype(F32)
    pad = jnp.zeros((8, 128), F32)
    for i in range(NZ):
        zs[i] = jnp.concatenate(
            [xsum[pl.ds(96 * i, 96)], xsum[pl.ds(96 * NZ + 24 * (i % 4), 24)], pad], axis=0
        ).astype(BF16)
    for d in (4, 3, 5, 2, 6, 1, 7):
        far = (z + d) % NZ
        send(57 + d, zs.at[far], zrecv.at[d], device(z_=far))

    ring_second(74, vs, halves, v_dst, vkeep)
    ring_second(81, ks, halves, k_dst, kkeep)
    ring_last(74, vs, halves, v_dst, vfin)
    spread(87, vfin)
    ring_last(81, ks, halves, k_dst, kfin)
    spread(94, kfin)

    out_row, in_row = iota((128, 128), 0), iota((128, 128), 1)
    owner, place = out_row // 16, out_row % 16
    source = 24 * third(place) + 3 * owner + (place - 3 * third(place))
    order = jnp.where((source == in_row) & (place < 15), 1.0, 0.0).astype(BF16)
    zsum = zs[z].astype(F32)
    for d in (1, 7, 2, 6, 3, 5, 4):
        got(57 + d, zrecv.at[d])
        zsum = zsum + zrecv[d].astype(F32)
    sorted_rows = dot(order, zsum.astype(BF16)).astype(BF16)
    for i in range(8):
        ys[i] = sorted_rows[16 * i:16 * i + 16]

    def to_owner(d, e):
        far = (yh + d) % NYH
        return pltpu.make_async_remote_copy(
            src_ref=ys.at[far * 2 + e], dst_ref=yrecv.at[d, c],
            send_sem=ss.at[65 + 2 * d + e], recv_sem=rs.at[65 + 2 * d + c],
            device_id=device(yh_=far, yl_=(yl + c) % 2, c_=e), device_id_type=MESH,
        )

    for d in range(NYH):
        for e in range(2):
            if d == 0 and e == 0:
                @pl.when(c == 0)
                def _():
                    yrecv[0, 0] = ys[yh * 2]

                @pl.when(c == 1)
                def _():
                    to_owner(0, 0).start()
            else:
                to_owner(d, e).start()

    spread_got(87, vfin)
    spread_got(94, kfin)

    total = jnp.zeros((16, 128), F32)
    for d in range(NYH):
        for e in range(2):
            if d == 0 and e == 0:
                @pl.when(c == 1)
                def _():
                    got(65, yrecv.at[0, 0])
            else:
                got(65 + 2 * d + e, yrecv.at[d, e])
    for d in range(NYH):
        for e in range(2):
            total = total + yrecv[d, e].astype(F32)
    ol_ref[...] = jnp.concatenate([total[3 * t:3 * t + 3] for t in range(4)], axis=1).astype(BF16)
    rope = total[12:15]
    or_ref[...] = jnp.where(z >= NZ // 2, rope[:, DR:], rope[:, :DR]).astype(BF16)

    for copy in sent:
        copy.wait_send()
    for d in range(NYH):
        for e in range(2):
            if d == 0 and e == 0:
                @pl.when(c == 1)
                def _():
                    to_owner(0, 0).wait_send()
            else:
                to_owner(d, e).wait_send()


def finish(gn_in, gr_in, ol_in, or_in, kfin, vfin, gn_ref, gr_ref, ol_ref, or_ref, gk_ref, gv_ref):
    gr_ref[...] = gr_in[...]
    ol_ref[...] = ol_in[...]
    or_ref[...] = or_in[...]
    for a in range(8):
        for h in range(2):
            gk_ref[h, pl.ds(16 * a, 16), :] = kfin[a // 4, a % 4, pl.ds(16 * h, 16), :].astype(F32)
            gv_ref[h, pl.ds(16 * a, 16), :] = vfin[a // 4, a % 4, pl.ds(16 * h, 16), :].astype(F32)
    gn_ref[...] = jnp.stack([gn_in[0].astype(F32), gn_in[1].astype(F32)], axis=1).astype(BF16)


def on_device(query_nope, query_rope, grad_output, latents, key_rope, key_up, value_up, pair_order):
    scratch = [
        ((TOK, 2, DN), BF16), ((2, DR, TOK), BF16), ((TOK, 2, DN), BF16), ((DR, TOK), BF16),
        ((2, DN, DL), BF16), ((2, DN, DL), BF16), ((1, PAIRS), jnp.int32),
        ((4, 2, 2, BLK, 128), BF16), ((NX * 2 * TOK, EXT), BF16), ((EXT, NX * 2 * TOK), BF16),
        ((ROWS, EXT), BF16), ((EXT, ROWS), BF16), ((ROWS, DL), BF16), ((DL, ROWS), BF16),
        ((2 * DN, ROWS), BF16), ((2 * DN, ROWS), BF16),
        ((8, TOK, 128), F32), ((8, ROWS), F32), ((8, TOK, ROWS), F32), ((8, TOK, ROWS), F32),
        ((8, 8, ROWS), F32), ((8, 8, ROWS), F32),
        ((8 * TOK, ROWS), BF16), ((8 * TOK, ROWS), BF16), ((DL, ROWS), BF16), ((DL, ROWS), BF16),
        ((4, CH, 128), BF16), ((4, CH, 128), BF16), ((4, CH, 128), F32), ((4, CH, 128), BF16),
        ((CH, 128), F32),
        ((CHH, 128), BF16), ((CHH, 128), BF16), ((CHH, 128), BF16), ((CHH, 128), BF16),
        ((CHH, 128), BF16), ((CHH, 128), BF16),
        ((8, 128, 128), BF16), ((8, 128, 128), BF16), ((8, 16, 128), BF16), ((4, 2, 16, 128), BF16),
    ] + (
        [((2, 4, 32, DL), BF16)] + [((4, 32, DL), BF16)] * 2 + [((16, DL), BF16)] * 6 + [((2, 16, DL), BF16)]
    ) * 2
    outs = (
        ((2, TOK, DN), BF16), ((2, DR, TOK), BF16), ((3, DL), BF16), ((3, DR), BF16),
        ((2, 4, 32, DL), BF16), ((2, 4, 32, DL), BF16),
    )
    any_spec = pl.BlockSpec(memory_space=pl.ANY)
    vmem_spec = pl.BlockSpec(memory_space=pltpu.VMEM)
    raw = pl.pallas_call(
        kernel,
        out_shape=[jax.ShapeDtypeStruct(s, t) for s, t in outs],
        in_specs=[any_spec] * 8,
        out_specs=[vmem_spec] * 6,
        scratch_shapes=[pltpu.VMEM(s, t) for s, t in scratch] + [
            pltpu.SemaphoreType.DMA((15,)),
            pltpu.SemaphoreType.DMA((N_SEM,)),
            pltpu.SemaphoreType.DMA((N_SEM,)),
            pltpu.SemaphoreType.REGULAR((4,)),
        ],
        compiler_params=pltpu.CompilerParams(
            collective_id=0, has_side_effects=True, vmem_limit_bytes=60 * 1024 * 1024
        ),
        name="mla_backward",
    )(
        query_nope,
        jnp.transpose(query_rope, (1, 2, 0)),
        grad_output,
        latents,
        key_rope.T,
        key_up,
        value_up,
        pair_order.reshape(1, -1),
    )
    results = (
        ((TOK, 2, DN), BF16), ((2, DR, TOK), BF16), ((3, DL), BF16), ((3, DR), BF16),
        ((2, DN, DL), F32), ((2, DN, DL), F32),
    )
    grad_nope, grad_rope, own_lat, own_rope, grad_kup, grad_vup = pl.pallas_call(
        finish,
        out_shape=[jax.ShapeDtypeStruct(s, t) for s, t in results],
        in_specs=[vmem_spec] * 6,
        out_specs=[vmem_spec] * 6,
        name="finish",
    )(*raw)
    return grad_nope, jnp.transpose(grad_rope, (2, 0, 1)), own_lat, own_rope, grad_kup, grad_vup


def solution(mesh):
    placed = (
        P("dp", "ctx", None),
        P("dp", "ctx", None),
        P("dp", "ctx", None),
        P("dp", None),
        P("dp", None),
        P("ctx", None, None),
        P("ctx", None, None),
        P(),
    )
    return jax.shard_map(
        on_device,
        mesh=mesh,
        in_specs=placed,
        out_specs=(
            P("dp", "ctx", None),
            P("dp", "ctx", None),
            P(("dp", "ctx"), None),
            P(("dp", "ctx"), None),
            P("ctx", None, None),
            P("ctx", None, None),
        ),
        check_vma=False,
    )
```

```python
import functools
import math

import jax
import jax.numpy as jnp
from jax import lax
from jax.experimental import pallas as pl
from jax.experimental.pallas import tpu as pltpu
from jax.sharding import PartitionSpec as P

MESH = pl.DeviceIdType.MESH
F32 = jnp.float32
BF16 = jnp.bfloat16
NEG = -1e30

NX, NYL, NZ, NYH = 4, 2, 8, 4
TOK = 192
HALF = TOK // 2
DL, DR, DN = 512, 64, 128
ROWS = 2 * TOK
EXT = DL + 2 * DR
PAIRS = 256
PER_DEV = 32
BLK = 4 * HALF + 48
CUT = 224
CHA = NZ * 72 + 96
CHH = CHA // 2
CH = CHA + TOK

REL = (0, 3, 1, 2)

N_SEM = 111


def dot(a, b, ca=1, cb=0):
    return lax.dot_general(a, b, (((ca,), (cb,)), ((), ())), preferred_element_type=F32)


def iota(shape, axis):
    return lax.broadcasted_iota(jnp.int32, shape, axis)


def third(v):
    return (v * 43691) >> 17


def kernel(
    q_hbm, qr_hbm, go_hbm, lat_hbm, kr_hbm, kup_hbm, vup_hbm, po_hbm,
    gn_ref, gr_ref, ol_ref, or_ref, kfin, vfin,
    q_v, qr_v, go_v, kr_v, kup_v, vup_v, po_v,
    agb, lx_s, lxt, ax, axt, gx, gxt, qtx, gotx,
    pcol, prow, st, gw, mb, lb, wt, gst, lot, gat,
    csend, crecv, cown, xs, xsum, r2p, r2m, ra1, ra2, rb1, rb2,
    zs, zrecv, bs, brecv, bx, bxr, ys, yrecv,
    vb, vry, vs, vr2p, vr2m, vra1, vra2, vrb1, vrb2, vkeep,
    kb, kry, ks, kr2p, kr2m, kra1, kra2, krb1, krb2, kkeep,
    lsem, ss, rs, known,
):
    dp, ctx = lax.axis_index("dp"), lax.axis_index("ctx")
    x, yl = dp // NYL, dp % NYL
    z, yh, c = ctx // (NYH * 2), (ctx // 2) % NYH, ctx % 2
    sib = 1 - c
    xp, xm, x2 = (x + 1) % NX, (x + 3) % NX, (x + 2) % NX

    def device(x_=None, yl_=None, z_=None, yh_=None, c_=None):
        x_, yl_ = x if x_ is None else x_, yl if yl_ is None else yl_
        z_, yh_, c_ = z if z_ is None else z_, yh if yh_ is None else yh_, c if c_ is None else c_
        return {"dp": x_ * NYL + yl_, "ctx": (z_ * NYH + yh_) * 2 + c_}

    to_sib = device(c_=sib)
    to_y = device(yl_=1 - yl)
    to_xp, to_xm = device(x_=xp), device(x_=xm)

    def remote(n, src, dst, dev):
        return pltpu.make_async_remote_copy(
            src_ref=src, dst_ref=dst, send_sem=ss.at[n], recv_sem=rs.at[n],
            device_id=dev, device_id_type=MESH,
        )

    sent = []

    def send(n, src, dst, dev):
        copy = remote(n, src, dst, dev)
        copy.start()
        sent.append(copy)

    def got(n, dst):
        remote(n, dst, dst, to_sib).wait_recv()

    barrier = pltpu.get_barrier_semaphore()

    row = yh * 2 + yl
    along_y = []
    for step in (1, 7):
        far = (row + step) % (2 * NYH)
        along_y.append(device(yl_=far % 2, yh_=far // 2))
    along_z = [device(z_=(z + step) % NZ) for step in (1, NZ - 1)]
    for dev in [to_sib, to_xp, to_xm] + along_y + along_z:
        pl.semaphore_signal(barrier, inc=1, device_id=dev, device_id_type=MESH)

    def tell(n):
        for dev in along_y + along_z:
            pl.semaphore_signal(known.at[n], inc=1, device_id=dev, device_id_type=MESH)

    def heard(n):
        pl.semaphore_wait(known.at[n], 4)

    local = []

    def fetch(src, dst):
        copy = pltpu.make_async_copy(src, dst, lsem.at[len(local)])
        copy.start()
        local.append(copy)
        return copy

    kr_in = fetch(kr_hbm, kr_v)
    lat_in = []
    for h in range(2):
        for t in range(4):
            lat_in.append(fetch(
                lat_hbm.at[pl.ds(h * HALF, HALF), pl.ds(t * 128, 128)],
                agb.at[0, 0, h, pl.ds(t * HALF, HALF)],
            ))
    q_in, kup_in = fetch(q_hbm, q_v), fetch(kup_hbm, kup_v)
    go_in, vup_in = fetch(go_hbm, go_v), fetch(vup_hbm, vup_v)
    qr_in, po_in = fetch(qr_hbm, qr_v), fetch(po_hbm, po_v)

    kr_in.wait()
    kr_own = kr_v[...].astype(F32).T
    krp = jnp.concatenate([kr_own[:HALF], kr_own[HALF:]], axis=1).astype(BF16)
    agb[0, 0, 0, pl.ds(4 * HALF, 48)] = krp[:48]
    agb[0, 0, 1, pl.ds(4 * HALF, 48)] = krp[48:]
    for copy in lat_in:
        copy.wait()

    pl.semaphore_wait(barrier, 7)

    far = (row + 1 + 6 * c) % (2 * NYH)
    to_yg = device(yl_=far % 2, yh_=far // 2)
    pieces = (pl.ds(0, CUT), pl.ds(CUT, BLK - CUT))
    x_id, y_id, sib_id = 0, 16, 32

    def block(k, j, p, core=c):
        return agb.at[k, j, core, pieces[p]]

    def gather_x(k, j, p, source):
        dst = block(k, j, p)
        send(x_id + 4 * k + 2 * j + p, source, dst, to_xp if (k, p) in ((1, 0), (1, 1), (3, 0)) else to_xm)

    def gather_y(k, p):
        send(y_id + 2 * k + p, block(k, 0, p), block(k, 1, p), to_yg)

    def gather_sib(k, j, p):
        send(sib_id + 4 * k + 2 * j + p, block(k, j, p), block(k, j, p), to_sib)

    def from_x(k, j, p):
        got(x_id + 4 * k + 2 * j + p, block(k, j, p))

    def from_y(k, p):
        got(y_id + 2 * k + p, block(k, 1, p))

    def from_sib(k, j):
        for p in range(2):
            got(sib_id + 4 * k + 2 * j + p, block(k, j, p, sib))

    gather_x(1, 0, 0, block(0, 0, 0))
    gather_x(2, 0, 1, block(0, 0, 1))
    gather_y(0, 0)
    gather_x(1, 0, 1, block(0, 0, 1))
    gather_x(2, 0, 0, block(0, 0, 0))
    gather_y(0, 1)
    tell(0)

    q_in.wait()
    go_in.wait()
    kup_in.wait()
    vup_in.wait()
    qr_in.wait()
    po_in.wait()
    blank = jnp.zeros((TOK, DN), F32)

    def block_diagonal(ref):
        both = ref[...].astype(F32)
        top = jnp.concatenate([both[:, 0, :], blank], axis=1)
        low = jnp.concatenate([blank, both[:, 1, :]], axis=1)
        return jnp.concatenate([top, low], axis=0)

    qx = block_diagonal(q_v)
    gox = block_diagonal(go_v)
    qtx[...] = qx.T.astype(BF16)
    gotx[...] = gox.T.astype(BF16)
    kup2 = kup_v[...].reshape(2 * DN, DL)
    vup2 = vup_v[...].reshape(2 * DN, DL)
    absorbed = dot(qx.astype(BF16), kup2)
    grad_lat = dot(gox.astype(BF16), vup2)
    qr_rows = jnp.concatenate([qr_v[0].astype(F32).T, qr_v[1].astype(F32).T], axis=0)
    qr2 = jnp.concatenate([qr_rows, qr_rows], axis=1)
    ax[:, :DL] = absorbed.astype(BF16)
    ax[:, DL:] = qr2.astype(BF16)
    axt[:DL, :] = absorbed.astype(BF16).T
    axt[DL:, :] = qr2.astype(BF16).T
    gx[...] = grad_lat.astype(BF16)
    gxt[...] = grad_lat.astype(BF16).T

    po_row = jnp.broadcast_to(po_v[...].astype(F32), (8, PAIRS))
    slot_t = third(iota((PAIRS, ROWS), 1) % HALF)
    pick = jnp.where(iota((PAIRS, ROWS), 0) == dp * PER_DEV + slot_t, 1.0, 0.0).astype(BF16)
    pid_row = dot(po_row.astype(BF16), pick)
    within = iota((8, ROWS), 1)
    in_half = within % HALF
    late = (within % TOK) >= HALF
    group = jnp.where(late, 2.0 * PAIRS - 1.0 - pid_row, pid_row)
    prow[...] = group * 3.0 + (in_half - 3 * third(in_half)).astype(F32)

    po_col = jnp.broadcast_to(po_row[:1], (128, PAIRS)).T.astype(BF16)
    half_of = iota((TOK, PER_DEV), 0) % HALF
    expand = jnp.where(third(half_of) == iota((TOK, PER_DEV), 1), 1.0, 0.0).astype(BF16)
    row_no = iota((TOK, 128), 0)
    row_half = row_no % HALF
    for b in range(NX * NYL):
        pid = dot(expand, po_col[b * PER_DEV:(b + 1) * PER_DEV])
        grp = jnp.where(row_no >= HALF, 2.0 * PAIRS - 1.0 - pid, pid)
        pcol[b] = grp * 3.0 + (row_half - 3 * third(row_half)).astype(F32)

    scale = 1.0 / math.sqrt(DN + DR)
    low_lane = iota((HALF, 128), 1) < DR

    def attend(k, j):
        b = 2 * k + j
        key_dev = ((x + REL[k]) % NX) * NYL + (yl + j) % 2
        halves = []
        krp = jnp.concatenate(
            [agb[k, j, 0, pl.ds(4 * HALF, 48)], agb[k, j, 1, pl.ds(4 * HALF, 48)]], axis=0
        )
        zero = jnp.zeros((HALF, 128), BF16)
        for h in range(2):
            tiles = [agb[k, j, h, pl.ds(t * HALF, HALF)] for t in range(4)]
            tiles.append(jnp.where(low_lane, krp, zero) if h == 0 else jnp.where(low_lane, zero, krp))
            halves.append(jnp.concatenate(tiles, axis=1))
        lx = jnp.concatenate(halves, axis=0)
        lx_s[pl.ds(b * TOK, TOK), :] = lx
        s = dot(lx, axt[...]) * scale
        gw[b] = dot(lx[:, :DL], gxt[...])
        key_pos = pcol[key_dev]
        allowed = jnp.concatenate([key_pos] * 3, axis=1) <= prow[0:1]
        s = jnp.where(allowed, s, NEG)
        m = jnp.max(s, axis=0, keepdims=True)
        p = jnp.where(allowed, jnp.exp(s - m), 0.0)
        st[b] = p
        mb[b] = jnp.broadcast_to(m, (8, ROWS))
        lb[b] = jnp.broadcast_to(jnp.sum(p, axis=0, keepdims=True), (8, ROWS))

    def turn(k):
        for t in range(EXT // 128):
            lxt[pl.ds(t * 128, 128), pl.ds(k * 2 * TOK, 2 * TOK)] = (
                lx_s[pl.ds(k * 2 * TOK, 2 * TOK), pl.ds(t * 128, 128)].T
            )

    def on_from_x(k, p):
        from_x(k, 0, p)
        if (k, p) in ((1, 0), (2, 1)):
            gather_x(3, 0, p, block(k, 0, p))
        gather_y(k, p)
        gather_sib(k, 0, p)

    def on_from_y(k, p):
        from_y(k, p)
        if (k, p) in ((1, 0), (2, 1)):
            gather_x(3, 1, p, block(k, 1, p))
        gather_sib(k, 1, p)

    def on_far(j):
        for p in range(2):
            from_x(3, j, p)
            gather_sib(3, j, p)

    heard(0)
    tell(1)
    on_from_x(1, 0)
    on_from_x(2, 1)
    on_from_y(0, 0)
    on_from_y(0, 1)
    heard(1)
    tell(2)
    attend(0, 0)
    on_from_x(1, 1)
    on_from_x(2, 0)
    heard(2)
    tell(3)
    from_sib(0, 1)
    attend(0, 1)
    on_from_y(1, 0)
    on_from_y(2, 1)
    turn(0)
    on_far(0)
    from_sib(1, 0)
    attend(1, 0)
    on_from_y(1, 1)
    on_from_y(2, 0)
    from_sib(2, 0)
    attend(2, 0)
    from_sib(3, 0)
    attend(3, 0)
    on_far(1)
    from_sib(1, 1)
    attend(1, 1)
    turn(1)
    from_sib(2, 1)
    attend(2, 1)
    turn(2)
    from_sib(3, 1)
    attend(3, 1)
    turn(3)
    heard(3)

    top = mb[0]
    for b in range(1, 8):
        top = jnp.maximum(top, mb[b])
    total = jnp.zeros_like(top)
    for b in range(8):
        share = jnp.exp(mb[b] - top)
        mb[b] = share
        total = total + lb[b] * share
    inv = 1.0 / total
    for b in range(8):
        w = st[b] * (mb[b] * inv)[:1]
        st[b] = w
        wt[pl.ds(b * TOK, TOK), :] = w.astype(BF16)

    dots = jnp.zeros((1, ROWS), F32)
    for t in range(4):
        part = dot(lxt[pl.ds(t * 128, 128), :], wt[...])
        dots = dots + jnp.sum(
            gxt[pl.ds(t * 128, 128), :].astype(F32) * part, axis=0, keepdims=True
        )
        lot[pl.ds(t * 128, 128), :] = part.astype(BF16)

    def ring_first(n, buf, halves, dst):
        lo, hi = halves
        send(n, buf.at[x2].at[lo], dst[0], to_xp)
        send(n + 1, buf.at[x2].at[hi], dst[1], to_xm)
        send(n + 2, buf.at[xp].at[hi], dst[2], to_xp)
        send(n + 3, buf.at[xm].at[lo], dst[4], to_xm)

    def ring_second(n, buf, halves, dst, keep):
        lo, hi = halves
        got(n, dst[0])
        keep[0] = (buf[xp, lo].astype(F32) + dst[0][...].astype(F32)).astype(BF16)
        send(n + 4, keep.at[0], dst[3], to_xp)
        got(n + 1, dst[1])
        keep[1] = (buf[xm, hi].astype(F32) + dst[1][...].astype(F32)).astype(BF16)
        send(n + 5, keep.at[1], dst[5], to_xm)

    def ring_last(n, buf, halves, dst, fin):
        got(n + 2, dst[2])
        got(n + 3, dst[4])
        got(n + 4, dst[3])
        got(n + 5, dst[5])
        for half, one, two in zip(halves, dst[3:1:-1], dst[4:6]):
            fin[yl, x, half] = (
                buf[x, half].astype(F32) + one[...].astype(F32) + two[...].astype(F32)
            ).astype(BF16)

    halves = (pl.ds(0, 16), pl.ds(16, 16))
    v_dst = (vr2p, vr2m, vra1, vra2, vrb1, vrb2)
    k_dst = (kr2p, kr2m, kra1, kra2, krb1, krb2)

    def to_pair(n, part, buf, dst):
        for a in range(8):
            for h in range(2):
                buf[a // 4, a % 4, pl.ds(16 * h, 16), :] = part[DN * h + 16 * a:DN * h + 16 * a + 16]
        send(n, buf.at[1 - yl], dst, to_y)

    def from_pair(n, buf, other, total):
        got(n, other)
        total[...] = (buf[yl].astype(F32) + other[...].astype(F32)).astype(BF16)

    def peers():
        for n, (dx, dy) in enumerate(((1, 0), (3, 0), (0, 1), (2, 0), (1, 1), (3, 1), (2, 1))):
            yield n, (x + dx) % NX, (x + NX - dx) % NX, (yl + dy) % 2

    def spread(n, fin):
        for i, to_x, _, side in peers():
            send(n + i, fin.at[yl, x], fin.at[yl, x], device(x_=to_x, yl_=side))

    def spread_got(n, fin):
        for i, _, from_x, side in peers():
            got(n + i, fin.at[side, from_x])

    for b in range(8):
        gst[pl.ds(b * TOK, TOK), :] = (st[b] * (gw[b] - dots) * scale).astype(BF16)

    def terms(k, j):
        start = pl.multiple_of((2 * k + j) * TOK, TOK)
        g = gst[pl.ds(start, TOK), :]
        full = dot(g, ax[...])
        lat = full[:, :DL] + dot(wt[pl.ds(start, TOK), :], gx[...])
        rope = jnp.where(low_lane, full[:HALF, DL:], full[HALF:, DL:])
        return lat, rope

    def put_terms(lat, rope, dst):
        for i in range(0, NZ, 2):
            dst[pl.ds(72 * i, 144), :] = jnp.concatenate(
                [lat[24 * r:24 * r + 24, 128 * t:128 * t + 128] for r in (i, i + 1) for t in range(3)], axis=0
            ).astype(dst.dtype)
        dst[pl.ds(72 * NZ, 96), :] = rope.astype(dst.dtype)
        dst[pl.ds(CHA, TOK), :] = lat[:, 384:].astype(dst.dtype)

    def both_cores(k, dst):
        got(48 + k, crecv.at[k])
        rows = pl.ds(0, CHA)
        dst[...] = (cown[k, rows] + crecv[k, rows].astype(F32)).astype(dst.dtype)

    low_rows, high_rows = pl.ds(0, CHH), pl.ds(CHH, CHH)

    def chunk(k):
        put_terms(*terms(k, sib), csend.at[k])
        send(48 + k, csend.at[k], crecv.at[k], to_sib)
        put_terms(*terms(k, c), cown.at[k])

    chunk(3)
    to_pair(73, dot(gotx[...], lot[...], 1, 1).astype(BF16), vb, vry)
    chunk(2)
    both_cores(3, xs.at[3])
    send(52, xs.at[3, low_rows], r2p, to_xp)
    send(53, xs.at[3, high_rows], r2m, to_xm)
    chunk(1)
    both_cores(2, xs.at[2])
    send(54, xs.at[2, high_rows], ra1, to_xp)
    chunk(0)
    both_cores(1, xs.at[1])
    send(55, xs.at[1, low_rows], rb1, to_xm)

    gat[...] = dot(lxt[:DL, :], gst[...]).astype(BF16)
    to_pair(80, dot(qtx[...], gat[...], 1, 1).astype(BF16), kb, kry)

    got(52, r2p)
    xs[0, low_rows] = (xs[2, low_rows].astype(F32) + r2p[...].astype(F32)).astype(BF16)
    send(56, xs.at[0, low_rows], ra2, to_xp)
    got(53, r2m)
    xs[0, high_rows] = (xs[1, high_rows].astype(F32) + r2m[...].astype(F32)).astype(BF16)
    send(57, xs.at[0, high_rows], rb2, to_xm)
    both_cores(0, xsum)
    rows = pl.ds(CHA, TOK)
    parts = [cown[k, rows] + crecv[k, rows].astype(F32) for k in range(NX)]
    for i in range(NZ):
        bs[i] = jnp.concatenate([part[24 * i:24 * i + 24] for part in parts], axis=0).astype(BF16)
    for d in (4, 3, 5, 2, 6, 1, 7):
        far = (z + d) % NZ
        send(100 + d, bs.at[far], brecv.at[d], device(z_=far))

    from_pair(73, vb, vry, vs)
    ring_first(74, vs, halves, v_dst)

    rope2 = dot(lxt[DL:, :], gst[...])
    rope_rows = (rope2[:DR] + rope2[DR:]).astype(BF16)
    gr_ref[0] = rope_rows[:, :TOK]
    gr_ref[1] = rope_rows[:, TOK:]
    grad_nope = dot(gat[...], kup2, 0, 1)
    gn_ref[0] = grad_nope[:TOK, :DN].astype(BF16)
    gn_ref[1] = grad_nope[TOK:, DN:].astype(BF16)

    from_pair(80, kb, kry, ks)
    ring_first(81, ks, halves, k_dst)

    got(54, ra1)
    got(55, rb1)
    got(56, ra2)
    got(57, rb2)
    xsum[low_rows] = xsum[low_rows] + ra2[...].astype(F32) + rb1[...].astype(F32)
    xsum[high_rows] = xsum[high_rows] + ra1[...].astype(F32) + rb2[...].astype(F32)
    pad = jnp.zeros((8, 128), F32)
    for i in range(NZ):
        zs[i] = jnp.concatenate(
            [xsum[pl.ds(72 * i, 72)], xsum[pl.ds(72 * NZ + 24 * (i % 4), 24)]], axis=0
        ).astype(BF16)
    for d in (4, 3, 5, 2, 6, 1, 7):
        far = (z + d) % NZ
        send(57 + d, zs.at[far], zrecv.at[d], device(z_=far))

    fourth = bs[z].astype(F32)
    for d in (1, 7, 2, 6, 3, 5, 4):
        got(100 + d, brecv.at[d])
        fourth = fourth + brecv[d].astype(F32)
    for k, there, dev in ((3, 3, device(x_=x2)), (2, 1, to_xp), (1, 2, to_xm)):
        bx[k] = jnp.concatenate([fourth[24 * k:24 * k + 24], pad], axis=0).astype(BF16)
        send(107 + there, bx.at[k], bxr.at[there], dev)

    ring_second(74, vs, halves, v_dst, vkeep)
    ring_second(81, ks, halves, k_dst, kkeep)
    ring_last(74, vs, halves, v_dst, vfin)
    spread(87, vfin)
    ring_last(81, ks, halves, k_dst, kfin)
    spread(94, kfin)

    out_row, in_row = iota((128, 128), 0), iota((128, 128), 1)
    owner, place = out_row // 16, out_row % 16
    source = 24 * third(place) + 3 * owner + (place - 3 * third(place))
    order = jnp.where((source == in_row) & (place < 15), 1.0, 0.0).astype(BF16)
    own = fourth[:24]
    for k in range(1, NX):
        got(107 + k, bxr.at[k])
        own = own + bxr[k].astype(F32)[:24]
    zsum = zs[z].astype(F32)
    for d in (1, 7, 2, 6, 3, 5, 4):
        got(57 + d, zrecv.at[d])
        zsum = zsum + zrecv[d].astype(F32)
    zsum = jnp.concatenate([zsum[:72], own, zsum[72:], pad], axis=0)
    sorted_rows = dot(order, zsum.astype(BF16)).astype(BF16)
    for i in range(8):
        ys[i] = sorted_rows[16 * i:16 * i + 16]

    def to_owner(d, e):
        far = (yh + d) % NYH
        return pltpu.make_async_remote_copy(
            src_ref=ys.at[far * 2 + e], dst_ref=yrecv.at[d, c],
            send_sem=ss.at[65 + 2 * d + e], recv_sem=rs.at[65 + 2 * d + c],
            device_id=device(yh_=far, yl_=(yl + c) % 2, c_=e), device_id_type=MESH,
        )

    for d in range(NYH):
        for e in range(2):
            if d == 0 and e == 0:
                @pl.when(c == 0)
                def _():
                    yrecv[0, 0] = ys[yh * 2]

                @pl.when(c == 1)
                def _():
                    to_owner(0, 0).start()
            else:
                to_owner(d, e).start()

    spread_got(87, vfin)
    spread_got(94, kfin)

    total = jnp.zeros((16, 128), F32)
    for d in range(NYH):
        for e in range(2):
            if d == 0 and e == 0:
                @pl.when(c == 1)
                def _():
                    got(65, yrecv.at[0, 0])
            else:
                got(65 + 2 * d + e, yrecv.at[d, e])
    for d in range(NYH):
        for e in range(2):
            total = total + yrecv[d, e].astype(F32)
    ol_ref[...] = jnp.concatenate([total[3 * t:3 * t + 3] for t in range(4)], axis=1).astype(BF16)
    rope = total[12:15]
    or_ref[...] = jnp.where(z >= NZ // 2, rope[:, DR:], rope[:, :DR]).astype(BF16)

    for copy in sent:
        copy.wait_send()
    for d in range(NYH):
        for e in range(2):
            if d == 0 and e == 0:
                @pl.when(c == 1)
                def _():
                    to_owner(0, 0).wait_send()
            else:
                to_owner(d, e).wait_send()


def finish(gn_in, gr_in, ol_in, or_in, kfin, vfin, gn_ref, gr_ref, ol_ref, or_ref, gk_ref, gv_ref):
    gr_ref[...] = gr_in[...]
    ol_ref[...] = ol_in[...]
    or_ref[...] = or_in[...]
    for a in range(8):
        for h in range(2):
            gk_ref[h, pl.ds(16 * a, 16), :] = kfin[a // 4, a % 4, pl.ds(16 * h, 16), :].astype(F32)
            gv_ref[h, pl.ds(16 * a, 16), :] = vfin[a // 4, a % 4, pl.ds(16 * h, 16), :].astype(F32)
    gn_ref[...] = jnp.stack([gn_in[0].astype(F32), gn_in[1].astype(F32)], axis=1).astype(BF16)


def on_device(query_nope, query_rope, grad_output, latents, key_rope, key_up, value_up, pair_order):
    scratch = [
        ((TOK, 2, DN), BF16), ((2, DR, TOK), BF16), ((TOK, 2, DN), BF16), ((DR, TOK), BF16),
        ((2, DN, DL), BF16), ((2, DN, DL), BF16), ((1, PAIRS), jnp.int32),
        ((4, 2, 2, BLK, 128), BF16), ((NX * 2 * TOK, EXT), BF16), ((EXT, NX * 2 * TOK), BF16),
        ((ROWS, EXT), BF16), ((EXT, ROWS), BF16), ((ROWS, DL), BF16), ((DL, ROWS), BF16),
        ((2 * DN, ROWS), BF16), ((2 * DN, ROWS), BF16),
        ((8, TOK, 128), F32), ((8, ROWS), F32), ((8, TOK, ROWS), F32), ((8, TOK, ROWS), F32),
        ((8, 8, ROWS), F32), ((8, 8, ROWS), F32),
        ((8 * TOK, ROWS), BF16), ((8 * TOK, ROWS), BF16), ((DL, ROWS), BF16), ((DL, ROWS), BF16),
        ((4, CH, 128), BF16), ((4, CH, 128), BF16), ((4, CH, 128), F32), ((4, CHA, 128), BF16),
        ((CHA, 128), F32),
        ((CHH, 128), BF16), ((CHH, 128), BF16), ((CHH, 128), BF16), ((CHH, 128), BF16),
        ((CHH, 128), BF16), ((CHH, 128), BF16),
        ((8, 96, 128), BF16), ((8, 96, 128), BF16), ((8, 96, 128), BF16), ((8, 96, 128), BF16),
        ((4, 32, 128), BF16), ((4, 32, 128), BF16), ((8, 16, 128), BF16), ((4, 2, 16, 128), BF16),
    ] + (
        [((2, 4, 32, DL), BF16)] + [((4, 32, DL), BF16)] * 2 + [((16, DL), BF16)] * 6 + [((2, 16, DL), BF16)]
    ) * 2
    outs = (
        ((2, TOK, DN), BF16), ((2, DR, TOK), BF16), ((3, DL), BF16), ((3, DR), BF16),
        ((2, 4, 32, DL), BF16), ((2, 4, 32, DL), BF16),
    )
    any_spec = pl.BlockSpec(memory_space=pl.ANY)
    vmem_spec = pl.BlockSpec(memory_space=pltpu.VMEM)
    raw = pl.pallas_call(
        kernel,
        out_shape=[pltpu.VMEM(s, t) for s, t in outs],
        in_specs=[any_spec] * 8,
        out_specs=[vmem_spec] * 6,
        scratch_shapes=[pltpu.VMEM(s, t) for s, t in scratch] + [
            pltpu.SemaphoreType.DMA((15,)),
            pltpu.SemaphoreType.DMA((N_SEM,)),
            pltpu.SemaphoreType.DMA((N_SEM,)),
            pltpu.SemaphoreType.REGULAR((4,)),
        ],
        compiler_params=pltpu.CompilerParams(
            collective_id=0, has_side_effects=True, vmem_limit_bytes=60 * 1024 * 1024
        ),
        name="mla_backward",
    )(
        query_nope,
        jnp.transpose(query_rope, (1, 2, 0)),
        grad_output,
        latents,
        key_rope.T,
        key_up,
        value_up,
        pair_order.reshape(1, -1),
    )
    results = (
        ((TOK, 2, DN), BF16), ((2, DR, TOK), BF16), ((3, DL), BF16), ((3, DR), BF16),
        ((2, DN, DL), F32), ((2, DN, DL), F32),
    )
    grad_nope, grad_rope, own_lat, own_rope, grad_kup, grad_vup = pl.pallas_call(
        finish,
        out_shape=[jax.ShapeDtypeStruct(s, t) for s, t in results],
        in_specs=[vmem_spec] * 6,
        out_specs=[vmem_spec] * 6,
        name="finish",
    )(*[pltpu.with_memory_space_constraint(r, pltpu.VMEM) for r in raw])
    return grad_nope, jnp.transpose(grad_rope, (2, 0, 1)), own_lat, own_rope, grad_kup, grad_vup


def solution(mesh):
    placed = (
        P("dp", "ctx", None),
        P("dp", "ctx", None),
        P("dp", "ctx", None),
        P("dp", None),
        P("dp", None),
        P("ctx", None, None),
        P("ctx", None, None),
        P(),
    )
    return jax.shard_map(
        on_device,
        mesh=mesh,
        in_specs=placed,
        out_specs=(
            P("dp", "ctx", None),
            P("dp", "ctx", None),
            P(("dp", "ctx"), None),
            P(("dp", "ctx"), None),
            P("ctx", None, None),
            P("ctx", None, None),
        ),
        check_vma=False,
    )
```

```python
import functools
import math

import jax
import jax.numpy as jnp
from jax import lax
from jax.experimental import pallas as pl
from jax.experimental.pallas import tpu as pltpu
from jax.sharding import PartitionSpec as P

MESH = pl.DeviceIdType.MESH
F32 = jnp.float32
BF16 = jnp.bfloat16
NEG = -1e30

NX, NYL, NZ, NYH = 4, 2, 8, 4
TOK = 192
HALF = TOK // 2
DL, DR, DN = 512, 64, 128
ROWS = 2 * TOK
EXT = DL + 2 * DR
PAIRS = 256
PER_DEV = 32
BLK = 4 * HALF + 48
CUT = 224
CHA = NZ * 72 + 96
CHH = CHA // 2
CH = CHA + TOK

REL = (0, 3, 1, 2)

N_SEM = 111


def dot(a, b, ca=1, cb=0):
    return lax.dot_general(a, b, (((ca,), (cb,)), ((), ())), preferred_element_type=F32)


def iota(shape, axis):
    return lax.broadcasted_iota(jnp.int32, shape, axis)


def third(v):
    return (v * 43691) >> 17


def kernel(
    q_hbm, qr_hbm, go_hbm, lat_hbm, kr_hbm, kup_hbm, vup_hbm, po_hbm,
    gn_ref, gr_ref, ol_ref, or_ref, kfin, vfin,
    q_v, qr_v, go_v, kr_v, kup_v, vup_v, po_v,
    agb, lx_s, lxt, ax, axt, gx, gxt, qtx, gotx,
    pcol, prow, st, gw, mb, lb, lacc, mtop, wt, gst, lot, gat,
    csend, crecv, cown, xs, xsum, r2p, r2m, ra1, ra2, rb1, rb2,
    zs, zrecv, bs, brecv, bx, bxr, ys, yrecv,
    vb, vry, vs, vr2p, vr2m, vra1, vra2, vrb1, vrb2, vkeep,
    kb, kry, ks, kr2p, kr2m, kra1, kra2, krb1, krb2, kkeep,
    lsem, ss, rs, known,
):
    dp, ctx = lax.axis_index("dp"), lax.axis_index("ctx")
    x, yl = dp // NYL, dp % NYL
    z, yh, c = ctx // (NYH * 2), (ctx // 2) % NYH, ctx % 2
    sib = 1 - c
    xp, xm, x2 = (x + 1) % NX, (x + 3) % NX, (x + 2) % NX

    def device(x_=None, yl_=None, z_=None, yh_=None, c_=None):
        x_, yl_ = x if x_ is None else x_, yl if yl_ is None else yl_
        z_, yh_, c_ = z if z_ is None else z_, yh if yh_ is None else yh_, c if c_ is None else c_
        return {"dp": x_ * NYL + yl_, "ctx": (z_ * NYH + yh_) * 2 + c_}

    to_sib = device(c_=sib)
    to_y = device(yl_=1 - yl)
    to_xp, to_xm = device(x_=xp), device(x_=xm)

    def remote(n, src, dst, dev):
        return pltpu.make_async_remote_copy(
            src_ref=src, dst_ref=dst, send_sem=ss.at[n], recv_sem=rs.at[n],
            device_id=dev, device_id_type=MESH,
        )

    sent = []

    def send(n, src, dst, dev):
        copy = remote(n, src, dst, dev)
        copy.start()
        sent.append(copy)

    def got(n, dst):
        remote(n, dst, dst, to_sib).wait_recv()

    barrier = pltpu.get_barrier_semaphore()

    row = yh * 2 + yl
    along_y = []
    for step in (1, 7):
        far = (row + step) % (2 * NYH)
        along_y.append(device(yl_=far % 2, yh_=far // 2))
    along_z = [device(z_=(z + step) % NZ) for step in (1, NZ - 1)]
    for dev in [to_sib, to_xp, to_xm] + along_y + along_z:
        pl.semaphore_signal(barrier, inc=1, device_id=dev, device_id_type=MESH)

    def tell(n):
        for dev in along_y + along_z:
            pl.semaphore_signal(known.at[n], inc=1, device_id=dev, device_id_type=MESH)

    def heard(n):
        pl.semaphore_wait(known.at[n], 4)

    local = []

    def fetch(src, dst):
        copy = pltpu.make_async_copy(src, dst, lsem.at[len(local)])
        copy.start()
        local.append(copy)
        return copy

    kr_in = fetch(kr_hbm, kr_v)
    lat_in = []
    for h in range(2):
        for t in range(4):
            lat_in.append(fetch(
                lat_hbm.at[pl.ds(h * HALF, HALF), pl.ds(t * 128, 128)],
                agb.at[0, 0, h, pl.ds(t * HALF, HALF)],
            ))
    q_in, kup_in = fetch(q_hbm, q_v), fetch(kup_hbm, kup_v)
    go_in, vup_in = fetch(go_hbm, go_v), fetch(vup_hbm, vup_v)
    qr_in, po_in = fetch(qr_hbm, qr_v), fetch(po_hbm, po_v)

    for copy in lat_in:
        copy.wait()
    pl.semaphore_wait(barrier, 7)

    far = (row + 1 + 6 * c) % (2 * NYH)
    to_yg = device(yl_=far % 2, yh_=far // 2)
    pieces = (pl.ds(0, CUT), pl.ds(CUT, BLK - CUT))
    x_id, y_id, sib_id = 0, 16, 32

    def block(k, j, p, core=c):
        return agb.at[k, j, core, pieces[p]]

    def gather_x(k, j, p, source):
        dst = block(k, j, p)
        send(x_id + 4 * k + 2 * j + p, source, dst, to_xp if (k, p) in ((1, 0), (1, 1), (3, 0)) else to_xm)

    def gather_y(k, p):
        send(y_id + 2 * k + p, block(k, 0, p), block(k, 1, p), to_yg)

    def gather_sib(k, j, p):
        send(sib_id + 4 * k + 2 * j + p, block(k, j, p), block(k, j, p), to_sib)

    def from_x(k, j, p):
        got(x_id + 4 * k + 2 * j + p, block(k, j, p))

    def from_y(k, p):
        got(y_id + 2 * k + p, block(k, 1, p))

    def from_sib(k, j):
        for p in range(2):
            got(sib_id + 4 * k + 2 * j + p, block(k, j, p, sib))

    gather_x(1, 0, 0, block(0, 0, 0))
    kr_in.wait()
    kr_own = kr_v[...].astype(F32).T
    krp = jnp.concatenate([kr_own[:HALF], kr_own[HALF:]], axis=1).astype(BF16)
    agb[0, 0, 0, pl.ds(4 * HALF, 48)] = krp[:48]
    agb[0, 0, 1, pl.ds(4 * HALF, 48)] = krp[48:]
    gather_x(2, 0, 1, block(0, 0, 1))
    gather_y(0, 0)
    gather_x(1, 0, 1, block(0, 0, 1))
    gather_x(2, 0, 0, block(0, 0, 0))
    gather_y(0, 1)
    tell(0)

    q_in.wait()
    go_in.wait()
    kup_in.wait()
    vup_in.wait()
    qr_in.wait()
    po_in.wait()
    blank = jnp.zeros((TOK, DN), F32)

    def block_diagonal(ref):
        both = ref[...].astype(F32)
        top = jnp.concatenate([both[:, 0, :], blank], axis=1)
        low = jnp.concatenate([blank, both[:, 1, :]], axis=1)
        return jnp.concatenate([top, low], axis=0)

    qx = block_diagonal(q_v)
    gox = block_diagonal(go_v)
    qtx[...] = qx.T.astype(BF16)
    gotx[...] = gox.T.astype(BF16)
    kup2 = kup_v[...].reshape(2 * DN, DL)
    vup2 = vup_v[...].reshape(2 * DN, DL)
    absorbed = dot(qx.astype(BF16), kup2)
    grad_lat = dot(gox.astype(BF16), vup2)
    qr_rows = jnp.concatenate([qr_v[0].astype(F32).T, qr_v[1].astype(F32).T], axis=0)
    qr2 = jnp.concatenate([qr_rows, qr_rows], axis=1)
    ax[:, :DL] = absorbed.astype(BF16)
    ax[:, DL:] = qr2.astype(BF16)
    axt[:DL, :] = absorbed.astype(BF16).T
    axt[DL:, :] = qr2.astype(BF16).T
    gx[...] = grad_lat.astype(BF16)
    gxt[...] = grad_lat.astype(BF16).T

    po_row = jnp.broadcast_to(po_v[...].astype(F32), (8, PAIRS))
    slot_t = third(iota((PAIRS, ROWS), 1) % HALF)
    pick = jnp.where(iota((PAIRS, ROWS), 0) == dp * PER_DEV + slot_t, 1.0, 0.0).astype(BF16)
    pid_row = dot(po_row.astype(BF16), pick)
    within = iota((8, ROWS), 1)
    in_half = within % HALF
    late = (within % TOK) >= HALF
    group = jnp.where(late, 2.0 * PAIRS - 1.0 - pid_row, pid_row)
    prow[...] = group * 3.0 + (in_half - 3 * third(in_half)).astype(F32)

    po_col = jnp.broadcast_to(po_row[:1], (128, PAIRS)).T.astype(BF16)
    half_of = iota((TOK, PER_DEV), 0) % HALF
    expand = jnp.where(third(half_of) == iota((TOK, PER_DEV), 1), 1.0, 0.0).astype(BF16)
    row_no = iota((TOK, 128), 0)
    row_half = row_no % HALF
    for b in range(NX * NYL):
        pid = dot(expand, po_col[b * PER_DEV:(b + 1) * PER_DEV])
        grp = jnp.where(row_no >= HALF, 2.0 * PAIRS - 1.0 - pid, pid)
        pcol[b] = grp * 3.0 + (row_half - 3 * third(row_half)).astype(F32)

    scale = 1.0 / math.sqrt(DN + DR)
    low_lane = iota((HALF, 128), 1) < DR

    def attend(k, j):
        b = 2 * k + j
        key_dev = ((x + REL[k]) % NX) * NYL + (yl + j) % 2
        halves = []
        krp = jnp.concatenate(
            [agb[k, j, 0, pl.ds(4 * HALF, 48)], agb[k, j, 1, pl.ds(4 * HALF, 48)]], axis=0
        )
        zero = jnp.zeros((HALF, 128), BF16)
        for h in range(2):
            tiles = [agb[k, j, h, pl.ds(t * HALF, HALF)] for t in range(4)]
            tiles.append(jnp.where(low_lane, krp, zero) if h == 0 else jnp.where(low_lane, zero, krp))
            halves.append(jnp.concatenate(tiles, axis=1))
        lx = jnp.concatenate(halves, axis=0)
        lx_s[pl.ds(b * TOK, TOK), :] = lx
        s = dot(lx, axt[...]) * scale
        gw[b] = dot(lx[:, :DL], gxt[...])
        key_pos = pcol[key_dev]
        allowed = jnp.concatenate([key_pos] * 3, axis=1) <= prow[0:1]
        s = jnp.where(allowed, s, NEG)
        m = jnp.max(s, axis=0, keepdims=True)
        p = jnp.where(allowed, jnp.exp(s - m), 0.0)
        st[b] = p
        mb[b] = jnp.broadcast_to(m, (8, ROWS))
        lb[b] = jnp.broadcast_to(jnp.sum(p, axis=0, keepdims=True), (8, ROWS))

    def turn(k):
        for t in range(EXT // 128):
            lxt[pl.ds(t * 128, 128), pl.ds(k * 2 * TOK, 2 * TOK)] = (
                lx_s[pl.ds(k * 2 * TOK, 2 * TOK), pl.ds(t * 128, 128)].T
            )
        top = jnp.maximum(mb[2 * k], mb[2 * k + 1])
        both = [st[b] * jnp.exp(mb[b] - top)[:1] for b in (2 * k, 2 * k + 1)]
        lacc[k] = dot(
            lxt[pl.ds(0, DL), pl.ds(k * 2 * TOK, 2 * TOK)], jnp.concatenate(both, axis=0).astype(BF16)
        )
        mtop[k] = top

    def on_from_x(k, p):
        from_x(k, 0, p)
        if (k, p) in ((1, 0), (2, 1)):
            gather_x(3, 0, p, block(k, 0, p))
        gather_y(k, p)
        gather_sib(k, 0, p)

    def on_from_y(k, p):
        from_y(k, p)
        if (k, p) in ((1, 0), (2, 1)):
            gather_x(3, 1, p, block(k, 1, p))
        gather_sib(k, 1, p)

    def on_far(j):
        for p in range(2):
            from_x(3, j, p)
            gather_sib(3, j, p)

    heard(0)
    tell(1)
    on_from_x(1, 0)
    on_from_x(2, 1)
    on_from_y(0, 0)
    on_from_y(0, 1)
    heard(1)
    tell(2)
    attend(0, 0)
    on_from_x(1, 1)
    on_from_x(2, 0)
    heard(2)
    tell(3)
    from_sib(0, 1)
    attend(0, 1)
    on_from_y(1, 0)
    on_from_y(2, 1)
    turn(0)
    on_far(0)
    from_sib(1, 0)
    attend(1, 0)
    on_from_y(1, 1)
    on_from_y(2, 0)
    from_sib(2, 0)
    attend(2, 0)
    from_sib(3, 0)
    attend(3, 0)
    on_far(1)
    from_sib(1, 1)
    attend(1, 1)
    turn(1)
    from_sib(2, 1)
    attend(2, 1)
    turn(2)
    from_sib(3, 1)
    attend(3, 1)
    turn(3)
    heard(3)

    top = jnp.maximum(jnp.maximum(mtop[0], mtop[1]), jnp.maximum(mtop[2], mtop[3]))
    total = jnp.zeros_like(top)
    for b in range(8):
        share = jnp.exp(mb[b] - top)
        mb[b] = share
        total = total + lb[b] * share
    inv = 1.0 / total
    parts = [(jnp.exp(mtop[k] - top) * inv)[:1] for k in range(NX)]
    dots = jnp.zeros((1, ROWS), F32)
    for t in range(4):
        rows = pl.ds(t * 128, 128)
        part = lacc[0, rows] * parts[0]
        for k in range(1, NX):
            part = part + lacc[k, rows] * parts[k]
        dots = dots + jnp.sum(gxt[rows, :].astype(F32) * part, axis=0, keepdims=True)
        lot[rows, :] = part.astype(BF16)

    def ring_first(n, buf, halves, dst):
        lo, hi = halves
        send(n, buf.at[x2].at[lo], dst[0], to_xp)
        send(n + 1, buf.at[x2].at[hi], dst[1], to_xm)
        send(n + 2, buf.at[xp].at[hi], dst[2], to_xp)
        send(n + 3, buf.at[xm].at[lo], dst[4], to_xm)

    def ring_second(n, buf, halves, dst, keep):
        lo, hi = halves
        got(n, dst[0])
        keep[0] = (buf[xp, lo].astype(F32) + dst[0][...].astype(F32)).astype(BF16)
        send(n + 4, keep.at[0], dst[3], to_xp)
        got(n + 1, dst[1])
        keep[1] = (buf[xm, hi].astype(F32) + dst[1][...].astype(F32)).astype(BF16)
        send(n + 5, keep.at[1], dst[5], to_xm)

    def ring_last(n, buf, halves, dst, fin):
        got(n + 2, dst[2])
        got(n + 3, dst[4])
        got(n + 4, dst[3])
        got(n + 5, dst[5])
        for half, one, two in zip(halves, dst[3:1:-1], dst[4:6]):
            fin[yl, x, half] = (
                buf[x, half].astype(F32) + one[...].astype(F32) + two[...].astype(F32)
            ).astype(BF16)

    halves = (pl.ds(0, 16), pl.ds(16, 16))
    v_dst = (vr2p, vr2m, vra1, vra2, vrb1, vrb2)
    k_dst = (kr2p, kr2m, kra1, kra2, krb1, krb2)

    def to_pair(n, part, buf, dst):
        for a in range(8):
            for h in range(2):
                buf[a // 4, a % 4, pl.ds(16 * h, 16), :] = part[DN * h + 16 * a:DN * h + 16 * a + 16]
        send(n, buf.at[1 - yl], dst, to_y)

    def from_pair(n, buf, other, total):
        got(n, other)
        total[...] = (buf[yl].astype(F32) + other[...].astype(F32)).astype(BF16)

    def peers():
        for n, (dx, dy) in enumerate(((1, 0), (3, 0), (0, 1), (2, 0), (1, 1), (3, 1), (2, 1))):
            yield n, (x + dx) % NX, (x + NX - dx) % NX, (yl + dy) % 2

    def spread(n, fin):
        for i, to_x, _, side in peers():
            send(n + i, fin.at[yl, x], fin.at[yl, x], device(x_=to_x, yl_=side))

    def spread_got(n, fin):
        for i, _, from_x, side in peers():
            got(n + i, fin.at[side, from_x])

    for b in range(8):
        w = st[b] * (mb[b] * inv)[:1]
        wt[pl.ds(b * TOK, TOK), :] = w.astype(BF16)
        gst[pl.ds(b * TOK, TOK), :] = (w * (gw[b] - dots) * scale).astype(BF16)

    def terms(k, j):
        start = pl.multiple_of((2 * k + j) * TOK, TOK)
        g = gst[pl.ds(start, TOK), :]
        full = dot(g, ax[...])
        lat = full[:, :DL] + dot(wt[pl.ds(start, TOK), :], gx[...])
        rope = jnp.where(low_lane, full[:HALF, DL:], full[HALF:, DL:])
        return lat, rope

    def put_terms(lat, rope, dst):
        for i in range(0, NZ, 2):
            dst[pl.ds(72 * i, 144), :] = jnp.concatenate(
                [lat[24 * r:24 * r + 24, 128 * t:128 * t + 128] for r in (i, i + 1) for t in range(3)], axis=0
            ).astype(dst.dtype)
        dst[pl.ds(72 * NZ, 96), :] = rope.astype(dst.dtype)
        dst[pl.ds(CHA, TOK), :] = lat[:, 384:].astype(dst.dtype)

    def both_cores(k, dst):
        got(48 + k, crecv.at[k])
        rows = pl.ds(0, CHA)
        dst[...] = (cown[k, rows] + crecv[k, rows].astype(F32)).astype(dst.dtype)

    low_rows, high_rows = pl.ds(0, CHH), pl.ds(CHH, CHH)

    def chunk(k):
        put_terms(*terms(k, sib), csend.at[k])
        send(48 + k, csend.at[k], crecv.at[k], to_sib)
        put_terms(*terms(k, c), cown.at[k])

    chunk(3)
    to_pair(73, dot(gotx[...], lot[...], 1, 1).astype(BF16), vb, vry)
    chunk(2)
    both_cores(3, xs.at[3])
    send(52, xs.at[3, low_rows], r2p, to_xp)
    send(53, xs.at[3, high_rows], r2m, to_xm)
    chunk(1)
    both_cores(2, xs.at[2])
    send(54, xs.at[2, high_rows], ra1, to_xp)
    chunk(0)
    both_cores(1, xs.at[1])
    send(55, xs.at[1, low_rows], rb1, to_xm)

    gat[...] = dot(lxt[:DL, :], gst[...]).astype(BF16)
    to_pair(80, dot(qtx[...], gat[...], 1, 1).astype(BF16), kb, kry)

    got(52, r2p)
    xs[0, low_rows] = (xs[2, low_rows].astype(F32) + r2p[...].astype(F32)).astype(BF16)
    send(56, xs.at[0, low_rows], ra2, to_xp)
    got(53, r2m)
    xs[0, high_rows] = (xs[1, high_rows].astype(F32) + r2m[...].astype(F32)).astype(BF16)
    send(57, xs.at[0, high_rows], rb2, to_xm)
    both_cores(0, xsum)
    rows = pl.ds(CHA, TOK)
    parts = [cown[k, rows] + crecv[k, rows].astype(F32) for k in range(NX)]
    for i in range(NZ):
        bs[i] = jnp.concatenate([part[24 * i:24 * i + 24] for part in parts], axis=0).astype(BF16)
    for d in (4, 3, 5, 2, 6, 1, 7):
        far = (z + d) % NZ
        send(100 + d, bs.at[far], brecv.at[d], device(z_=far))

    from_pair(73, vb, vry, vs)
    ring_first(74, vs, halves, v_dst)

    rope2 = dot(lxt[DL:, :], gst[...])
    rope_rows = (rope2[:DR] + rope2[DR:]).astype(BF16)
    gr_ref[0] = rope_rows[:, :TOK]
    gr_ref[1] = rope_rows[:, TOK:]
    grad_nope = dot(gat[...], kup2, 0, 1)
    gn_ref[0] = grad_nope[:TOK, :DN].astype(BF16)
    gn_ref[1] = grad_nope[TOK:, DN:].astype(BF16)

    from_pair(80, kb, kry, ks)
    ring_first(81, ks, halves, k_dst)

    got(54, ra1)
    got(55, rb1)
    got(56, ra2)
    got(57, rb2)
    xsum[low_rows] = xsum[low_rows] + ra2[...].astype(F32) + rb1[...].astype(F32)
    xsum[high_rows] = xsum[high_rows] + ra1[...].astype(F32) + rb2[...].astype(F32)
    pad = jnp.zeros((8, 128), F32)
    for i in range(NZ):
        zs[i] = jnp.concatenate(
            [xsum[pl.ds(72 * i, 72)], xsum[pl.ds(72 * NZ + 24 * (i % 4), 24)]], axis=0
        ).astype(BF16)
    for d in (4, 3, 5, 2, 6, 1, 7):
        far = (z + d) % NZ
        send(57 + d, zs.at[far], zrecv.at[d], device(z_=far))

    ring_second(74, vs, halves, v_dst, vkeep)
    ring_second(81, ks, halves, k_dst, kkeep)

    fourth = bs[z].astype(F32)
    for d in (1, 7, 2, 6, 3, 5, 4):
        got(100 + d, brecv.at[d])
        fourth = fourth + brecv[d].astype(F32)
    for k, there, dev in ((3, 3, device(x_=x2)), (2, 1, to_xp), (1, 2, to_xm)):
        bx[k] = jnp.concatenate([fourth[24 * k:24 * k + 24], pad], axis=0).astype(BF16)
        send(107 + there, bx.at[k], bxr.at[there], dev)

    ring_last(74, vs, halves, v_dst, vfin)
    spread(87, vfin)
    ring_last(81, ks, halves, k_dst, kfin)
    spread(94, kfin)

    out_row, in_row = iota((128, 128), 0), iota((128, 128), 1)
    owner, place = out_row // 16, out_row % 16
    source = 24 * third(place) + 3 * owner + (place - 3 * third(place))
    order = jnp.where((source == in_row) & (place < 15), 1.0, 0.0).astype(BF16)
    own = fourth[:24]
    for k in range(1, NX):
        got(107 + k, bxr.at[k])
        own = own + bxr[k].astype(F32)[:24]
    zsum = zs[z].astype(F32)
    for d in (1, 7, 2, 6, 3, 5, 4):
        got(57 + d, zrecv.at[d])
        zsum = zsum + zrecv[d].astype(F32)
    zsum = jnp.concatenate([zsum[:72], own, zsum[72:], pad], axis=0)
    sorted_rows = dot(order, zsum.astype(BF16)).astype(BF16)
    for i in range(8):
        ys[i] = sorted_rows[16 * i:16 * i + 16]

    def to_owner(d, e):
        far = (yh + d) % NYH
        return pltpu.make_async_remote_copy(
            src_ref=ys.at[far * 2 + e], dst_ref=yrecv.at[d, c],
            send_sem=ss.at[65 + 2 * d + e], recv_sem=rs.at[65 + 2 * d + c],
            device_id=device(yh_=far, yl_=(yl + c) % 2, c_=e), device_id_type=MESH,
        )

    for d in range(NYH):
        for e in range(2):
            if d == 0 and e == 0:
                @pl.when(c == 0)
                def _():
                    yrecv[0, 0] = ys[yh * 2]

                @pl.when(c == 1)
                def _():
                    to_owner(0, 0).start()
            else:
                to_owner(d, e).start()

    spread_got(87, vfin)
    spread_got(94, kfin)

    total = jnp.zeros((16, 128), F32)
    for d in range(NYH):
        for e in range(2):
            if d == 0 and e == 0:
                @pl.when(c == 1)
                def _():
                    got(65, yrecv.at[0, 0])
            else:
                got(65 + 2 * d + e, yrecv.at[d, e])
    for d in range(NYH):
        for e in range(2):
            total = total + yrecv[d, e].astype(F32)
    ol_ref[...] = jnp.concatenate([total[3 * t:3 * t + 3] for t in range(4)], axis=1).astype(BF16)
    rope = total[12:15]
    or_ref[...] = jnp.where(z >= NZ // 2, rope[:, DR:], rope[:, :DR]).astype(BF16)

    for copy in sent:
        copy.wait_send()
    for d in range(NYH):
        for e in range(2):
            if d == 0 and e == 0:
                @pl.when(c == 1)
                def _():
                    to_owner(0, 0).wait_send()
            else:
                to_owner(d, e).wait_send()


def finish(gn_in, gr_in, ol_in, or_in, kfin, vfin, gn_ref, gr_ref, ol_ref, or_ref, gk_ref, gv_ref):
    gr_ref[...] = gr_in[...]
    ol_ref[...] = ol_in[...]
    or_ref[...] = or_in[...]
    for a in range(8):
        for h in range(2):
            gk_ref[h, pl.ds(16 * a, 16), :] = kfin[a // 4, a % 4, pl.ds(16 * h, 16), :].astype(F32)
            gv_ref[h, pl.ds(16 * a, 16), :] = vfin[a // 4, a % 4, pl.ds(16 * h, 16), :].astype(F32)
    gn_ref[...] = jnp.stack([gn_in[0].astype(F32), gn_in[1].astype(F32)], axis=1).astype(BF16)


def on_device(query_nope, query_rope, grad_output, latents, key_rope, key_up, value_up, pair_order):
    scratch = [
        ((TOK, 2, DN), BF16), ((2, DR, TOK), BF16), ((TOK, 2, DN), BF16), ((DR, TOK), BF16),
        ((2, DN, DL), BF16), ((2, DN, DL), BF16), ((1, PAIRS), jnp.int32),
        ((4, 2, 2, BLK, 128), BF16), ((NX * 2 * TOK, EXT), BF16), ((EXT, NX * 2 * TOK), BF16),
        ((ROWS, EXT), BF16), ((EXT, ROWS), BF16), ((ROWS, DL), BF16), ((DL, ROWS), BF16),
        ((2 * DN, ROWS), BF16), ((2 * DN, ROWS), BF16),
        ((8, TOK, 128), F32), ((8, ROWS), F32), ((8, TOK, ROWS), F32), ((8, TOK, ROWS), F32),
        ((8, 8, ROWS), F32), ((8, 8, ROWS), F32), ((NX, DL, ROWS), F32), ((NX, 8, ROWS), F32),
        ((8 * TOK, ROWS), BF16), ((8 * TOK, ROWS), BF16), ((DL, ROWS), BF16), ((DL, ROWS), BF16),
        ((4, CH, 128), BF16), ((4, CH, 128), BF16), ((4, CH, 128), F32), ((4, CHA, 128), BF16),
        ((CHA, 128), F32),
        ((CHH, 128), BF16), ((CHH, 128), BF16), ((CHH, 128), BF16), ((CHH, 128), BF16),
        ((CHH, 128), BF16), ((CHH, 128), BF16),
        ((8, 96, 128), BF16), ((8, 96, 128), BF16), ((8, 96, 128), BF16), ((8, 96, 128), BF16),
        ((4, 32, 128), BF16), ((4, 32, 128), BF16), ((8, 16, 128), BF16), ((4, 2, 16, 128), BF16),
    ] + (
        [((2, 4, 32, DL), BF16)] + [((4, 32, DL), BF16)] * 2 + [((16, DL), BF16)] * 6 + [((2, 16, DL), BF16)]
    ) * 2
    outs = (
        ((2, TOK, DN), BF16), ((2, DR, TOK), BF16), ((3, DL), BF16), ((3, DR), BF16),
        ((2, 4, 32, DL), BF16), ((2, 4, 32, DL), BF16),
    )
    any_spec = pl.BlockSpec(memory_space=pl.ANY)
    vmem_spec = pl.BlockSpec(memory_space=pltpu.VMEM)
    raw = pl.pallas_call(
        kernel,
        out_shape=[pltpu.VMEM(s, t) for s, t in outs],
        in_specs=[any_spec] * 8,
        out_specs=[vmem_spec] * 6,
        scratch_shapes=[pltpu.VMEM(s, t) for s, t in scratch] + [
            pltpu.SemaphoreType.DMA((15,)),
            pltpu.SemaphoreType.DMA((N_SEM,)),
            pltpu.SemaphoreType.DMA((N_SEM,)),
            pltpu.SemaphoreType.REGULAR((4,)),
        ],
        compiler_params=pltpu.CompilerParams(
            collective_id=0, has_side_effects=True, vmem_limit_bytes=60 * 1024 * 1024
        ),
        name="mla_backward",
    )(
        query_nope,
        jnp.transpose(query_rope, (1, 2, 0)),
        grad_output,
        latents,
        key_rope.T,
        key_up,
        value_up,
        pair_order.reshape(1, -1),
    )
    results = (
        ((TOK, 2, DN), BF16), ((2, DR, TOK), BF16), ((3, DL), BF16), ((3, DR), BF16),
        ((2, DN, DL), F32), ((2, DN, DL), F32),
    )
    grad_nope, grad_rope, own_lat, own_rope, grad_kup, grad_vup = pl.pallas_call(
        finish,
        out_shape=[jax.ShapeDtypeStruct(s, t) for s, t in results],
        in_specs=[vmem_spec] * 6,
        out_specs=[vmem_spec] * 6,
        name="finish",
    )(*[pltpu.with_memory_space_constraint(r, pltpu.VMEM) for r in raw])
    return grad_nope, jnp.transpose(grad_rope, (2, 0, 1)), own_lat, own_rope, grad_kup, grad_vup


def solution(mesh):
    placed = (
        P("dp", "ctx", None),
        P("dp", "ctx", None),
        P("dp", "ctx", None),
        P("dp", None),
        P("dp", None),
        P("ctx", None, None),
        P("ctx", None, None),
        P(),
    )
    return jax.shard_map(
        on_device,
        mesh=mesh,
        in_specs=placed,
        out_specs=(
            P("dp", "ctx", None),
            P("dp", "ctx", None),
            P(("dp", "ctx"), None),
            P(("dp", "ctx"), None),
            P("ctx", None, None),
            P("ctx", None, None),
        ),
        check_vma=False,
    )
```

```python
import functools
import math

import jax
import jax.numpy as jnp
from jax import lax
from jax.experimental import pallas as pl
from jax.experimental.pallas import tpu as pltpu
from jax.sharding import PartitionSpec as P

MESH = pl.DeviceIdType.MESH
F32 = jnp.float32
BF16 = jnp.bfloat16
NEG = -1e30

NX, NYL, NZ, NYH = 4, 2, 8, 4
TOK = 192
HALF = TOK // 2
DL, DR, DN = 512, 64, 128
ROWS = 2 * TOK
EXT = DL + 2 * DR
PAIRS = 256
PER_DEV = 32
BLK = 4 * HALF + 48
CUT = 224
CHA = NZ * 72 + 96
CHH = CHA // 2
CH = CHA + TOK

REL = (0, 3, 1, 2)

N_SEM = 111


def dot(a, b, ca=1, cb=0):
    return lax.dot_general(a, b, (((ca,), (cb,)), ((), ())), preferred_element_type=F32)


def iota(shape, axis):
    return lax.broadcasted_iota(jnp.int32, shape, axis)


def third(v):
    return (v * 43691) >> 17


def kernel(
    q_hbm, qr_hbm, go_hbm, lat_hbm, kr_hbm, kup_hbm, vup_hbm, po_hbm,
    gn_ref, gr_ref, ol_ref, or_ref, kfin, vfin,
    q_v, qr_v, go_v, kr_v, kup_v, vup_v, po_v,
    agb, lx_s, lxt, ax, axt, gx, gxt, qtx, gotx,
    pcol, prow, st, gw, mb, lb, lacc, mtop, wt, gst, lot, gat,
    csend, crecv, cown, xs, xsum, r2p, r2m, ra1, ra2, rb1, rb2,
    zs, zrecv, bs, brecv, bx, bxr, ys, yrecv,
    vb, vry, vs, vr2p, vr2m, vra1, vra2, vrb1, vrb2, vkeep,
    kb, kry, ks, kr2p, kr2m, kra1, kra2, krb1, krb2, kkeep,
    lsem, ss, rs, known,
):
    dp, ctx = lax.axis_index("dp"), lax.axis_index("ctx")
    x, yl = dp // NYL, dp % NYL
    z, yh, c = ctx // (NYH * 2), (ctx // 2) % NYH, ctx % 2
    sib = 1 - c
    xp, xm, x2 = (x + 1) % NX, (x + 3) % NX, (x + 2) % NX

    def device(x_=None, yl_=None, z_=None, yh_=None, c_=None):
        x_, yl_ = x if x_ is None else x_, yl if yl_ is None else yl_
        z_, yh_, c_ = z if z_ is None else z_, yh if yh_ is None else yh_, c if c_ is None else c_
        return {"dp": x_ * NYL + yl_, "ctx": (z_ * NYH + yh_) * 2 + c_}

    to_sib = device(c_=sib)
    to_y = device(yl_=1 - yl)
    to_xp, to_xm = device(x_=xp), device(x_=xm)

    def remote(n, src, dst, dev):
        return pltpu.make_async_remote_copy(
            src_ref=src, dst_ref=dst, send_sem=ss.at[n], recv_sem=rs.at[n],
            device_id=dev, device_id_type=MESH,
        )

    sent = []

    def send(n, src, dst, dev):
        copy = remote(n, src, dst, dev)
        copy.start()
        sent.append(copy)

    def got(n, dst):
        remote(n, dst, dst, to_sib).wait_recv()

    barrier = pltpu.get_barrier_semaphore()

    row = yh * 2 + yl
    along_y = []
    for step in (1, 7):
        far = (row + step) % (2 * NYH)
        along_y.append(device(yl_=far % 2, yh_=far // 2))
    along_z = [device(z_=(z + step) % NZ) for step in (1, NZ - 1)]
    for dev in [to_sib, to_xp, to_xm] + along_y + along_z:
        pl.semaphore_signal(barrier, inc=1, device_id=dev, device_id_type=MESH)

    def tell(n):
        for dev in along_y + along_z:
            pl.semaphore_signal(known.at[n], inc=1, device_id=dev, device_id_type=MESH)

    def heard(n):
        pl.semaphore_wait(known.at[n], 4)

    local = []

    def fetch(src, dst):
        copy = pltpu.make_async_copy(src, dst, lsem.at[len(local)])
        copy.start()
        local.append(copy)
        return copy

    kr_in = fetch(kr_hbm, kr_v)
    lat_in = []
    for h in range(2):
        for t in range(4):
            lat_in.append(fetch(
                lat_hbm.at[pl.ds(h * HALF, HALF), pl.ds(t * 128, 128)],
                agb.at[0, 0, h, pl.ds(t * HALF, HALF)],
            ))
    q_in, kup_in = fetch(q_hbm, q_v), fetch(kup_hbm, kup_v)
    go_in, vup_in = fetch(go_hbm, go_v), fetch(vup_hbm, vup_v)
    qr_in, po_in = fetch(qr_hbm, qr_v), fetch(po_hbm, po_v)

    for copy in lat_in:
        copy.wait()
    pl.semaphore_wait(barrier, 7)

    far = (row + 1 + 6 * c) % (2 * NYH)
    to_yg = device(yl_=far % 2, yh_=far // 2)
    pieces = (pl.ds(0, CUT), pl.ds(CUT, BLK - CUT))
    x_id, y_id, sib_id = 0, 16, 32

    def block(k, j, p, core=c):
        return agb.at[k, j, core, pieces[p]]

    def gather_x(k, j, p, source):
        dst = block(k, j, p)
        send(x_id + 4 * k + 2 * j + p, source, dst, to_xp if (k, p) in ((1, 0), (1, 1), (3, 0)) else to_xm)

    def gather_y(k, p):
        send(y_id + 2 * k + p, block(k, 0, p), block(k, 1, p), to_yg)

    def gather_sib(k, j, p):
        send(sib_id + 4 * k + 2 * j + p, block(k, j, p), block(k, j, p), to_sib)

    def from_x(k, j, p):
        got(x_id + 4 * k + 2 * j + p, block(k, j, p))

    def from_y(k, p):
        got(y_id + 2 * k + p, block(k, 1, p))

    def from_sib(k, j):
        for p in range(2):
            got(sib_id + 4 * k + 2 * j + p, block(k, j, p, sib))

    gather_x(1, 0, 0, block(0, 0, 0))
    kr_in.wait()
    kr_own = kr_v[...].astype(F32).T
    krp = jnp.concatenate([kr_own[:HALF], kr_own[HALF:]], axis=1).astype(BF16)
    agb[0, 0, 0, pl.ds(4 * HALF, 48)] = krp[:48]
    agb[0, 0, 1, pl.ds(4 * HALF, 48)] = krp[48:]
    gather_x(2, 0, 1, block(0, 0, 1))
    gather_y(0, 0)
    gather_x(1, 0, 1, block(0, 0, 1))
    gather_x(2, 0, 0, block(0, 0, 0))
    gather_y(0, 1)
    tell(0)

    q_in.wait()
    go_in.wait()
    kup_in.wait()
    vup_in.wait()
    qr_in.wait()
    po_in.wait()
    blank = jnp.zeros((TOK, DN), F32)

    def block_diagonal(ref):
        both = ref[...].astype(F32)
        top = jnp.concatenate([both[:, 0, :], blank], axis=1)
        low = jnp.concatenate([blank, both[:, 1, :]], axis=1)
        return jnp.concatenate([top, low], axis=0)

    qx = block_diagonal(q_v)
    gox = block_diagonal(go_v)
    qtx[...] = qx.T.astype(BF16)
    gotx[...] = gox.T.astype(BF16)
    kup2 = kup_v[...].reshape(2 * DN, DL)
    vup2 = vup_v[...].reshape(2 * DN, DL)
    absorbed = dot(qx.astype(BF16), kup2)
    grad_lat = dot(gox.astype(BF16), vup2)
    qr_rows = jnp.concatenate([qr_v[0].astype(F32).T, qr_v[1].astype(F32).T], axis=0)
    qr2 = jnp.concatenate([qr_rows, qr_rows], axis=1)
    ax[:, :DL] = absorbed.astype(BF16)
    ax[:, DL:] = qr2.astype(BF16)
    axt[:DL, :] = absorbed.astype(BF16).T
    axt[DL:, :] = qr2.astype(BF16).T
    gx[...] = grad_lat.astype(BF16)
    gxt[...] = grad_lat.astype(BF16).T

    po_row = jnp.broadcast_to(po_v[...].astype(F32), (8, PAIRS))
    slot_t = third(iota((PAIRS, ROWS), 1) % HALF)
    pick = jnp.where(iota((PAIRS, ROWS), 0) == dp * PER_DEV + slot_t, 1.0, 0.0).astype(BF16)
    pid_row = dot(po_row.astype(BF16), pick)
    within = iota((8, ROWS), 1)
    in_half = within % HALF
    late = (within % TOK) >= HALF
    group = jnp.where(late, 2.0 * PAIRS - 1.0 - pid_row, pid_row)
    prow[...] = group * 3.0 + (in_half - 3 * third(in_half)).astype(F32)

    po_col = jnp.broadcast_to(po_row[:1], (128, PAIRS)).T.astype(BF16)
    half_of = iota((TOK, PER_DEV), 0) % HALF
    expand = jnp.where(third(half_of) == iota((TOK, PER_DEV), 1), 1.0, 0.0).astype(BF16)
    row_no = iota((TOK, 128), 0)
    row_half = row_no % HALF
    for b in range(NX * NYL):
        pid = dot(expand, po_col[b * PER_DEV:(b + 1) * PER_DEV])
        grp = jnp.where(row_no >= HALF, 2.0 * PAIRS - 1.0 - pid, pid)
        pcol[b] = grp * 3.0 + (row_half - 3 * third(row_half)).astype(F32)

    scale = 1.0 / math.sqrt(DN + DR)
    low_lane = iota((HALF, 128), 1) < DR

    def attend(k, j):
        b = 2 * k + j
        key_dev = ((x + REL[k]) % NX) * NYL + (yl + j) % 2
        halves = []
        krp = jnp.concatenate(
            [agb[k, j, 0, pl.ds(4 * HALF, 48)], agb[k, j, 1, pl.ds(4 * HALF, 48)]], axis=0
        )
        zero = jnp.zeros((HALF, 128), BF16)
        for h in range(2):
            tiles = [agb[k, j, h, pl.ds(t * HALF, HALF)] for t in range(4)]
            tiles.append(jnp.where(low_lane, krp, zero) if h == 0 else jnp.where(low_lane, zero, krp))
            halves.append(jnp.concatenate(tiles, axis=1))
        lx = jnp.concatenate(halves, axis=0)
        lx_s[pl.ds(b * TOK, TOK), :] = lx
        s = dot(lx, axt[...]) * scale
        gw[b] = dot(lx[:, :DL], gxt[...])
        key_pos = pcol[key_dev]
        allowed = jnp.concatenate([key_pos] * 3, axis=1) <= prow[0:1]
        s = jnp.where(allowed, s, NEG)
        m = jnp.max(s, axis=0, keepdims=True)
        p = jnp.where(allowed, jnp.exp(s - m), 0.0)
        st[b] = p
        mb[b] = jnp.broadcast_to(m, (8, ROWS))
        lb[b] = jnp.broadcast_to(jnp.sum(p, axis=0, keepdims=True), (8, ROWS))

    def turn(k):
        for t in range(EXT // 128):
            lxt[pl.ds(t * 128, 128), pl.ds(k * 2 * TOK, 2 * TOK)] = (
                lx_s[pl.ds(k * 2 * TOK, 2 * TOK), pl.ds(t * 128, 128)].T
            )
        top = jnp.maximum(mb[2 * k], mb[2 * k + 1])
        both = [st[b] * jnp.exp(mb[b] - top)[:1] for b in (2 * k, 2 * k + 1)]
        lacc[k] = dot(
            lxt[pl.ds(0, DL), pl.ds(k * 2 * TOK, 2 * TOK)], jnp.concatenate(both, axis=0).astype(BF16)
        )
        mtop[k] = top

    def on_from_x(k, p):
        from_x(k, 0, p)
        if (k, p) in ((1, 0), (2, 1)):
            gather_x(3, 0, p, block(k, 0, p))
        gather_y(k, p)
        gather_sib(k, 0, p)

    def on_from_y(k, p):
        from_y(k, p)
        if (k, p) in ((1, 0), (2, 1)):
            gather_x(3, 1, p, block(k, 1, p))
        gather_sib(k, 1, p)

    def on_far(j):
        for p in range(2):
            from_x(3, j, p)
            gather_sib(3, j, p)

    heard(0)
    tell(1)
    on_from_x(1, 0)
    on_from_x(2, 1)
    on_from_y(0, 0)
    on_from_y(0, 1)
    heard(1)
    tell(2)
    attend(0, 0)
    on_from_x(1, 1)
    on_from_x(2, 0)
    heard(2)
    tell(3)
    from_sib(0, 1)
    attend(0, 1)
    on_from_y(1, 0)
    on_from_y(2, 1)
    turn(0)
    on_far(0)
    from_sib(1, 0)
    attend(1, 0)
    on_from_y(1, 1)
    on_from_y(2, 0)
    from_sib(2, 0)
    attend(2, 0)
    from_sib(3, 0)
    attend(3, 0)
    on_far(1)
    from_sib(1, 1)
    attend(1, 1)
    turn(1)
    from_sib(2, 1)
    attend(2, 1)
    turn(2)
    from_sib(3, 1)
    attend(3, 1)
    turn(3)
    heard(3)

    top = jnp.maximum(jnp.maximum(mtop[0], mtop[1]), jnp.maximum(mtop[2], mtop[3]))
    total = jnp.zeros_like(top)
    for b in range(8):
        share = jnp.exp(mb[b] - top)
        mb[b] = share
        total = total + lb[b] * share
    inv = 1.0 / total
    parts = [(jnp.exp(mtop[k] - top) * inv)[:1] for k in range(NX)]
    dots = jnp.zeros((1, ROWS), F32)
    for t in range(4):
        rows = pl.ds(t * 128, 128)
        part = lacc[0, rows] * parts[0]
        for k in range(1, NX):
            part = part + lacc[k, rows] * parts[k]
        dots = dots + jnp.sum(gxt[rows, :].astype(F32) * part, axis=0, keepdims=True)
        lot[rows, :] = part.astype(BF16)

    def ring_first(n, buf, halves, dst):
        lo, hi = halves
        send(n, buf.at[x2].at[lo], dst[0], to_xp)
        send(n + 1, buf.at[x2].at[hi], dst[1], to_xm)
        send(n + 2, buf.at[xp].at[hi], dst[2], to_xp)
        send(n + 3, buf.at[xm].at[lo], dst[4], to_xm)

    def ring_second(n, buf, halves, dst, keep):
        lo, hi = halves
        got(n, dst[0])
        keep[0] = (buf[xp, lo].astype(F32) + dst[0][...].astype(F32)).astype(BF16)
        send(n + 4, keep.at[0], dst[3], to_xp)
        got(n + 1, dst[1])
        keep[1] = (buf[xm, hi].astype(F32) + dst[1][...].astype(F32)).astype(BF16)
        send(n + 5, keep.at[1], dst[5], to_xm)

    def ring_last(n, buf, halves, dst, fin):
        got(n + 2, dst[2])
        got(n + 3, dst[4])
        got(n + 4, dst[3])
        got(n + 5, dst[5])
        for half, one, two in zip(halves, dst[3:1:-1], dst[4:6]):
            fin[yl, x, half] = (
                buf[x, half].astype(F32) + one[...].astype(F32) + two[...].astype(F32)
            ).astype(BF16)

    halves = (pl.ds(0, 16), pl.ds(16, 16))
    v_dst = (vr2p, vr2m, vra1, vra2, vrb1, vrb2)
    k_dst = (kr2p, kr2m, kra1, kra2, krb1, krb2)

    def to_pair(n, part, buf, dst):
        for a in range(8):
            for h in range(2):
                buf[a // 4, a % 4, pl.ds(16 * h, 16), :] = part[DN * h + 16 * a:DN * h + 16 * a + 16]
        send(n, buf.at[1 - yl], dst, to_y)

    def from_pair(n, buf, other, total):
        got(n, other)
        total[...] = (buf[yl].astype(F32) + other[...].astype(F32)).astype(BF16)

    def along_x(n, fin, side):
        for d in range(1, NX):
            send(n + d, fin.at[side, x], fin.at[side, x], device(x_=(x + d) % NX))

    def spread(n, fin):
        send(n, fin.at[yl, x], fin.at[yl, x], to_y)
        along_x(n, fin, yl)

    def relay(n, fin):
        got(n, fin.at[1 - yl, x])
        along_x(n + 3, fin, 1 - yl)

    def spread_got(n, fin):
        for d in range(1, NX):
            got(n + d, fin.at[yl, (x + NX - d) % NX])
            got(n + 3 + d, fin.at[1 - yl, (x + NX - d) % NX])

    for b in range(8):
        w = st[b] * (mb[b] * inv)[:1]
        wt[pl.ds(b * TOK, TOK), :] = w.astype(BF16)
        gst[pl.ds(b * TOK, TOK), :] = (w * (gw[b] - dots) * scale).astype(BF16)

    def terms(k, j):
        start = pl.multiple_of((2 * k + j) * TOK, TOK)
        g = gst[pl.ds(start, TOK), :]
        full = dot(g, ax[...])
        lat = full[:, :DL] + dot(wt[pl.ds(start, TOK), :], gx[...])
        rope = jnp.where(low_lane, full[:HALF, DL:], full[HALF:, DL:])
        return lat, rope

    def put_terms(lat, rope, dst):
        for i in range(0, NZ, 2):
            dst[pl.ds(72 * i, 144), :] = jnp.concatenate(
                [lat[24 * r:24 * r + 24, 128 * t:128 * t + 128] for r in (i, i + 1) for t in range(3)], axis=0
            ).astype(dst.dtype)
        dst[pl.ds(72 * NZ, 96), :] = rope.astype(dst.dtype)
        dst[pl.ds(CHA, TOK), :] = lat[:, 384:].astype(dst.dtype)

    def both_cores(k, dst):
        got(48 + k, crecv.at[k])
        rows = pl.ds(0, CHA)
        dst[...] = (cown[k, rows] + crecv[k, rows].astype(F32)).astype(dst.dtype)

    low_rows, high_rows = pl.ds(0, CHH), pl.ds(CHH, CHH)

    def chunk(k):
        put_terms(*terms(k, sib), csend.at[k])
        send(48 + k, csend.at[k], crecv.at[k], to_sib)
        put_terms(*terms(k, c), cown.at[k])

    chunk(3)
    to_pair(73, dot(gotx[...], lot[...], 1, 1).astype(BF16), vb, vry)
    chunk(2)
    both_cores(3, xs.at[3])
    send(52, xs.at[3, low_rows], r2p, to_xp)
    send(53, xs.at[3, high_rows], r2m, to_xm)
    chunk(1)
    both_cores(2, xs.at[2])
    send(54, xs.at[2, high_rows], ra1, to_xp)
    chunk(0)
    both_cores(1, xs.at[1])
    send(55, xs.at[1, low_rows], rb1, to_xm)

    gat[...] = dot(lxt[:DL, :], gst[...]).astype(BF16)
    to_pair(80, dot(qtx[...], gat[...], 1, 1).astype(BF16), kb, kry)

    got(52, r2p)
    xs[0, low_rows] = (xs[2, low_rows].astype(F32) + r2p[...].astype(F32)).astype(BF16)
    send(56, xs.at[0, low_rows], ra2, to_xp)
    got(53, r2m)
    xs[0, high_rows] = (xs[1, high_rows].astype(F32) + r2m[...].astype(F32)).astype(BF16)
    send(57, xs.at[0, high_rows], rb2, to_xm)
    both_cores(0, xsum)
    rows = pl.ds(CHA, TOK)
    parts = [cown[k, rows] + crecv[k, rows].astype(F32) for k in range(NX)]
    for i in range(NZ):
        bs[i] = jnp.concatenate([part[24 * i:24 * i + 24] for part in parts], axis=0).astype(BF16)
    for d in (4, 3, 5, 2, 6, 1, 7):
        far = (z + d) % NZ
        send(100 + d, bs.at[far], brecv.at[d], device(z_=far))

    from_pair(73, vb, vry, vs)
    ring_first(74, vs, halves, v_dst)

    rope2 = dot(lxt[DL:, :], gst[...])
    rope_rows = (rope2[:DR] + rope2[DR:]).astype(BF16)
    gr_ref[0] = rope_rows[:, :TOK]
    gr_ref[1] = rope_rows[:, TOK:]
    grad_nope = dot(gat[...], kup2, 0, 1)
    gn_ref[0] = grad_nope[:TOK, :DN].astype(BF16)
    gn_ref[1] = grad_nope[TOK:, DN:].astype(BF16)

    from_pair(80, kb, kry, ks)
    ring_first(81, ks, halves, k_dst)

    got(54, ra1)
    got(55, rb1)
    got(56, ra2)
    got(57, rb2)
    xsum[low_rows] = xsum[low_rows] + ra2[...].astype(F32) + rb1[...].astype(F32)
    xsum[high_rows] = xsum[high_rows] + ra1[...].astype(F32) + rb2[...].astype(F32)
    pad = jnp.zeros((8, 128), F32)
    for i in range(NZ):
        zs[i] = jnp.concatenate(
            [xsum[pl.ds(72 * i, 72)], xsum[pl.ds(72 * NZ + 24 * (i % 4), 24)]], axis=0
        ).astype(BF16)
    for d in (4, 3, 5, 2, 6, 1, 7):
        far = (z + d) % NZ
        send(57 + d, zs.at[far], zrecv.at[d], device(z_=far))

    ring_second(74, vs, halves, v_dst, vkeep)
    ring_second(81, ks, halves, k_dst, kkeep)

    fourth = bs[z].astype(F32)
    for d in (1, 7, 2, 6, 3, 5, 4):
        got(100 + d, brecv.at[d])
        fourth = fourth + brecv[d].astype(F32)
    for k, there, dev in ((3, 3, device(x_=x2)), (2, 1, to_xp), (1, 2, to_xm)):
        bx[k] = jnp.concatenate([fourth[24 * k:24 * k + 24], pad], axis=0).astype(BF16)
        send(107 + there, bx.at[k], bxr.at[there], dev)

    ring_last(74, vs, halves, v_dst, vfin)
    spread(87, vfin)
    ring_last(81, ks, halves, k_dst, kfin)
    spread(94, kfin)
    relay(87, vfin)
    relay(94, kfin)

    out_row, in_row = iota((128, 128), 0), iota((128, 128), 1)
    owner, place = out_row // 16, out_row % 16
    source = 24 * third(place) + 3 * owner + (place - 3 * third(place))
    order = jnp.where((source == in_row) & (place < 15), 1.0, 0.0).astype(BF16)
    own = fourth[:24]
    for k in range(1, NX):
        got(107 + k, bxr.at[k])
        own = own + bxr[k].astype(F32)[:24]
    zsum = zs[z].astype(F32)
    for d in (1, 7, 2, 6, 3, 5, 4):
        got(57 + d, zrecv.at[d])
        zsum = zsum + zrecv[d].astype(F32)
    zsum = jnp.concatenate([zsum[:72], own, zsum[72:], pad], axis=0)
    sorted_rows = dot(order, zsum.astype(BF16)).astype(BF16)
    for i in range(8):
        ys[i] = sorted_rows[16 * i:16 * i + 16]

    def to_owner(d, e):
        far = (yh + d) % NYH
        return pltpu.make_async_remote_copy(
            src_ref=ys.at[far * 2 + e], dst_ref=yrecv.at[d, c],
            send_sem=ss.at[65 + 2 * d + e], recv_sem=rs.at[65 + 2 * d + c],
            device_id=device(yh_=far, yl_=(yl + c) % 2, c_=e), device_id_type=MESH,
        )

    for d in range(NYH):
        for e in range(2):
            if d == 0 and e == 0:
                @pl.when(c == 0)
                def _():
                    yrecv[0, 0] = ys[yh * 2]

                @pl.when(c == 1)
                def _():
                    to_owner(0, 0).start()
            else:
                to_owner(d, e).start()

    spread_got(87, vfin)
    spread_got(94, kfin)

    total = jnp.zeros((16, 128), F32)
    for d in range(NYH):
        for e in range(2):
            if d == 0 and e == 0:
                @pl.when(c == 1)
                def _():
                    got(65, yrecv.at[0, 0])
            else:
                got(65 + 2 * d + e, yrecv.at[d, e])
    for d in range(NYH):
        for e in range(2):
            total = total + yrecv[d, e].astype(F32)
    ol_ref[...] = jnp.concatenate([total[3 * t:3 * t + 3] for t in range(4)], axis=1).astype(BF16)
    rope = total[12:15]
    or_ref[...] = jnp.where(z >= NZ // 2, rope[:, DR:], rope[:, :DR]).astype(BF16)

    for copy in sent:
        copy.wait_send()
    for d in range(NYH):
        for e in range(2):
            if d == 0 and e == 0:
                @pl.when(c == 1)
                def _():
                    to_owner(0, 0).wait_send()
            else:
                to_owner(d, e).wait_send()


def finish(gn_in, gr_in, ol_in, or_in, kfin, vfin, gn_ref, gr_ref, ol_ref, or_ref, gk_ref, gv_ref):
    gr_ref[...] = gr_in[...]
    ol_ref[...] = ol_in[...]
    or_ref[...] = or_in[...]
    for a in range(8):
        for h in range(2):
            gk_ref[h, pl.ds(16 * a, 16), :] = kfin[a // 4, a % 4, pl.ds(16 * h, 16), :].astype(F32)
            gv_ref[h, pl.ds(16 * a, 16), :] = vfin[a // 4, a % 4, pl.ds(16 * h, 16), :].astype(F32)
    gn_ref[...] = jnp.stack([gn_in[0].astype(F32), gn_in[1].astype(F32)], axis=1).astype(BF16)


def on_device(query_nope, query_rope, grad_output, latents, key_rope, key_up, value_up, pair_order):
    scratch = [
        ((TOK, 2, DN), BF16), ((2, DR, TOK), BF16), ((TOK, 2, DN), BF16), ((DR, TOK), BF16),
        ((2, DN, DL), BF16), ((2, DN, DL), BF16), ((1, PAIRS), jnp.int32),
        ((4, 2, 2, BLK, 128), BF16), ((NX * 2 * TOK, EXT), BF16), ((EXT, NX * 2 * TOK), BF16),
        ((ROWS, EXT), BF16), ((EXT, ROWS), BF16), ((ROWS, DL), BF16), ((DL, ROWS), BF16),
        ((2 * DN, ROWS), BF16), ((2 * DN, ROWS), BF16),
        ((8, TOK, 128), F32), ((8, ROWS), F32), ((8, TOK, ROWS), F32), ((8, TOK, ROWS), F32),
        ((8, 8, ROWS), F32), ((8, 8, ROWS), F32), ((NX, DL, ROWS), F32), ((NX, 8, ROWS), F32),
        ((8 * TOK, ROWS), BF16), ((8 * TOK, ROWS), BF16), ((DL, ROWS), BF16), ((DL, ROWS), BF16),
        ((4, CH, 128), BF16), ((4, CH, 128), BF16), ((4, CH, 128), F32), ((4, CHA, 128), BF16),
        ((CHA, 128), F32),
        ((CHH, 128), BF16), ((CHH, 128), BF16), ((CHH, 128), BF16), ((CHH, 128), BF16),
        ((CHH, 128), BF16), ((CHH, 128), BF16),
        ((8, 96, 128), BF16), ((8, 96, 128), BF16), ((8, 96, 128), BF16), ((8, 96, 128), BF16),
        ((4, 32, 128), BF16), ((4, 32, 128), BF16), ((8, 16, 128), BF16), ((4, 2, 16, 128), BF16),
    ] + (
        [((2, 4, 32, DL), BF16)] + [((4, 32, DL), BF16)] * 2 + [((16, DL), BF16)] * 6 + [((2, 16, DL), BF16)]
    ) * 2
    outs = (
        ((2, TOK, DN), BF16), ((2, DR, TOK), BF16), ((3, DL), BF16), ((3, DR), BF16),
        ((2, 4, 32, DL), BF16), ((2, 4, 32, DL), BF16),
    )
    any_spec = pl.BlockSpec(memory_space=pl.ANY)
    vmem_spec = pl.BlockSpec(memory_space=pltpu.VMEM)
    raw = pl.pallas_call(
        kernel,
        out_shape=[pltpu.VMEM(s, t) for s, t in outs],
        in_specs=[any_spec] * 8,
        out_specs=[vmem_spec] * 6,
        scratch_shapes=[pltpu.VMEM(s, t) for s, t in scratch] + [
            pltpu.SemaphoreType.DMA((15,)),
            pltpu.SemaphoreType.DMA((N_SEM,)),
            pltpu.SemaphoreType.DMA((N_SEM,)),
            pltpu.SemaphoreType.REGULAR((4,)),
        ],
        compiler_params=pltpu.CompilerParams(
            collective_id=0, has_side_effects=True, vmem_limit_bytes=60 * 1024 * 1024
        ),
        name="mla_backward",
    )(
        query_nope,
        jnp.transpose(query_rope, (1, 2, 0)),
        grad_output,
        latents,
        key_rope.T,
        key_up,
        value_up,
        pair_order.reshape(1, -1),
    )
    results = (
        ((TOK, 2, DN), BF16), ((2, DR, TOK), BF16), ((3, DL), BF16), ((3, DR), BF16),
        ((2, DN, DL), F32), ((2, DN, DL), F32),
    )
    grad_nope, grad_rope, own_lat, own_rope, grad_kup, grad_vup = pl.pallas_call(
        finish,
        out_shape=[jax.ShapeDtypeStruct(s, t) for s, t in results],
        in_specs=[vmem_spec] * 6,
        out_specs=[vmem_spec] * 6,
        name="finish",
    )(*[pltpu.with_memory_space_constraint(r, pltpu.VMEM) for r in raw])
    return grad_nope, jnp.transpose(grad_rope, (2, 0, 1)), own_lat, own_rope, grad_kup, grad_vup


def solution(mesh):
    placed = (
        P("dp", "ctx", None),
        P("dp", "ctx", None),
        P("dp", "ctx", None),
        P("dp", None),
        P("dp", None),
        P("ctx", None, None),
        P("ctx", None, None),
        P(),
    )
    return jax.shard_map(
        on_device,
        mesh=mesh,
        in_specs=placed,
        out_specs=(
            P("dp", "ctx", None),
            P("dp", "ctx", None),
            P(("dp", "ctx"), None),
            P(("dp", "ctx"), None),
            P("ctx", None, None),
            P("ctx", None, None),
        ),
        check_vma=False,
    )
```

```python
import functools
import math

import jax
import jax.numpy as jnp
from jax import lax
from jax.experimental import pallas as pl
from jax.experimental.pallas import tpu as pltpu
from jax.sharding import PartitionSpec as P

MESH = pl.DeviceIdType.MESH
F32 = jnp.float32
BF16 = jnp.bfloat16
NEG = -1e30

NX, NYL, NZ, NYH = 4, 2, 8, 4
TOK = 192
HALF = TOK // 2
DL, DR, DN = 512, 64, 128
ROWS = 2 * TOK
EXT = DL + 2 * DR
PAIRS = 256
PER_DEV = 32
BLK = 4 * HALF + 48
CUT = 224
CHA = NZ * 72 + 96
CHH = CHA // 2
CH = CHA + TOK

REL = (0, 3, 1, 2)

N_SEM = 111


def dot(a, b, ca=1, cb=0):
    return lax.dot_general(a, b, (((ca,), (cb,)), ((), ())), preferred_element_type=F32)


def iota(shape, axis):
    return lax.broadcasted_iota(jnp.int32, shape, axis)


def third(v):
    return (v * 43691) >> 17


def kernel(
    q_hbm, qr_hbm, go_hbm, lat_hbm, kr_hbm, kup_hbm, vup_hbm, po_hbm,
    gn_ref, gr_ref, ol_ref, or_ref, kfin, vfin,
    q_v, qr_v, go_v, kr_v, kup_v, vup_v, po_v,
    agb, lx_s, lxt, ax, axt, gx, gxt, qtx, gotx,
    pcol, prow, st, gw, mb, lb, lacc, mtop, wt, gst, lot, gat,
    csend, crecv, cown, xs, xsum, r2p, r2m, ra1, ra2, rb1, rb2,
    zs, zrecv, bs, brecv, bx, bxr, ys, yrecv,
    vb, vry, vs, vr2p, vr2m, vra1, vra2, vrb1, vrb2, vkeep,
    kb, kry, ks, kr2p, kr2m, kra1, kra2, krb1, krb2, kkeep,
    lsem, ss, rs, known,
):
    dp, ctx = lax.axis_index("dp"), lax.axis_index("ctx")
    x, yl = dp // NYL, dp % NYL
    z, yh, c = ctx // (NYH * 2), (ctx // 2) % NYH, ctx % 2
    sib = 1 - c
    xp, xm, x2 = (x + 1) % NX, (x + 3) % NX, (x + 2) % NX

    def device(x_=None, yl_=None, z_=None, yh_=None, c_=None):
        x_, yl_ = x if x_ is None else x_, yl if yl_ is None else yl_
        z_, yh_, c_ = z if z_ is None else z_, yh if yh_ is None else yh_, c if c_ is None else c_
        return {"dp": x_ * NYL + yl_, "ctx": (z_ * NYH + yh_) * 2 + c_}

    to_sib = device(c_=sib)
    to_y = device(yl_=1 - yl)
    to_xp, to_xm = device(x_=xp), device(x_=xm)

    def remote(n, src, dst, dev):
        return pltpu.make_async_remote_copy(
            src_ref=src, dst_ref=dst, send_sem=ss.at[n], recv_sem=rs.at[n],
            device_id=dev, device_id_type=MESH,
        )

    sent = []

    def send(n, src, dst, dev):
        copy = remote(n, src, dst, dev)
        copy.start()
        sent.append(copy)

    def got(n, dst):
        remote(n, dst, dst, to_sib).wait_recv()

    barrier = pltpu.get_barrier_semaphore()

    row = yh * 2 + yl
    along_y = []
    for step in (1, 7):
        far = (row + step) % (2 * NYH)
        along_y.append(device(yl_=far % 2, yh_=far // 2))
    along_z = [device(z_=(z + step) % NZ) for step in (1, NZ - 1)]
    for dev in [to_sib, to_xp, to_xm] + along_y + along_z:
        pl.semaphore_signal(barrier, inc=1, device_id=dev, device_id_type=MESH)

    def tell(n):
        for dev in along_y + along_z:
            pl.semaphore_signal(known.at[n], inc=1, device_id=dev, device_id_type=MESH)

    def heard(n):
        pl.semaphore_wait(known.at[n], 4)

    local = []

    def fetch(src, dst):
        copy = pltpu.make_async_copy(src, dst, lsem.at[len(local)])
        copy.start()
        local.append(copy)
        return copy

    lat_in = []
    for h in range(2):
        for t in range(4):
            lat_in.append(fetch(
                lat_hbm.at[pl.ds(h * HALF, HALF), pl.ds(t * 128, 128)],
                agb.at[0, 0, h, pl.ds(t * HALF, HALF)],
            ))
    kr_in = fetch(kr_hbm, kr_v)
    q_in, kup_in = fetch(q_hbm, q_v), fetch(kup_hbm, kup_v)
    go_in, vup_in = fetch(go_hbm, go_v), fetch(vup_hbm, vup_v)
    qr_in, po_in = fetch(qr_hbm, qr_v), fetch(po_hbm, po_v)

    for copy in lat_in:
        copy.wait()
    pl.semaphore_wait(barrier, 7)

    far = (row + 1 + 6 * c) % (2 * NYH)
    to_yg = device(yl_=far % 2, yh_=far // 2)
    pieces = (pl.ds(0, CUT), pl.ds(CUT, BLK - CUT))
    x_id, y_id, sib_id = 0, 16, 32

    def block(k, j, p, core=c):
        return agb.at[k, j, core, pieces[p]]

    def gather_x(k, j, p, source):
        dst = block(k, j, p)
        send(x_id + 4 * k + 2 * j + p, source, dst, to_xp if (k, p) in ((1, 0), (1, 1), (3, 0)) else to_xm)

    def gather_y(k, p):
        send(y_id + 2 * k + p, block(k, 0, p), block(k, 1, p), to_yg)

    def gather_sib(k, j, p):
        send(sib_id + 4 * k + 2 * j + p, block(k, j, p), block(k, j, p), to_sib)

    def from_x(k, j, p):
        got(x_id + 4 * k + 2 * j + p, block(k, j, p))

    def from_y(k, p):
        got(y_id + 2 * k + p, block(k, 1, p))

    def from_sib(k, j):
        for p in range(2):
            got(sib_id + 4 * k + 2 * j + p, block(k, j, p, sib))

    gather_x(1, 0, 0, block(0, 0, 0))
    kr_in.wait()
    kr_own = kr_v[...].astype(F32).T
    krp = jnp.concatenate([kr_own[:HALF], kr_own[HALF:]], axis=1).astype(BF16)
    agb[0, 0, 0, pl.ds(4 * HALF, 48)] = krp[:48]
    agb[0, 0, 1, pl.ds(4 * HALF, 48)] = krp[48:]
    gather_x(2, 0, 1, block(0, 0, 1))
    gather_y(0, 0)
    gather_x(1, 0, 1, block(0, 0, 1))
    gather_x(2, 0, 0, block(0, 0, 0))
    gather_y(0, 1)
    tell(0)

    q_in.wait()
    go_in.wait()
    kup_in.wait()
    vup_in.wait()
    qr_in.wait()
    po_in.wait()
    blank = jnp.zeros((TOK, DN), F32)

    def block_diagonal(ref):
        both = ref[...].astype(F32)
        top = jnp.concatenate([both[:, 0, :], blank], axis=1)
        low = jnp.concatenate([blank, both[:, 1, :]], axis=1)
        return jnp.concatenate([top, low], axis=0)

    qx = block_diagonal(q_v)
    gox = block_diagonal(go_v)
    qtx[...] = qx.T.astype(BF16)
    gotx[...] = gox.T.astype(BF16)
    kup2 = kup_v[...].reshape(2 * DN, DL)
    vup2 = vup_v[...].reshape(2 * DN, DL)
    absorbed = dot(qx.astype(BF16), kup2)
    grad_lat = dot(gox.astype(BF16), vup2)
    qr_rows = jnp.concatenate([qr_v[0].astype(F32).T, qr_v[1].astype(F32).T], axis=0)
    qr2 = jnp.concatenate([qr_rows, qr_rows], axis=1)
    ax[:, :DL] = absorbed.astype(BF16)
    ax[:, DL:] = qr2.astype(BF16)
    axt[:DL, :] = absorbed.astype(BF16).T
    axt[DL:, :] = qr2.astype(BF16).T
    gx[...] = grad_lat.astype(BF16)
    gxt[...] = grad_lat.astype(BF16).T

    po_row = jnp.broadcast_to(po_v[...].astype(F32), (8, PAIRS))
    slot_t = third(iota((PAIRS, ROWS), 1) % HALF)
    pick = jnp.where(iota((PAIRS, ROWS), 0) == dp * PER_DEV + slot_t, 1.0, 0.0).astype(BF16)
    pid_row = dot(po_row.astype(BF16), pick)
    within = iota((8, ROWS), 1)
    in_half = within % HALF
    late = (within % TOK) >= HALF
    group = jnp.where(late, 2.0 * PAIRS - 1.0 - pid_row, pid_row)
    prow[...] = group * 3.0 + (in_half - 3 * third(in_half)).astype(F32)

    po_col = jnp.broadcast_to(po_row[:1], (128, PAIRS)).T.astype(BF16)
    half_of = iota((TOK, PER_DEV), 0) % HALF
    expand = jnp.where(third(half_of) == iota((TOK, PER_DEV), 1), 1.0, 0.0).astype(BF16)
    row_no = iota((TOK, 128), 0)
    row_half = row_no % HALF
    for b in range(NX * NYL):
        pid = dot(expand, po_col[b * PER_DEV:(b + 1) * PER_DEV])
        grp = jnp.where(row_no >= HALF, 2.0 * PAIRS - 1.0 - pid, pid)
        pcol[b] = grp * 3.0 + (row_half - 3 * third(row_half)).astype(F32)

    scale = 1.0 / math.sqrt(DN + DR)
    low_lane = iota((HALF, 128), 1) < DR

    def attend(k, j):
        b = 2 * k + j
        key_dev = ((x + REL[k]) % NX) * NYL + (yl + j) % 2
        halves = []
        krp = jnp.concatenate(
            [agb[k, j, 0, pl.ds(4 * HALF, 48)], agb[k, j, 1, pl.ds(4 * HALF, 48)]], axis=0
        )
        zero = jnp.zeros((HALF, 128), BF16)
        for h in range(2):
            tiles = [agb[k, j, h, pl.ds(t * HALF, HALF)] for t in range(4)]
            tiles.append(jnp.where(low_lane, krp, zero) if h == 0 else jnp.where(low_lane, zero, krp))
            halves.append(jnp.concatenate(tiles, axis=1))
        lx = jnp.concatenate(halves, axis=0)
        lx_s[pl.ds(b * TOK, TOK), :] = lx
        s = dot(lx, axt[...]) * scale
        gw[b] = dot(lx[:, :DL], gxt[...])
        key_pos = pcol[key_dev]
        allowed = jnp.concatenate([key_pos] * 3, axis=1) <= prow[0:1]
        s = jnp.where(allowed, s, NEG)
        m = jnp.max(s, axis=0, keepdims=True)
        p = jnp.where(allowed, jnp.exp(s - m), 0.0)
        st[b] = p
        mb[b] = jnp.broadcast_to(m, (8, ROWS))
        lb[b] = jnp.broadcast_to(jnp.sum(p, axis=0, keepdims=True), (8, ROWS))

    def turn(k):
        for t in range(EXT // 128):
            lxt[pl.ds(t * 128, 128), pl.ds(k * 2 * TOK, 2 * TOK)] = (
                lx_s[pl.ds(k * 2 * TOK, 2 * TOK), pl.ds(t * 128, 128)].T
            )
        top = jnp.maximum(mb[2 * k], mb[2 * k + 1])
        both = [st[b] * jnp.exp(mb[b] - top)[:1] for b in (2 * k, 2 * k + 1)]
        lacc[k] = dot(
            lxt[pl.ds(0, DL), pl.ds(k * 2 * TOK, 2 * TOK)], jnp.concatenate(both, axis=0).astype(BF16)
        )
        mtop[k] = top

    def on_from_x(k, p):
        from_x(k, 0, p)
        if (k, p) in ((1, 0), (2, 1)):
            gather_x(3, 0, p, block(k, 0, p))
        gather_y(k, p)
        gather_sib(k, 0, p)

    def on_from_y(k, p):
        from_y(k, p)
        if (k, p) in ((1, 0), (2, 1)):
            gather_x(3, 1, p, block(k, 1, p))
        gather_sib(k, 1, p)

    def on_far(j, p):
        from_x(3, j, p)
        gather_sib(3, j, p)

    heard(0)
    tell(1)
    on_from_x(1, 0)
    on_from_x(2, 1)
    on_from_y(0, 0)
    on_from_y(0, 1)
    heard(1)
    tell(2)
    attend(0, 0)
    on_from_x(1, 1)
    on_from_x(2, 0)
    heard(2)
    tell(3)
    from_sib(0, 1)
    attend(0, 1)
    on_from_y(1, 0)
    on_from_y(2, 1)
    turn(0)
    on_far(0, 0)
    on_far(0, 1)
    from_sib(1, 0)
    attend(1, 0)
    on_from_y(1, 1)
    on_from_y(2, 0)
    from_sib(2, 0)
    attend(2, 0)
    from_sib(3, 0)
    attend(3, 0)
    on_far(1, 0)
    from_sib(1, 1)
    attend(1, 1)
    on_far(1, 1)
    turn(1)
    from_sib(2, 1)
    attend(2, 1)
    turn(2)
    from_sib(3, 1)
    attend(3, 1)
    turn(3)
    heard(3)

    top = jnp.maximum(jnp.maximum(mtop[0], mtop[1]), jnp.maximum(mtop[2], mtop[3]))
    total = jnp.zeros_like(top)
    for b in range(8):
        share = jnp.exp(mb[b] - top)
        mb[b] = share
        total = total + lb[b] * share
    inv = 1.0 / total
    parts = [(jnp.exp(mtop[k] - top) * inv)[:1] for k in range(NX)]
    dots = jnp.zeros((1, ROWS), F32)
    for t in range(4):
        rows = pl.ds(t * 128, 128)
        part = lacc[0, rows] * parts[0]
        for k in range(1, NX):
            part = part + lacc[k, rows] * parts[k]
        dots = dots + jnp.sum(gxt[rows, :].astype(F32) * part, axis=0, keepdims=True)
        lot[rows, :] = part.astype(BF16)

    def ring_first(n, buf, halves, dst):
        lo, hi = halves
        send(n, buf.at[x2].at[lo], dst[0], to_xp)
        send(n + 1, buf.at[x2].at[hi], dst[1], to_xm)
        send(n + 2, buf.at[xp].at[hi], dst[2], to_xp)
        send(n + 3, buf.at[xm].at[lo], dst[4], to_xm)

    def ring_second(n, buf, halves, dst, keep):
        lo, hi = halves
        got(n, dst[0])
        keep[0] = (buf[xp, lo].astype(F32) + dst[0][...].astype(F32)).astype(BF16)
        send(n + 4, keep.at[0], dst[3], to_xp)
        got(n + 1, dst[1])
        keep[1] = (buf[xm, hi].astype(F32) + dst[1][...].astype(F32)).astype(BF16)
        send(n + 5, keep.at[1], dst[5], to_xm)

    def ring_last(n, buf, halves, dst, fin):
        got(n + 2, dst[2])
        got(n + 3, dst[4])
        got(n + 4, dst[3])
        got(n + 5, dst[5])
        for half, one, two in zip(halves, dst[3:1:-1], dst[4:6]):
            fin[yl, x, half] = (
                buf[x, half].astype(F32) + one[...].astype(F32) + two[...].astype(F32)
            ).astype(BF16)

    halves = (pl.ds(0, 16), pl.ds(16, 16))
    v_dst = (vr2p, vr2m, vra1, vra2, vrb1, vrb2)
    k_dst = (kr2p, kr2m, kra1, kra2, krb1, krb2)

    def to_pair(n, part, buf, dst):
        for a in range(8):
            for h in range(2):
                buf[a // 4, a % 4, pl.ds(16 * h, 16), :] = part[DN * h + 16 * a:DN * h + 16 * a + 16]
        send(n, buf.at[1 - yl], dst, to_y)

    def from_pair(n, buf, other, total):
        got(n, other)
        total[...] = (buf[yl].astype(F32) + other[...].astype(F32)).astype(BF16)

    def along_x(n, fin, side):
        for d in range(1, NX):
            send(n + d, fin.at[side, x], fin.at[side, x], device(x_=(x + d) % NX))

    def spread(n, fin):
        send(n, fin.at[yl, x], fin.at[yl, x], to_y)
        along_x(n, fin, yl)

    def relay(n, fin):
        got(n, fin.at[1 - yl, x])
        along_x(n + 3, fin, 1 - yl)

    def spread_got(n, fin):
        for d in range(1, NX):
            got(n + d, fin.at[yl, (x + NX - d) % NX])
            got(n + 3 + d, fin.at[1 - yl, (x + NX - d) % NX])

    for b in range(8):
        w = st[b] * (mb[b] * inv)[:1]
        wt[pl.ds(b * TOK, TOK), :] = w.astype(BF16)
        gst[pl.ds(b * TOK, TOK), :] = (w * (gw[b] - dots) * scale).astype(BF16)

    def terms(k, j):
        start = pl.multiple_of((2 * k + j) * TOK, TOK)
        g = gst[pl.ds(start, TOK), :]
        full = dot(g, ax[...])
        lat = full[:, :DL] + dot(wt[pl.ds(start, TOK), :], gx[...])
        rope = jnp.where(low_lane, full[:HALF, DL:], full[HALF:, DL:])
        return lat, rope

    def put_terms(lat, rope, dst):
        for i in range(0, NZ, 2):
            dst[pl.ds(72 * i, 144), :] = jnp.concatenate(
                [lat[24 * r:24 * r + 24, 128 * t:128 * t + 128] for r in (i, i + 1) for t in range(3)], axis=0
            ).astype(dst.dtype)
        dst[pl.ds(72 * NZ, 96), :] = rope.astype(dst.dtype)
        dst[pl.ds(CHA, TOK), :] = lat[:, 384:].astype(dst.dtype)

    def both_cores(k, dst):
        got(48 + k, crecv.at[k])
        rows = pl.ds(0, CHA)
        dst[...] = (cown[k, rows] + crecv[k, rows].astype(F32)).astype(dst.dtype)

    low_rows, high_rows = pl.ds(0, CHH), pl.ds(CHH, CHH)

    def chunk(k):
        put_terms(*terms(k, sib), csend.at[k])
        send(48 + k, csend.at[k], crecv.at[k], to_sib)
        put_terms(*terms(k, c), cown.at[k])

    chunk(3)
    to_pair(73, dot(gotx[...], lot[...], 1, 1).astype(BF16), vb, vry)
    chunk(2)
    both_cores(3, xs.at[3])
    send(52, xs.at[3, low_rows], r2p, to_xp)
    send(53, xs.at[3, high_rows], r2m, to_xm)
    chunk(1)
    both_cores(2, xs.at[2])
    send(54, xs.at[2, high_rows], ra1, to_xp)
    chunk(0)
    both_cores(1, xs.at[1])
    send(55, xs.at[1, low_rows], rb1, to_xm)

    gat[...] = dot(lxt[:DL, :], gst[...]).astype(BF16)
    to_pair(80, dot(qtx[...], gat[...], 1, 1).astype(BF16), kb, kry)

    got(52, r2p)
    xs[0, low_rows] = (xs[2, low_rows].astype(F32) + r2p[...].astype(F32)).astype(BF16)
    send(56, xs.at[0, low_rows], ra2, to_xp)
    got(53, r2m)
    xs[0, high_rows] = (xs[1, high_rows].astype(F32) + r2m[...].astype(F32)).astype(BF16)
    send(57, xs.at[0, high_rows], rb2, to_xm)
    both_cores(0, xsum)
    rows = pl.ds(CHA, TOK)
    parts = [cown[k, rows] + crecv[k, rows].astype(F32) for k in range(NX)]
    for i in range(NZ):
        bs[i] = jnp.concatenate([part[24 * i:24 * i + 24] for part in parts], axis=0).astype(BF16)
    for d in (4, 3, 5, 2, 6, 1, 7):
        far = (z + d) % NZ
        send(100 + d, bs.at[far], brecv.at[d], device(z_=far))

    from_pair(73, vb, vry, vs)
    ring_first(74, vs, halves, v_dst)

    rope2 = dot(lxt[DL:, :], gst[...])
    rope_rows = (rope2[:DR] + rope2[DR:]).astype(BF16)
    gr_ref[0] = rope_rows[:, :TOK]
    gr_ref[1] = rope_rows[:, TOK:]
    grad_nope = dot(gat[...], kup2, 0, 1)
    gn_ref[0] = grad_nope[:TOK, :DN].astype(BF16)
    gn_ref[1] = grad_nope[TOK:, DN:].astype(BF16)

    from_pair(80, kb, kry, ks)
    ring_first(81, ks, halves, k_dst)

    got(54, ra1)
    got(55, rb1)
    got(56, ra2)
    got(57, rb2)
    xsum[low_rows] = xsum[low_rows] + ra2[...].astype(F32) + rb1[...].astype(F32)
    xsum[high_rows] = xsum[high_rows] + ra1[...].astype(F32) + rb2[...].astype(F32)
    pad = jnp.zeros((8, 128), F32)
    for i in range(NZ):
        zs[i] = jnp.concatenate(
            [xsum[pl.ds(72 * i, 72)], xsum[pl.ds(72 * NZ + 24 * (i % 4), 24)]], axis=0
        ).astype(BF16)
    for d in (4, 3, 5, 2, 6, 1, 7):
        far = (z + d) % NZ
        send(57 + d, zs.at[far], zrecv.at[d], device(z_=far))

    ring_second(74, vs, halves, v_dst, vkeep)
    ring_second(81, ks, halves, k_dst, kkeep)

    fourth = bs[z].astype(F32)
    for d in (1, 7, 2, 6, 3, 5, 4):
        got(100 + d, brecv.at[d])
        fourth = fourth + brecv[d].astype(F32)
    for k, there, dev in ((3, 3, device(x_=x2)), (2, 1, to_xp), (1, 2, to_xm)):
        bx[k] = jnp.concatenate([fourth[24 * k:24 * k + 24], pad], axis=0).astype(BF16)
        send(107 + there, bx.at[k], bxr.at[there], dev)

    ring_last(74, vs, halves, v_dst, vfin)
    spread(87, vfin)
    ring_last(81, ks, halves, k_dst, kfin)
    spread(94, kfin)
    relay(87, vfin)
    relay(94, kfin)

    out_row, in_row = iota((128, 128), 0), iota((128, 128), 1)
    owner, place = out_row // 16, out_row % 16
    source = 24 * third(place) + 3 * owner + (place - 3 * third(place))
    order = jnp.where((source == in_row) & (place < 15), 1.0, 0.0).astype(BF16)
    own = fourth[:24]
    for k in range(1, NX):
        got(107 + k, bxr.at[k])
        own = own + bxr[k].astype(F32)[:24]
    zsum = zs[z].astype(F32)
    for d in (1, 7, 2, 6, 3, 5, 4):
        got(57 + d, zrecv.at[d])
        zsum = zsum + zrecv[d].astype(F32)
    zsum = jnp.concatenate([zsum[:72], own, zsum[72:], pad], axis=0)
    sorted_rows = dot(order, zsum.astype(BF16)).astype(BF16)
    for i in range(8):
        ys[i] = sorted_rows[16 * i:16 * i + 16]

    def to_owner(d, e):
        far = (yh + d) % NYH
        return pltpu.make_async_remote_copy(
            src_ref=ys.at[far * 2 + e], dst_ref=yrecv.at[d, c],
            send_sem=ss.at[65 + 2 * d + e], recv_sem=rs.at[65 + 2 * d + c],
            device_id=device(yh_=far, yl_=(yl + c) % 2, c_=e), device_id_type=MESH,
        )

    for d in range(NYH):
        for e in range(2):
            if d == 0 and e == 0:
                @pl.when(c == 0)
                def _():
                    yrecv[0, 0] = ys[yh * 2]

                @pl.when(c == 1)
                def _():
                    to_owner(0, 0).start()
            else:
                to_owner(d, e).start()

    spread_got(87, vfin)
    spread_got(94, kfin)

    total = jnp.zeros((16, 128), F32)
    for d in range(NYH):
        for e in range(2):
            if d == 0 and e == 0:
                @pl.when(c == 1)
                def _():
                    got(65, yrecv.at[0, 0])
            else:
                got(65 + 2 * d + e, yrecv.at[d, e])
    for d in range(NYH):
        for e in range(2):
            total = total + yrecv[d, e].astype(F32)
    ol_ref[...] = jnp.concatenate([total[3 * t:3 * t + 3] for t in range(4)], axis=1).astype(BF16)
    rope = total[12:15]
    or_ref[...] = jnp.where(z >= NZ // 2, rope[:, DR:], rope[:, :DR]).astype(BF16)

    for copy in sent:
        copy.wait_send()
    for d in range(NYH):
        for e in range(2):
            if d == 0 and e == 0:
                @pl.when(c == 1)
                def _():
                    to_owner(0, 0).wait_send()
            else:
                to_owner(d, e).wait_send()


def finish(
    gn_in, gr_in, ol_in, or_in, kfin, vfin, gn_out, gr_out, ol_out, or_out, gk_out, gv_out,
    gn_s, gk_s, gv_s, sems,
):
    copies = []

    def put(src, dst):
        copy = pltpu.make_async_copy(src, dst, sems.at[len(copies)])
        copy.start()
        copies.append(copy)

    for fin, rows, out in ((kfin, gk_s, gk_out), (vfin, gv_s, gv_out)):
        for h in range(2):
            for a in range(8):
                rows[h, pl.ds(16 * a, 16), :] = fin[a // 4, a % 4, pl.ds(16 * h, 16), :].astype(F32)
            put(rows.at[h], out.at[h])
    put(gr_in, gr_out)
    put(ol_in, ol_out)
    put(or_in, or_out)
    gn_s[...] = jnp.stack([gn_in[0].astype(F32), gn_in[1].astype(F32)], axis=1).astype(BF16)
    put(gn_s, gn_out)
    for copy in copies:
        copy.wait()


def on_device(query_nope, query_rope, grad_output, latents, key_rope, key_up, value_up, pair_order):
    scratch = [
        ((TOK, 2, DN), BF16), ((2, DR, TOK), BF16), ((TOK, 2, DN), BF16), ((DR, TOK), BF16),
        ((2, DN, DL), BF16), ((2, DN, DL), BF16), ((1, PAIRS), jnp.int32),
        ((4, 2, 2, BLK, 128), BF16), ((NX * 2 * TOK, EXT), BF16), ((EXT, NX * 2 * TOK), BF16),
        ((ROWS, EXT), BF16), ((EXT, ROWS), BF16), ((ROWS, DL), BF16), ((DL, ROWS), BF16),
        ((2 * DN, ROWS), BF16), ((2 * DN, ROWS), BF16),
        ((8, TOK, 128), F32), ((8, ROWS), F32), ((8, TOK, ROWS), F32), ((8, TOK, ROWS), F32),
        ((8, 8, ROWS), F32), ((8, 8, ROWS), F32), ((NX, DL, ROWS), F32), ((NX, 8, ROWS), F32),
        ((8 * TOK, ROWS), BF16), ((8 * TOK, ROWS), BF16), ((DL, ROWS), BF16), ((DL, ROWS), BF16),
        ((4, CH, 128), BF16), ((4, CH, 128), BF16), ((4, CH, 128), F32), ((4, CHA, 128), BF16),
        ((CHA, 128), F32),
        ((CHH, 128), BF16), ((CHH, 128), BF16), ((CHH, 128), BF16), ((CHH, 128), BF16),
        ((CHH, 128), BF16), ((CHH, 128), BF16),
        ((8, 96, 128), BF16), ((8, 96, 128), BF16), ((8, 96, 128), BF16), ((8, 96, 128), BF16),
        ((4, 32, 128), BF16), ((4, 32, 128), BF16), ((8, 16, 128), BF16), ((4, 2, 16, 128), BF16),
    ] + (
        [((2, 4, 32, DL), BF16)] + [((4, 32, DL), BF16)] * 2 + [((16, DL), BF16)] * 6 + [((2, 16, DL), BF16)]
    ) * 2
    outs = (
        ((2, TOK, DN), BF16), ((2, DR, TOK), BF16), ((3, DL), BF16), ((3, DR), BF16),
        ((2, 4, 32, DL), BF16), ((2, 4, 32, DL), BF16),
    )
    any_spec = pl.BlockSpec(memory_space=pl.ANY)
    vmem_spec = pl.BlockSpec(memory_space=pltpu.VMEM)
    raw = pl.pallas_call(
        kernel,
        out_shape=[pltpu.VMEM(s, t) for s, t in outs],
        in_specs=[any_spec] * 8,
        out_specs=[vmem_spec] * 6,
        scratch_shapes=[pltpu.VMEM(s, t) for s, t in scratch] + [
            pltpu.SemaphoreType.DMA((15,)),
            pltpu.SemaphoreType.DMA((N_SEM,)),
            pltpu.SemaphoreType.DMA((N_SEM,)),
            pltpu.SemaphoreType.REGULAR((4,)),
        ],
        compiler_params=pltpu.CompilerParams(
            collective_id=0, has_side_effects=True, vmem_limit_bytes=60 * 1024 * 1024
        ),
        name="mla_backward",
    )(
        query_nope,
        jnp.transpose(query_rope, (1, 2, 0)),
        grad_output,
        latents,
        key_rope.T,
        key_up,
        value_up,
        pair_order.reshape(1, -1),
    )
    results = (
        ((TOK, 2, DN), BF16), ((2, DR, TOK), BF16), ((3, DL), BF16), ((3, DR), BF16),
        ((2, DN, DL), F32), ((2, DN, DL), F32),
    )
    grad_nope, grad_rope, own_lat, own_rope, grad_kup, grad_vup = pl.pallas_call(
        finish,
        out_shape=[jax.ShapeDtypeStruct(s, t) for s, t in results],
        in_specs=[vmem_spec] * 6,
        out_specs=[any_spec] * 6,
        scratch_shapes=[
            pltpu.VMEM((TOK, 2, DN), BF16),
            pltpu.VMEM((2, DN, DL), F32),
            pltpu.VMEM((2, DN, DL), F32),
            pltpu.SemaphoreType.DMA((8,)),
        ],
        name="finish",
    )(*[pltpu.with_memory_space_constraint(r, pltpu.VMEM) for r in raw])
    return grad_nope, jnp.transpose(grad_rope, (2, 0, 1)), own_lat, own_rope, grad_kup, grad_vup


def solution(mesh):
    placed = (
        P("dp", "ctx", None),
        P("dp", "ctx", None),
        P("dp", "ctx", None),
        P("dp", None),
        P("dp", None),
        P("ctx", None, None),
        P("ctx", None, None),
        P(),
    )
    return jax.shard_map(
        on_device,
        mesh=mesh,
        in_specs=placed,
        out_specs=(
            P("dp", "ctx", None),
            P("dp", "ctx", None),
            P(("dp", "ctx"), None),
            P(("dp", "ctx"), None),
            P("ctx", None, None),
            P("ctx", None, None),
        ),
        check_vma=False,
    )
```

```python
import functools
import math

import jax
import jax.numpy as jnp
from jax import lax
from jax.experimental import pallas as pl
from jax.experimental.pallas import tpu as pltpu
from jax.sharding import PartitionSpec as P

MESH = pl.DeviceIdType.MESH
F32 = jnp.float32
BF16 = jnp.bfloat16
NEG = -1e30

NX, NYL, NZ, NYH = 4, 2, 8, 4
TOK = 192
HALF = TOK // 2
DL, DR, DN = 512, 64, 128
ROWS = 2 * TOK
EXT = DL + 2 * DR
PAIRS = 256
PER_DEV = 32
BLK = 4 * HALF + 48
CUT = 224
CHA = NZ * 72 + 96
CHH = CHA // 2
CH = CHA + TOK

REL = (0, 3, 1, 2)

N_SEM = 111


def dot(a, b, ca=1, cb=0):
    return lax.dot_general(a, b, (((ca,), (cb,)), ((), ())), preferred_element_type=F32)


def iota(shape, axis):
    return lax.broadcasted_iota(jnp.int32, shape, axis)


def third(v):
    return (v * 43691) >> 17


def kernel(
    q_hbm, qr_hbm, go_hbm, lat_hbm, kr_hbm, kup_hbm, vup_hbm, po_hbm,
    gn_ref, gr_ref, ol_ref, or_ref, kfin, vfin,
    q_v, qr_v, go_v, kr_v, kup_v, vup_v, po_v,
    agb, lx_s, lxt, ax, axt, gx, gxt, qtx, gotx,
    pcol, prow, st, gw, mb, lb, lacc, mtop, wt, gst, lot, gat,
    csend, crecv, cown, xs, xsum, r2p, r2m, ra1, ra2, rb1, rb2,
    zs, zrecv, bs, brecv, bx, bxr, ys, yrecv,
    vb, vry, vs, vr2p, vr2m, vra1, vra2, vrb1, vrb2, vkeep,
    kb, kry, ks, kr2p, kr2m, kra1, kra2, krb1, krb2, kkeep,
    lsem, ss, rs, known,
):
    dp, ctx = lax.axis_index("dp"), lax.axis_index("ctx")
    x, yl = dp // NYL, dp % NYL
    z, yh, c = ctx // (NYH * 2), (ctx // 2) % NYH, ctx % 2
    sib = 1 - c
    xp, xm, x2 = (x + 1) % NX, (x + 3) % NX, (x + 2) % NX

    def device(x_=None, yl_=None, z_=None, yh_=None, c_=None):
        x_, yl_ = x if x_ is None else x_, yl if yl_ is None else yl_
        z_, yh_, c_ = z if z_ is None else z_, yh if yh_ is None else yh_, c if c_ is None else c_
        return {"dp": x_ * NYL + yl_, "ctx": (z_ * NYH + yh_) * 2 + c_}

    to_sib = device(c_=sib)
    to_y = device(yl_=1 - yl)
    to_xp, to_xm = device(x_=xp), device(x_=xm)

    def remote(n, src, dst, dev):
        return pltpu.make_async_remote_copy(
            src_ref=src, dst_ref=dst, send_sem=ss.at[n], recv_sem=rs.at[n],
            device_id=dev, device_id_type=MESH,
        )

    sent = []

    def send(n, src, dst, dev):
        copy = remote(n, src, dst, dev)
        copy.start()
        sent.append(copy)

    def got(n, dst):
        remote(n, dst, dst, to_sib).wait_recv()

    barrier = pltpu.get_barrier_semaphore()

    row = yh * 2 + yl
    along_y = []
    for step in (1, 7):
        far = (row + step) % (2 * NYH)
        along_y.append(device(yl_=far % 2, yh_=far // 2))
    along_z = [device(z_=(z + step) % NZ) for step in (1, NZ - 1)]
    for dev in [to_sib, to_xp, to_xm] + along_y + along_z:
        pl.semaphore_signal(barrier, inc=1, device_id=dev, device_id_type=MESH)

    def tell(n):
        for dev in along_y + along_z:
            pl.semaphore_signal(known.at[n], inc=1, device_id=dev, device_id_type=MESH)

    def heard(n):
        pl.semaphore_wait(known.at[n], 4)

    local = []

    def fetch(src, dst):
        copy = pltpu.make_async_copy(src, dst, lsem.at[len(local)])
        copy.start()
        local.append(copy)
        return copy

    lat_in = []
    for h in range(2):
        for t in range(4):
            lat_in.append(fetch(
                lat_hbm.at[pl.ds(h * HALF, HALF), pl.ds(t * 128, 128)],
                agb.at[0, 0, h, pl.ds(t * HALF, HALF)],
            ))
    kr_in = fetch(kr_hbm, kr_v)
    q_in, kup_in = fetch(q_hbm, q_v), fetch(kup_hbm, kup_v)
    go_in, vup_in = fetch(go_hbm, go_v), fetch(vup_hbm, vup_v)
    qr_in, po_in = fetch(qr_hbm, qr_v), fetch(po_hbm, po_v)

    for copy in lat_in:
        copy.wait()
    pl.semaphore_wait(barrier, 7)

    far = (row + 1 + 6 * c) % (2 * NYH)
    to_yg = device(yl_=far % 2, yh_=far // 2)
    pieces = (pl.ds(0, CUT), pl.ds(CUT, BLK - CUT))
    x_id, y_id, sib_id = 0, 16, 32

    def block(k, j, p, core=c):
        return agb.at[k, j, core, pieces[p]]

    def gather_x(k, j, p, source):
        dst = block(k, j, p)
        send(x_id + 4 * k + 2 * j + p, source, dst, to_xp if (k, p) in ((1, 0), (1, 1), (3, 0)) else to_xm)

    def gather_y(k, p):
        send(y_id + 2 * k + p, block(k, 0, p), block(k, 1, p), to_yg)

    def gather_sib(k, j, p):
        send(sib_id + 4 * k + 2 * j + p, block(k, j, p), block(k, j, p), to_sib)

    def from_x(k, j, p):
        got(x_id + 4 * k + 2 * j + p, block(k, j, p))

    def from_y(k, p):
        got(y_id + 2 * k + p, block(k, 1, p))

    def from_sib(k, j):
        for p in range(2):
            got(sib_id + 4 * k + 2 * j + p, block(k, j, p, sib))

    gather_x(1, 0, 0, block(0, 0, 0))
    kr_in.wait()
    kr_own = kr_v[...].astype(F32).T
    krp = jnp.concatenate([kr_own[:HALF], kr_own[HALF:]], axis=1).astype(BF16)
    agb[0, 0, 0, pl.ds(4 * HALF, 48)] = krp[:48]
    agb[0, 0, 1, pl.ds(4 * HALF, 48)] = krp[48:]
    gather_x(2, 0, 1, block(0, 0, 1))
    gather_y(0, 0)
    gather_x(1, 0, 1, block(0, 0, 1))
    gather_x(2, 0, 0, block(0, 0, 0))
    gather_y(0, 1)
    tell(0)

    q_in.wait()
    go_in.wait()
    kup_in.wait()
    vup_in.wait()
    qr_in.wait()
    po_in.wait()
    blank = jnp.zeros((TOK, DN), F32)

    def block_diagonal(ref):
        both = ref[...].astype(F32)
        top = jnp.concatenate([both[:, 0, :], blank], axis=1)
        low = jnp.concatenate([blank, both[:, 1, :]], axis=1)
        return jnp.concatenate([top, low], axis=0)

    qx = block_diagonal(q_v)
    gox = block_diagonal(go_v)
    qtx[...] = qx.T.astype(BF16)
    gotx[...] = gox.T.astype(BF16)
    kup2 = kup_v[...].reshape(2 * DN, DL)
    vup2 = vup_v[...].reshape(2 * DN, DL)
    absorbed = dot(qx.astype(BF16), kup2)
    grad_lat = dot(gox.astype(BF16), vup2)
    qr_rows = jnp.concatenate([qr_v[0].astype(F32).T, qr_v[1].astype(F32).T], axis=0)
    qr2 = jnp.concatenate([qr_rows, qr_rows], axis=1)
    ax[:, :DL] = absorbed.astype(BF16)
    ax[:, DL:] = qr2.astype(BF16)
    axt[:DL, :] = absorbed.astype(BF16).T
    axt[DL:, :] = qr2.astype(BF16).T
    gx[...] = grad_lat.astype(BF16)
    gxt[...] = grad_lat.astype(BF16).T

    po_row = jnp.broadcast_to(po_v[...].astype(F32), (8, PAIRS))
    slot_t = third(iota((PAIRS, ROWS), 1) % HALF)
    pick = jnp.where(iota((PAIRS, ROWS), 0) == dp * PER_DEV + slot_t, 1.0, 0.0).astype(BF16)
    pid_row = dot(po_row.astype(BF16), pick)
    within = iota((8, ROWS), 1)
    in_half = within % HALF
    late = (within % TOK) >= HALF
    group = jnp.where(late, 2.0 * PAIRS - 1.0 - pid_row, pid_row)
    prow[...] = group * 3.0 + (in_half - 3 * third(in_half)).astype(F32)

    po_col = jnp.broadcast_to(po_row[:1], (128, PAIRS)).T.astype(BF16)
    half_of = iota((TOK, PER_DEV), 0) % HALF
    expand = jnp.where(third(half_of) == iota((TOK, PER_DEV), 1), 1.0, 0.0).astype(BF16)
    row_no = iota((TOK, 128), 0)
    row_half = row_no % HALF
    for b in range(NX * NYL):
        pid = dot(expand, po_col[b * PER_DEV:(b + 1) * PER_DEV])
        grp = jnp.where(row_no >= HALF, 2.0 * PAIRS - 1.0 - pid, pid)
        pcol[b] = grp * 3.0 + (row_half - 3 * third(row_half)).astype(F32)

    scale = 1.0 / math.sqrt(DN + DR)
    low_lane = iota((HALF, 128), 1) < DR

    def attend(k, j):
        b = 2 * k + j
        key_dev = ((x + REL[k]) % NX) * NYL + (yl + j) % 2
        halves = []
        krp = jnp.concatenate(
            [agb[k, j, 0, pl.ds(4 * HALF, 48)], agb[k, j, 1, pl.ds(4 * HALF, 48)]], axis=0
        )
        zero = jnp.zeros((HALF, 128), BF16)
        for h in range(2):
            tiles = [agb[k, j, h, pl.ds(t * HALF, HALF)] for t in range(4)]
            tiles.append(jnp.where(low_lane, krp, zero) if h == 0 else jnp.where(low_lane, zero, krp))
            halves.append(jnp.concatenate(tiles, axis=1))
        lx = jnp.concatenate(halves, axis=0)
        lx_s[pl.ds(b * TOK, TOK), :] = lx
        s = dot(lx, axt[...]) * scale
        gw[b] = dot(lx[:, :DL], gxt[...])
        key_pos = pcol[key_dev]
        allowed = jnp.concatenate([key_pos] * 3, axis=1) <= prow[0:1]
        s = jnp.where(allowed, s, NEG)
        m = jnp.max(s, axis=0, keepdims=True)
        p = jnp.where(allowed, jnp.exp(s - m), 0.0)
        st[b] = p
        mb[b] = jnp.broadcast_to(m, (8, ROWS))
        lb[b] = jnp.broadcast_to(jnp.sum(p, axis=0, keepdims=True), (8, ROWS))

    def turn(k):
        for t in range(EXT // 128):
            lxt[pl.ds(t * 128, 128), pl.ds(k * 2 * TOK, 2 * TOK)] = (
                lx_s[pl.ds(k * 2 * TOK, 2 * TOK), pl.ds(t * 128, 128)].T
            )
        top = jnp.maximum(mb[2 * k], mb[2 * k + 1])
        both = [st[b] * jnp.exp(mb[b] - top)[:1] for b in (2 * k, 2 * k + 1)]
        lacc[k] = dot(
            lxt[pl.ds(0, DL), pl.ds(k * 2 * TOK, 2 * TOK)], jnp.concatenate(both, axis=0).astype(BF16)
        )
        mtop[k] = top

    def on_from_x(k, p):
        from_x(k, 0, p)
        if (k, p) in ((1, 0), (2, 1)):
            gather_x(3, 0, p, block(k, 0, p))
        gather_y(k, p)
        gather_sib(k, 0, p)

    def on_from_y(k, p):
        from_y(k, p)
        if (k, p) in ((1, 0), (2, 1)):
            gather_x(3, 1, p, block(k, 1, p))
        gather_sib(k, 1, p)

    def on_far(j, p):
        from_x(3, j, p)
        gather_sib(3, j, p)

    heard(0)
    tell(1)
    on_from_x(1, 0)
    on_from_x(2, 1)
    on_from_y(0, 0)
    on_from_y(0, 1)
    heard(1)
    tell(2)
    attend(0, 0)
    on_from_x(1, 1)
    on_from_x(2, 0)
    heard(2)
    tell(3)
    from_sib(0, 1)
    attend(0, 1)
    on_from_y(1, 0)
    on_from_y(2, 1)
    turn(0)
    on_far(0, 0)
    on_far(0, 1)
    from_sib(1, 0)
    attend(1, 0)
    on_from_y(1, 1)
    on_from_y(2, 0)
    from_sib(2, 0)
    attend(2, 0)
    from_sib(3, 0)
    attend(3, 0)
    on_far(1, 0)
    from_sib(1, 1)
    attend(1, 1)
    on_far(1, 1)
    turn(1)
    from_sib(2, 1)
    attend(2, 1)
    turn(2)
    from_sib(3, 1)
    attend(3, 1)
    turn(3)
    heard(3)

    top = jnp.maximum(jnp.maximum(mtop[0], mtop[1]), jnp.maximum(mtop[2], mtop[3]))
    total = jnp.zeros_like(top)
    for b in range(8):
        share = jnp.exp(mb[b] - top)
        mb[b] = share
        total = total + lb[b] * share
    inv = 1.0 / total
    parts = [(jnp.exp(mtop[k] - top) * inv)[:1] for k in range(NX)]
    dots = jnp.zeros((1, ROWS), F32)
    for t in range(4):
        rows = pl.ds(t * 128, 128)
        part = lacc[0, rows] * parts[0]
        for k in range(1, NX):
            part = part + lacc[k, rows] * parts[k]
        dots = dots + jnp.sum(gxt[rows, :].astype(F32) * part, axis=0, keepdims=True)
        lot[rows, :] = part.astype(BF16)

    def ring_first(n, buf, halves, dst):
        lo, hi = halves
        send(n, buf.at[x2].at[lo], dst[0], to_xp)
        send(n + 1, buf.at[x2].at[hi], dst[1], to_xm)
        send(n + 2, buf.at[xp].at[hi], dst[2], to_xp)
        send(n + 3, buf.at[xm].at[lo], dst[4], to_xm)

    def ring_second(n, buf, halves, dst, keep):
        lo, hi = halves
        got(n, dst[0])
        keep[0] = (buf[xp, lo].astype(F32) + dst[0][...].astype(F32)).astype(BF16)
        send(n + 4, keep.at[0], dst[3], to_xp)
        got(n + 1, dst[1])
        keep[1] = (buf[xm, hi].astype(F32) + dst[1][...].astype(F32)).astype(BF16)
        send(n + 5, keep.at[1], dst[5], to_xm)

    def ring_last(n, buf, halves, dst, fin):
        got(n + 2, dst[2])
        got(n + 3, dst[4])
        got(n + 4, dst[3])
        got(n + 5, dst[5])
        for half, one, two in zip(halves, dst[3:1:-1], dst[4:6]):
            fin[yl, x, half] = (
                buf[x, half].astype(F32) + one[...].astype(F32) + two[...].astype(F32)
            ).astype(BF16)

    halves = (pl.ds(0, 16), pl.ds(16, 16))
    v_dst = (vr2p, vr2m, vra1, vra2, vrb1, vrb2)
    k_dst = (kr2p, kr2m, kra1, kra2, krb1, krb2)

    def to_pair(n, part, buf, dst):
        for a in range(8):
            for h in range(2):
                buf[a // 4, a % 4, pl.ds(16 * h, 16), :] = part[DN * h + 16 * a:DN * h + 16 * a + 16]
        send(n, buf.at[1 - yl], dst, to_y)

    def from_pair(n, buf, other, total):
        got(n, other)
        total[...] = (buf[yl].astype(F32) + other[...].astype(F32)).astype(BF16)

    def along_x(n, fin, side):
        for d in range(1, NX):
            send(n + d, fin.at[side, x], fin.at[side, x], device(x_=(x + d) % NX))

    def spread(n, fin):
        send(n, fin.at[yl, x], fin.at[yl, x], to_y)
        along_x(n, fin, yl)

    def relay(n, fin):
        got(n, fin.at[1 - yl, x])
        along_x(n + 3, fin, 1 - yl)

    def spread_got(n, fin):
        for d in range(1, NX):
            got(n + d, fin.at[yl, (x + NX - d) % NX])
            got(n + 3 + d, fin.at[1 - yl, (x + NX - d) % NX])

    for b in range(8):
        w = st[b] * (mb[b] * inv)[:1]
        wt[pl.ds(b * TOK, TOK), :] = w.astype(BF16)
        gst[pl.ds(b * TOK, TOK), :] = (w * (gw[b] - dots) * scale).astype(BF16)

    def terms(k, j):
        start = pl.multiple_of((2 * k + j) * TOK, TOK)
        g = gst[pl.ds(start, TOK), :]
        full = dot(g, ax[...])
        lat = full[:, :DL] + dot(wt[pl.ds(start, TOK), :], gx[...])
        rope = jnp.where(low_lane, full[:HALF, DL:], full[HALF:, DL:])
        return lat, rope

    def put_terms(lat, rope, dst):
        for i in range(0, NZ, 2):
            dst[pl.ds(72 * i, 144), :] = jnp.concatenate(
                [lat[24 * r:24 * r + 24, 128 * t:128 * t + 128] for r in (i, i + 1) for t in range(3)], axis=0
            ).astype(dst.dtype)
        dst[pl.ds(72 * NZ, 96), :] = rope.astype(dst.dtype)
        dst[pl.ds(CHA, TOK), :] = lat[:, 384:].astype(dst.dtype)

    def both_cores(k, dst):
        got(48 + k, crecv.at[k])
        rows = pl.ds(0, CHA)
        dst[...] = (cown[k, rows] + crecv[k, rows].astype(F32)).astype(dst.dtype)

    low_rows, high_rows = pl.ds(0, CHH), pl.ds(CHH, CHH)

    def chunk(k):
        put_terms(*terms(k, sib), csend.at[k])
        send(48 + k, csend.at[k], crecv.at[k], to_sib)
        put_terms(*terms(k, c), cown.at[k])

    chunk(3)
    to_pair(73, dot(gotx[...], lot[...], 1, 1).astype(BF16), vb, vry)
    chunk(2)
    both_cores(3, xs.at[3])
    send(52, xs.at[3, low_rows], r2p, to_xp)
    send(53, xs.at[3, high_rows], r2m, to_xm)
    chunk(1)
    both_cores(2, xs.at[2])
    send(54, xs.at[2, high_rows], ra1, to_xp)
    chunk(0)
    both_cores(1, xs.at[1])
    send(55, xs.at[1, low_rows], rb1, to_xm)

    gat[...] = dot(lxt[:DL, :], gst[...]).astype(BF16)
    to_pair(80, dot(qtx[...], gat[...], 1, 1).astype(BF16), kb, kry)

    got(52, r2p)
    xs[0, low_rows] = (xs[2, low_rows].astype(F32) + r2p[...].astype(F32)).astype(BF16)
    send(56, xs.at[0, low_rows], ra2, to_xp)
    got(53, r2m)
    xs[0, high_rows] = (xs[1, high_rows].astype(F32) + r2m[...].astype(F32)).astype(BF16)
    send(57, xs.at[0, high_rows], rb2, to_xm)
    both_cores(0, xsum)
    rows = pl.ds(CHA, TOK)
    parts = [cown[k, rows] + crecv[k, rows].astype(F32) for k in range(NX)]
    for i in range(NZ):
        bs[i] = jnp.concatenate([part[24 * i:24 * i + 24] for part in parts], axis=0).astype(BF16)
    for d in (4, 3, 5, 2, 6, 1, 7):
        far = (z + d) % NZ
        send(100 + d, bs.at[far], brecv.at[d], device(z_=far))

    from_pair(73, vb, vry, vs)
    ring_first(74, vs, halves, v_dst)

    rope2 = dot(lxt[DL:, :], gst[...])
    rope_rows = (rope2[:DR] + rope2[DR:]).astype(BF16)
    gr_ref[0] = rope_rows[:, :TOK]
    gr_ref[1] = rope_rows[:, TOK:]
    grad_nope = dot(gat[...], kup2, 0, 1)
    gn_ref[0] = grad_nope[:TOK, :DN].astype(BF16)
    gn_ref[1] = grad_nope[TOK:, DN:].astype(BF16)


    got(54, ra1)
    got(55, rb1)
    got(56, ra2)
    got(57, rb2)
    xsum[low_rows] = xsum[low_rows] + ra2[...].astype(F32) + rb1[...].astype(F32)
    xsum[high_rows] = xsum[high_rows] + ra1[...].astype(F32) + rb2[...].astype(F32)
    pad = jnp.zeros((8, 128), F32)
    for i in range(NZ):
        zs[i] = jnp.concatenate(
            [xsum[pl.ds(72 * i, 72)], xsum[pl.ds(72 * NZ + 24 * (i % 4), 24)]], axis=0
        ).astype(BF16)
    for d in (4, 3, 5, 2, 6, 1, 7):
        far = (z + d) % NZ
        send(57 + d, zs.at[far], zrecv.at[d], device(z_=far))

    from_pair(80, kb, kry, ks)
    ring_first(81, ks, halves, k_dst)
    ring_second(74, vs, halves, v_dst, vkeep)
    ring_second(81, ks, halves, k_dst, kkeep)

    fourth = bs[z].astype(F32)
    for d in (1, 7, 2, 6, 3, 5, 4):
        got(100 + d, brecv.at[d])
        fourth = fourth + brecv[d].astype(F32)
    for k, there, dev in ((3, 3, device(x_=x2)), (2, 1, to_xp), (1, 2, to_xm)):
        bx[k] = jnp.concatenate([fourth[24 * k:24 * k + 24], pad], axis=0).astype(BF16)
        send(107 + there, bx.at[k], bxr.at[there], dev)

    ring_last(74, vs, halves, v_dst, vfin)
    spread(87, vfin)
    ring_last(81, ks, halves, k_dst, kfin)
    spread(94, kfin)
    relay(87, vfin)

    out_row, in_row = iota((128, 128), 0), iota((128, 128), 1)
    owner, place = out_row // 16, out_row % 16
    source = 24 * third(place) + 3 * owner + (place - 3 * third(place))
    order = jnp.where((source == in_row) & (place < 15), 1.0, 0.0).astype(BF16)
    own = fourth[:24]
    for k in range(1, NX):
        got(107 + k, bxr.at[k])
        own = own + bxr[k].astype(F32)[:24]
    zsum = zs[z].astype(F32)
    for d in (1, 7, 2, 6, 3, 5, 4):
        got(57 + d, zrecv.at[d])
        zsum = zsum + zrecv[d].astype(F32)
    zsum = jnp.concatenate([zsum[:72], own, zsum[72:], pad], axis=0)
    sorted_rows = dot(order, zsum.astype(BF16)).astype(BF16)
    for i in range(8):
        ys[i] = sorted_rows[16 * i:16 * i + 16]

    def to_owner(d, e):
        far = (yh + d) % NYH
        return pltpu.make_async_remote_copy(
            src_ref=ys.at[far * 2 + e], dst_ref=yrecv.at[d, c],
            send_sem=ss.at[65 + 2 * d + e], recv_sem=rs.at[65 + 2 * d + c],
            device_id=device(yh_=far, yl_=(yl + c) % 2, c_=e), device_id_type=MESH,
        )

    for d in range(NYH):
        for e in range(2):
            if d == 0 and e == 0:
                @pl.when(c == 0)
                def _():
                    yrecv[0, 0] = ys[yh * 2]

                @pl.when(c == 1)
                def _():
                    to_owner(0, 0).start()
            else:
                to_owner(d, e).start()

    relay(94, kfin)
    spread_got(87, vfin)
    spread_got(94, kfin)

    total = jnp.zeros((16, 128), F32)
    for d in range(NYH):
        for e in range(2):
            if d == 0 and e == 0:
                @pl.when(c == 1)
                def _():
                    got(65, yrecv.at[0, 0])
            else:
                got(65 + 2 * d + e, yrecv.at[d, e])
    for d in range(NYH):
        for e in range(2):
            total = total + yrecv[d, e].astype(F32)
    ol_ref[...] = jnp.concatenate([total[3 * t:3 * t + 3] for t in range(4)], axis=1).astype(BF16)
    rope = total[12:15]
    or_ref[...] = jnp.where(z >= NZ // 2, rope[:, DR:], rope[:, :DR]).astype(BF16)

    for copy in sent:
        copy.wait_send()
    for d in range(NYH):
        for e in range(2):
            if d == 0 and e == 0:
                @pl.when(c == 1)
                def _():
                    to_owner(0, 0).wait_send()
            else:
                to_owner(d, e).wait_send()


def finish(
    gn_in, gr_in, ol_in, or_in, kfin, vfin, gn_out, gr_out, ol_out, or_out, gk_out, gv_out,
    gn_s, gk_s, gv_s, sems,
):
    copies = []

    def put(src, dst):
        copy = pltpu.make_async_copy(src, dst, sems.at[len(copies)])
        copy.start()
        copies.append(copy)

    for fin, rows, out in ((kfin, gk_s, gk_out), (vfin, gv_s, gv_out)):
        for h in range(2):
            for a in range(8):
                rows[h, pl.ds(16 * a, 16), :] = fin[a // 4, a % 4, pl.ds(16 * h, 16), :].astype(F32)
            put(rows.at[h], out.at[h])
    put(gr_in, gr_out)
    put(ol_in, ol_out)
    put(or_in, or_out)
    gn_s[...] = jnp.stack([gn_in[0].astype(F32), gn_in[1].astype(F32)], axis=1).astype(BF16)
    put(gn_s, gn_out)
    for copy in copies:
        copy.wait()


def on_device(query_nope, query_rope, grad_output, latents, key_rope, key_up, value_up, pair_order):
    scratch = [
        ((TOK, 2, DN), BF16), ((2, DR, TOK), BF16), ((TOK, 2, DN), BF16), ((DR, TOK), BF16),
        ((2, DN, DL), BF16), ((2, DN, DL), BF16), ((1, PAIRS), jnp.int32),
        ((4, 2, 2, BLK, 128), BF16), ((NX * 2 * TOK, EXT), BF16), ((EXT, NX * 2 * TOK), BF16),
        ((ROWS, EXT), BF16), ((EXT, ROWS), BF16), ((ROWS, DL), BF16), ((DL, ROWS), BF16),
        ((2 * DN, ROWS), BF16), ((2 * DN, ROWS), BF16),
        ((8, TOK, 128), F32), ((8, ROWS), F32), ((8, TOK, ROWS), F32), ((8, TOK, ROWS), F32),
        ((8, 8, ROWS), F32), ((8, 8, ROWS), F32), ((NX, DL, ROWS), F32), ((NX, 8, ROWS), F32),
        ((8 * TOK, ROWS), BF16), ((8 * TOK, ROWS), BF16), ((DL, ROWS), BF16), ((DL, ROWS), BF16),
        ((4, CH, 128), BF16), ((4, CH, 128), BF16), ((4, CH, 128), F32), ((4, CHA, 128), BF16),
        ((CHA, 128), F32),
        ((CHH, 128), BF16), ((CHH, 128), BF16), ((CHH, 128), BF16), ((CHH, 128), BF16),
        ((CHH, 128), BF16), ((CHH, 128), BF16),
        ((8, 96, 128), BF16), ((8, 96, 128), BF16), ((8, 96, 128), BF16), ((8, 96, 128), BF16),
        ((4, 32, 128), BF16), ((4, 32, 128), BF16), ((8, 16, 128), BF16), ((4, 2, 16, 128), BF16),
    ] + (
        [((2, 4, 32, DL), BF16)] + [((4, 32, DL), BF16)] * 2 + [((16, DL), BF16)] * 6 + [((2, 16, DL), BF16)]
    ) * 2
    outs = (
        ((2, TOK, DN), BF16), ((2, DR, TOK), BF16), ((3, DL), BF16), ((3, DR), BF16),
        ((2, 4, 32, DL), BF16), ((2, 4, 32, DL), BF16),
    )
    any_spec = pl.BlockSpec(memory_space=pl.ANY)
    vmem_spec = pl.BlockSpec(memory_space=pltpu.VMEM)
    raw = pl.pallas_call(
        kernel,
        out_shape=[pltpu.VMEM(s, t) for s, t in outs],
        in_specs=[any_spec] * 8,
        out_specs=[vmem_spec] * 6,
        scratch_shapes=[pltpu.VMEM(s, t) for s, t in scratch] + [
            pltpu.SemaphoreType.DMA((15,)),
            pltpu.SemaphoreType.DMA((N_SEM,)),
            pltpu.SemaphoreType.DMA((N_SEM,)),
            pltpu.SemaphoreType.REGULAR((4,)),
        ],
        compiler_params=pltpu.CompilerParams(
            collective_id=0, has_side_effects=True, vmem_limit_bytes=60 * 1024 * 1024
        ),
        name="mla_backward",
    )(
        query_nope,
        jnp.transpose(query_rope, (1, 2, 0)),
        grad_output,
        latents,
        key_rope.T,
        key_up,
        value_up,
        pair_order.reshape(1, -1),
    )
    results = (
        ((TOK, 2, DN), BF16), ((2, DR, TOK), BF16), ((3, DL), BF16), ((3, DR), BF16),
        ((2, DN, DL), F32), ((2, DN, DL), F32),
    )
    grad_nope, grad_rope, own_lat, own_rope, grad_kup, grad_vup = pl.pallas_call(
        finish,
        out_shape=[jax.ShapeDtypeStruct(s, t) for s, t in results],
        in_specs=[vmem_spec] * 6,
        out_specs=[any_spec] * 6,
        scratch_shapes=[
            pltpu.VMEM((TOK, 2, DN), BF16),
            pltpu.VMEM((2, DN, DL), F32),
            pltpu.VMEM((2, DN, DL), F32),
            pltpu.SemaphoreType.DMA((8,)),
        ],
        name="finish",
    )(*[pltpu.with_memory_space_constraint(r, pltpu.VMEM) for r in raw])
    return grad_nope, jnp.transpose(grad_rope, (2, 0, 1)), own_lat, own_rope, grad_kup, grad_vup


def solution(mesh):
    placed = (
        P("dp", "ctx", None),
        P("dp", "ctx", None),
        P("dp", "ctx", None),
        P("dp", None),
        P("dp", None),
        P("ctx", None, None),
        P("ctx", None, None),
        P(),
    )
    return jax.shard_map(
        on_device,
        mesh=mesh,
        in_specs=placed,
        out_specs=(
            P("dp", "ctx", None),
            P("dp", "ctx", None),
            P(("dp", "ctx"), None),
            P(("dp", "ctx"), None),
            P("ctx", None, None),
            P("ctx", None, None),
        ),
        check_vma=False,
    )
```
